32 devices in a mesh: dp: 16 (over z, y, x), pair: 2 (over core).
Axes of the slice: x: 2, y: 2, z: 4, core: 2. Of those that a mesh axis runs over, the one named last changes fastest.
Arguments:
- features: bfloat16 [32768, 512], P(('dp', 'pair')), may hold values from -6 to 6
- cotangent: bfloat16 [32768, 256], P(('dp', 'pair')), may hold values from -6 to 6
- canvas_lengths: int32 [32, 2], P(('dp', 'pair')), may hold values from 1 to 768, 1024 in all within a row
- crop_ids: int32 [32768], P(('dp', 'pair')), may hold values from 0 to 511, never falling along the last dimension, each value on 1 to 128 neighbouring positions
- mats: float32 [5632, 256], P(('dp', 'pair'))
- mats_m: float32 [5632, 256], P(('dp', 'pair'))
- mats_v: float32 [5632, 256], P(('dp', 'pair')), as said below
- vecs: float32 [17, 256], replicated, as said below
- vecs_m: float32 [17, 256], replicated
- vecs_v: float32 [17, 256], replicated, as said below
Outputs:
- output: float32 [32768, 256], P(('dp', 'pair'))
- feature_grad: float32 [32768, 512], P(('dp', 'pair'))
- mats_new: float32 [5632, 256], P(('dp', 'pair'))
- mats_m_new: float32 [5632, 256], P(('dp', 'pair'))
- mats_v_new: float32 [5632, 256], P(('dp', 'pair'))
- mats_low_new: bfloat16 [5632, 256], P(('dp', 'pair'))
- vecs_new: float32 [17, 256], replicated
- vecs_m_new: float32 [17, 256], replicated
- vecs_v_new: float32 [17, 256], replicated
The draws below stay inside these ranges and needn't reach their ends.
Inputs may be any that keep to these rules, and one draw needn't show every extreme that they name: `canvas_lengths`: each device's two canvas lengths sum to 1024. `crop_ids`: crop numbers never fall along the token slots; a crop has 1 to 128 slots. `mats_v`: second moments are positive. `vecs_v`: second moments are positive. `vecs`: rows 4 and 7 are gains near one.
All inputs are finite; a program needn't handle non-finite values.
Results may differ from the reference program's by a relative error of at most 0.023.
Values may be sent and summed in bfloat16 or wider, within the bound.
No kernel may reach another device: no remote copies, remote signals or barrier semaphores. Data moves between devices by JAX's collectives and lax.ppermute only.
A program may use at most 192 MiB of HBM per device.

```python
import math
import jax
import jax.numpy as jnp
import numpy as np
from jax import lax

FEAT = 512
D = 256
HEADS = 8
FF = 2048
TOK_DEV = 1024
CROP = 64
STEP = 10
HDIM = 32
TOKENS = 32768
MROWS = 5632
VROWS = 17
N_DP = 16
N_PAIR = 2


def row_scales():
    row_ids = jnp.arange(MROWS)
    attn_end = FEAT + 4 * D
    weight_scale = jnp.where(row_ids < FEAT, FEAT ** (-0.5), jnp.where(row_ids < FEAT + 3 * D, D ** (-0.5), jnp.where(row_ids < attn_end, 0.25, jnp.where(row_ids < attn_end + FF, D ** (-0.5), FF ** (-0.5)))))
    grad_scale = jnp.where(row_ids < FEAT, 0.5, jnp.where(row_ids < FEAT + 2 * D, 0.1, jnp.where(row_ids < FEAT + 3 * D, 0.3, jnp.where(row_ids < attn_end, 0.1, jnp.where(row_ids < attn_end + FF, 0.3, 0.4)))))
    grad_scale = grad_scale * TOKENS ** 0.5
    return (weight_scale[:, None].astype(jnp.float32), grad_scale[:, None].astype(jnp.float32))


def base_noise(key, shape):
    return jax.random.normal(key, shape, jnp.float32)


def second_spread(key, shape):
    return jnp.exp(jax.random.uniform(key, shape, jnp.float32, jnp.log(0.5), jnp.log(8.0)))


def draw_mats(key, part):
    weight_scale, grad_scale = row_scales()
    return (base_noise(key, (MROWS, D)) * weight_scale).astype(jnp.float32)


def draw_mats_m(key, part):
    weight_scale, grad_scale = row_scales()
    return (0.11 * grad_scale * base_noise(key, (MROWS, D))).astype(jnp.float32)


def draw_mats_v(key, part):
    weight_scale, grad_scale = row_scales()
    return (0.001 * grad_scale * grad_scale * second_spread(key, (MROWS, D))).astype(jnp.float32)


def draw_vecs(key, part):
    row_ids = jnp.arange(VROWS)[:, None]
    gain_rows = (row_ids == 4) | (row_ids == 7)
    noise = base_noise(key, (VROWS, D))
    return jnp.where(gain_rows, 1.0 + 0.1 * noise, 0.3 * noise).astype(jnp.float32)


def draw_vecs_m(key, part):
    grad_size = 0.7 * TOKENS ** 0.5
    return (0.11 * grad_size * base_noise(key, (VROWS, D))).astype(jnp.float32)


def draw_vecs_v(key, part):
    grad_size = 0.7 * TOKENS ** 0.5
    return (0.001 * grad_size * grad_size * second_spread(key, (VROWS, D))).astype(jnp.float32)


def level_of(key, extent, shards, least, top_value):
    def one(axis_at, parts):
        steps = jax.random.uniform(jax.random.fold_in(jax.random.fold_in(key, 6), axis_at), (parts,), jnp.float32, least / len(shards), top_value / len(shards))
        return jnp.repeat(jnp.exp(steps), extent[axis_at] // parts).reshape((-1,) + (1,) * (len(extent) - axis_at - 1))

    loudness = one(*shards[0])
    for cut in shards[1:]:
        loudness = loudness * one(*cut)
    return loudness


def length_profile(count, total, reach, skew):
    portions = [(1 << 20) // math.isqrt(standing ** skew) + 1 for standing in range(2, count + 1)]
    rest, counts = total - reach - (count - 1), [1] * (count - 1)
    while rest > 0:
        free = [i for i in range(count - 1) if counts[i] < reach]
        whole, remaining = sum([portions[i] for i in free]), rest
        for i in free:
            addition = min(reach - counts[i], max(1, remaining * portions[i] // whole), rest)
            counts[i] = counts[i] + addition
            rest = rest - addition
    return np.array([reach] + counts)


def ragged_sizes(stream_key, amount, total, reach, lean):
    if amount == 2:
        one = jax.random.randint(stream_key, (), max(1, total - reach), min(reach, total - 1) + 1)
        return jnp.stack([one, total - one])
    sizes = jnp.asarray(length_profile(amount, total, reach, lean), jnp.int32)
    couples = (amount - 1) // 2
    donor, sink = sizes[1:1 + 2 * couples:2], sizes[2:2 + 2 * couples:2]
    margin = jnp.minimum(donor - 1, reach - sink)
    moved = jax.random.randint(jax.random.fold_in(stream_key, 1), (couples,), 0, 1 << 20) % (margin + 1)
    sizes = sizes.at[1:1 + 2 * couples:2].set(donor - moved).at[2:2 + 2 * couples:2].set(sink + moved)
    return sizes[jax.random.permutation(jax.random.fold_in(stream_key, 2), amount)]


def centred(key, dims, width, reach, shards=(), kind=jnp.bfloat16):
    drawn = jax.random.normal(key, dims, jnp.float32) * width
    if len(shards) > 0:
        drawn = level_of(key, dims, shards, -0.22, 0.18) * drawn
    return jnp.clip(drawn, min=-reach, max=reach).astype(kind)


def setup_inputs(seed: int = 0) -> dict:
    key_of = jax.random.split(jax.random.key(seed), 11)
    return {
        "features": centred(key_of[0], (TOKENS, FEAT), 1.0, 6.0, ((0, 32),)),
        "cotangent": centred(key_of[1], (TOKENS, D), 1.0, 6.0, ((0, 32),)),
        "canvas_lengths": jax.vmap(lambda own: ragged_sizes(own, 2, TOK_DEV, TOK_DEV * 3 // 4, 0))(jax.random.split(key_of[2], (N_DP * N_PAIR))).reshape((N_DP * N_PAIR, 2)).astype(jnp.int32),
        "crop_ids": jnp.searchsorted(jnp.cumsum(ragged_sizes(key_of[3], TOKENS // CROP, TOKENS, 2 * CROP, 0)), jnp.arange(TOKENS), side="right").astype(jnp.int32),
        "mats": draw_mats(jax.random.fold_in(key_of[10], 71), 0),
        "mats_m": draw_mats_m(jax.random.fold_in(key_of[10], 71), 0),
        "mats_v": draw_mats_v(jax.random.fold_in(key_of[10], 71), 0),
        "vecs": draw_vecs(jax.random.fold_in(key_of[10], 71), 0),
        "vecs_m": draw_vecs_m(jax.random.fold_in(key_of[10], 71), 0),
        "vecs_v": draw_vecs_v(jax.random.fold_in(key_of[10], 71), 0),
    }


@jax.custom_vjp
def low(v):
    return lax.optimization_barrier(v.astype(jnp.bfloat16)).astype(jnp.float32)

@jax.custom_vjp
def low_back(v):
    return v

def low_keep(v):
    return (low(v), None)

def low_pass(kept, grad):
    return (grad,)

def back_keep(v):
    return (v, None)

def back_low(kept, grad):
    return (low(grad),)
low.defvjp(low_keep, low_pass)
low_back.defvjp(back_keep, back_low)
PRECISION = lax.Precision.HIGHEST
EPS_NORM = 1e-05
RATE = 0.2
BETA_ONE = 0.9
BETA_TWO = 0.999
ADAM_EPS = 1e-08
DECAY = 0.0001
MASKED = -1000000000.0

def both_round(tensor):
    return low_back(low(tensor))

def dense(left_op, right_op):
    return jnp.dot(left_op, right_op, precision=PRECISION, preferred_element_type=jnp.float32)

def sine_table(within, model_width):
    half_width = model_width // 2
    frequency = jnp.exp(-jnp.log(10000.0) * jnp.arange(half_width, dtype=jnp.float32) / half_width)
    angles = within.astype(jnp.float32)[:, None] * frequency[None, :]
    return jnp.concatenate([jnp.sin(angles), jnp.cos(angles)], axis=1)

def norm_plain(tensor, gain_vec, shift_vec):
    centered = tensor - lax.optimization_barrier(jnp.mean(tensor, axis=1, keepdims=True))
    inverse = lax.rsqrt(lax.optimization_barrier(jnp.mean(centered * centered, axis=1, keepdims=True)) + EPS_NORM)
    return centered * inverse * gain_vec + shift_vec

def unpack(gathered, feat_dim, model_width, hidden):
    offset = feat_dim
    w_proj = gathered[:feat_dim]
    w_query = gathered[offset:offset + model_width]
    w_key = gathered[offset + model_width:offset + 2 * model_width]
    w_value = gathered[offset + 2 * model_width:offset + 3 * model_width]
    w_out = gathered[offset + 3 * model_width:offset + 4 * model_width]
    offset = offset + 4 * model_width
    w_hidden = gathered[offset:offset + hidden].reshape(model_width, hidden)
    w_back = gathered[offset + hidden:offset + 2 * hidden]
    return (w_proj, w_query, w_key, w_value, w_out, w_hidden, w_back)

def attend_block(inputs):
    q_block, k_block, v_block, canvas_block, crop_block = inputs
    allowed = (canvas_block[:, None] == canvas_block[None, :]) & (crop_block[:, None] == crop_block[None, :])
    q_heads = q_block.reshape(TOK_DEV, HEADS, HDIM)
    k_heads = k_block.reshape(TOK_DEV, HEADS, HDIM)
    v_heads = v_block.reshape(TOK_DEV, HEADS, HDIM)
    raw_scores = low_back(jnp.einsum('qhd,khd->hqk', q_heads, k_heads, precision=PRECISION) * HDIM ** (-0.5))
    masked = jnp.where(allowed[None], raw_scores, MASKED)
    probs = jax.nn.softmax(masked, axis=2)
    return jnp.einsum('hqk,khd->qhd', low(probs), v_heads, precision=PRECISION).reshape(TOK_DEV, D)

def forward(features, mats, vecs, canvas_id, crop_ids, pos_table):
    w_proj, w_query, w_key, w_value, w_out, w_hidden, w_back = unpack(low(mats), FEAT, D, FF)
    embedded = low_back(dense(features, w_proj) + vecs[0])
    source = low(embedded + pos_table)
    embed_low = low(embedded)
    queries = both_round(dense(source, w_query) + vecs[1])
    key_rows = both_round(dense(source, w_key))
    val_rows = both_round(dense(embed_low, w_value) + vecs[2])
    blocks = (queries.reshape(-1, TOK_DEV, D), key_rows.reshape(-1, TOK_DEV, D), val_rows.reshape(-1, TOK_DEV, D), canvas_id.reshape(-1, TOK_DEV), crop_ids.reshape(-1, TOK_DEV))
    attended = both_round(lax.map(jax.checkpoint(attend_block), blocks).reshape(-1, D))
    normed_one = norm_plain(embedded + low_back(dense(attended, w_out) + vecs[3]), vecs[4], vecs[5])
    pre_act = low_back(dense(low(normed_one), w_hidden) + vecs[9:].reshape(FF))
    act_low = low(jax.nn.gelu(pre_act))
    branch = low_back(dense(act_low, w_back) + vecs[6])
    return norm_plain(normed_one + branch, vecs[7], vecs[8])

def adam_step(weight, moment_one, moment_two, gradient, step_rate, decay_rate):
    moment_one = BETA_ONE * moment_one + (1.0 - BETA_ONE) * gradient
    moment_two = BETA_TWO * moment_two + (1.0 - BETA_TWO) * gradient * gradient
    mean_hat = moment_one / (1.0 - BETA_ONE ** STEP)
    square_hat = moment_two / (1.0 - BETA_TWO ** STEP)
    weight = weight - step_rate * (mean_hat / (jnp.sqrt(square_hat) + ADAM_EPS) + decay_rate * weight)
    return (weight, moment_one, moment_two)

def reference(features, cotangent, canvas_lengths, crop_ids, mats, mats_m, mats_v, vecs, vecs_m, vecs_v):
    position = jnp.arange(TOK_DEV, dtype=jnp.int32)[None, :]
    first_len = canvas_lengths[:, 0:1]
    canvas_id = (position >= first_len).astype(jnp.int32)
    within = (position - first_len * canvas_id).reshape(-1)
    pos_table = sine_table(within, D)
    canvas_flat = canvas_id.reshape(-1)

    def wrapped(feat_in, mats_in, vecs_in):
        return forward(feat_in, mats_in, vecs_in, canvas_flat, crop_ids, pos_table)
    output, pull = jax.vjp(wrapped, features.astype(jnp.float32), mats, vecs)
    feature_grad, mat_grad, vec_grad = pull(cotangent.astype(jnp.float32))
    row_ids = jnp.arange(MROWS, dtype=jnp.int32)
    row_rate = jnp.where(row_ids < FEAT, 0.1 * RATE, RATE)[:, None]
    mats_new, mats_m_new, mats_v_new = adam_step(mats, mats_m, mats_v, mat_grad, row_rate, DECAY)
    vecs_new, vecs_m_new, vecs_v_new = adam_step(vecs, vecs_m, vecs_v, vec_grad, RATE, 0.0)
    return (output, feature_grad, mats_new, mats_m_new, mats_v_new, mats_new.astype(jnp.bfloat16), vecs_new, vecs_m_new, vecs_v_new)
```

```python
import functools

import jax
import jax.numpy as jnp
from jax import lax
from jax.experimental import pallas as pl
from jax.experimental.pallas import tpu as pltpu
from jax.sharding import PartitionSpec as P

HEADS = 8
FF = 2048
STEP = 10

EPS_NORM = 1e-05
RATE = 0.2
BETA_ONE = 0.9
BETA_TWO = 0.999
ADAM_EPS = 1e-08
DECAY = 0.0001
MASKED = -1000000000.0

TILE = 128
WINDOW = 384
ROWS = 256
BLOCK = 256
BLOCKS = FF // BLOCK
GELU_A = 0.7978845608028654
GELU_B = 0.044715
VEC_PAD = 32

F32 = jnp.float32
BF16 = jnp.bfloat16
VMEM = pltpu.VMEM


def nn(a, b):
    return lax.dot_general(a, b, (((1,), (0,)), ((), ())), preferred_element_type=F32)


def nt(a, b):
    return lax.dot_general(a, b, (((1,), (1,)), ((), ())), preferred_element_type=F32)


def row_mean(x):
    return jnp.sum(x, axis=1, keepdims=True) * (1.0 / x.shape[1])


def fold_rows(x):
    return jnp.sum(x.reshape(x.shape[0] // 8, 8, x.shape[1]), axis=0)


def column_sum(x):
    return jnp.sum(x.astype(F32), axis=0, keepdims=True)


def head_lanes(h, rows, width):
    lane = lax.broadcasted_iota(jnp.int32, (rows, width), 1)
    size = width // HEADS
    return (lane >= h * size) & (lane < (h + 1) * size)


def window_start(i, tok):
    return jnp.clip((i - 1) * TILE, 0, tok - WINDOW)


def call(kernel, outs, ins, scratch, name, flops, spaces=None, vmem=48):
    spaces = spaces or [VMEM] * len(ins)
    nbytes = sum(a.size * a.dtype.itemsize for a in ins) + sum(
        a.size * a.dtype.itemsize for a in outs
    )
    return pl.pallas_call(
        kernel,
        out_shape=tuple(outs),
        in_specs=[pl.BlockSpec(memory_space=s) for s in spaces],
        out_specs=tuple(pl.BlockSpec(memory_space=VMEM) for _ in outs),
        scratch_shapes=scratch,
        compiler_params=pltpu.CompilerParams(vmem_limit_bytes=vmem << 20),
        cost_estimate=pl.CostEstimate(flops=flops, bytes_accessed=nbytes, transcendentals=0),
        name=name,
    )(*ins)


def shape(dims, kind):
    return jax.ShapeDtypeStruct(dims, kind)


def load_pieces(refs, offsets, dst, sems):
    copies = []
    for ref, offs in zip(refs, offsets):
        if len(ref.shape) == 2:
            views = [ref]
        else:
            views = [ref.at[i] for i in range(ref.shape[0])]
        for view, off in zip(views, offs):
            copies.append(
                pltpu.make_async_copy(
                    view, dst.at[pl.ds(off, view.shape[0]), :], sems.at[len(copies)]
                )
            )
    for copy in copies:
        copy.start()
    for copy in copies:
        copy.wait()


def place_offsets(place, piece, planes):
    offsets = []
    for other in (0, 1):
        for slot in range(4):
            core = place[3] ^ other if other else place[3]
            inner = 2 * (place[1] ^ slot) + core
            offsets.append(
                [pl.multiple_of((8 * plane + inner) * piece, 16) for plane in range(planes)]
            )
    return offsets


def attention_kernel(flat, piece, place, feat, pos, mask, vec, *rest):
    count = 1 if flat else 8
    pieces, rest = rest[:count], rest[count:]
    w, emb, src, q, k, v, attn, p, v_t, q_t, sems = rest
    tok, width = emb.shape
    feat_dim = feat.shape[1]
    size = width // HEADS
    scale = size ** (-0.5)
    offsets = [[0]] if flat else place_offsets(place, piece, 1)
    load_pieces(pieces, offsets, w, sems)
    for i in range(tok // ROWS):
        r = pl.ds(i * ROWS, ROWS)
        e = nn(feat[r, :], w[0:feat_dim, :]) + vec[0:1, :]
        emb[r, :] = e
        s = (e + pos[r, :]).astype(BF16)
        src[r, :] = s
        low = e.astype(BF16)
        at = feat_dim
        q[r, :] = (nn(s, w[at : at + width, :]) + vec[1:2, :]).astype(BF16)
        k[r, :] = nn(s, w[at + width : at + 2 * width, :]).astype(BF16)
        v[r, :] = (nn(low, w[at + 2 * width : at + 3 * width, :]) + vec[2:3, :]).astype(BF16)
    v_t[...] = v[...].T
    q_t[...] = jnp.zeros_like(q_t)
    masked = MASKED / scale

    def tile(i, carry):
        rows = pl.ds(pl.multiple_of(i * TILE, TILE), TILE)
        win = pl.ds(pl.multiple_of(window_start(i, tok), TILE), WINDOW)
        own_t = q[rows, :].T
        keys = k[win, :]
        vals_t = v_t[:, win]
        allowed = mask[i] > 0.5
        for h in range(HEADS):
            d = slice(h * size, (h + 1) * size)
            q_t[d, h * TILE : (h + 1) * TILE] = own_t[d, :]
        parts = []
        for g in range(HEADS // 2):
            both = nn(keys, q_t[:, 2 * g * TILE : (2 * g + 2) * TILE])
            for u in range(2):
                h = 2 * g + u
                s = jnp.where(allowed, both[:, u * TILE : (u + 1) * TILE], masked)
                top = jnp.max(s, axis=0, keepdims=True)
                e = jnp.exp((s - top) * scale)
                total = jnp.sum(e, axis=0, keepdims=True)
                probs = (e * (1.0 / total)).astype(BF16)
                p[i, :, h * TILE : (h + 1) * TILE] = probs
                parts.append(nn(vals_t[h * size : (h + 1) * size, :], probs))
        attn[rows, :] = jnp.concatenate(parts, axis=0).T.astype(BF16)
        return carry

    lax.fori_loop(0, tok // TILE, tile, 0, unroll=2)


def attention(flat, place, feat, pos, mask, vec, pieces, attn_rows):
    tok, width = feat.shape[0], vec.shape[1]
    piece = pieces[0].shape[0]
    low = shape((tok, width), BF16)
    outs = [
        shape((attn_rows, width), BF16),
        shape((tok, width), F32),
        low,
        low,
        low,
        low,
        low,
        shape((tok // TILE, WINDOW, HEADS * TILE), BF16),
    ]
    ins = [place, feat, pos, mask, vec, *pieces]
    return call(
        functools.partial(attention_kernel, flat, piece),
        outs,
        ins,
        [
            VMEM((width, tok), BF16),
            VMEM((width, HEADS * TILE), BF16),
            pltpu.SemaphoreType.DMA((8,)),
        ],
        "attention_forward",
        12_000_000_000,
        [pltpu.SMEM] + [VMEM] * 4 + [pl.ANY] * len(pieces),
    )


def feed_kernel(flat, piece, place, emb, attn, cot, vec, wa, *rest):
    count = 1 if flat else 8
    pieces, rest = rest[:count], rest[count:]
    outs = 5 if flat else 6
    res, rest = rest[: outs + 1], rest[outs + 1 :]
    out, g_one, w_out, vec_grad, dwo = res[:5]
    (wf, wh, wh_t, wb_t, half_a, half_b, act, pre, slope, n_t, b_t, o_t, acc, gff, sems) = rest
    halves = (half_a, half_b)
    tok, width = emb.shape
    first = width // 2
    offsets = [[0]] if flat else place_offsets(place, piece, 3)
    load_pieces(pieces, offsets, wf, sems)
    for u in range(2):
        halves[u][...] = wf[first : first + FF, u * 128 : (u + 1) * 128].astype(F32)
    w_out[0:first, :] = wa[wa.shape[0] - first :, :]
    w_out[first:, :] = wf[0:first, :]
    for j in range(BLOCKS):
        c = slice(j * BLOCK, (j + 1) * BLOCK)
        w = jnp.concatenate(
            [halves[u][pl.ds(j, width, stride=BLOCKS), :] for u in range(2)], axis=1
        ).astype(BF16)
        wh[:, c] = w
        wh_t[c, :] = w.T
        wb_t[:, c] = wf[first + FF + j * BLOCK : first + FF + (j + 1) * BLOCK, :].T
    acc[...] = jnp.zeros_like(acc)
    n_t[width : width + 8, :] = jnp.ones((8, tok), BF16)

    def tile(i, carry):
        r = pl.ds(pl.multiple_of(i * ROWS, ROWS), ROWS)
        res_one = emb[r, :] + nn(attn[r, :], w_out[...]) + vec[3:4, :]
        cen = res_one - row_mean(res_one)
        inv_one = lax.rsqrt(row_mean(cen * cen) + EPS_NORM)
        hat_one = cen * inv_one
        normed = hat_one * vec[4:5, :] + vec[5:6, :]
        low = normed.astype(BF16)
        for j in range(BLOCKS):
            c = slice(j * BLOCK, (j + 1) * BLOCK)
            x = nn(low, wh[:, c]) + vec[9 + j : 10 + j, :]
            sq = x * x
            t = jnp.tanh(x * (GELU_A + (GELU_A * GELU_B) * sq))
            half = 0.5 + 0.5 * t
            act[r, c] = (x * half).astype(BF16)
            bend = x * ((2 * GELU_A) + (6 * GELU_A * GELU_B) * sq)
            slope[:, c] = (half + (half - half * half) * bend).astype(BF16)
        res_two = normed + nn(act[r, :], wf[first + FF : first + 2 * FF, :]) + vec[6:7, :]
        cen = res_two - row_mean(res_two)
        inv_two = lax.rsqrt(row_mean(cen * cen) + EPS_NORM)
        hat_two = cen * inv_two
        out[r, :] = hat_two * vec[7:8, :] + vec[8:9, :]
        ct = cot[r, :].astype(F32)
        gs = ct * vec[7:8, :]
        g_two = inv_two * (gs - row_mean(gs) - hat_two * row_mean(gs * hat_two))
        back = g_two.astype(BF16)
        b_t[:, r] = back.T
        acc[0] += fold_rows(back.astype(F32))
        acc[1] += fold_rows(ct * hat_two)
        acc[2] += fold_rows(ct)
        for j in range(BLOCKS):
            c = slice(j * BLOCK, (j + 1) * BLOCK)
            pre[r, c] = (nn(back, wb_t[:, c]) * slope[:, c].astype(F32)).astype(BF16)
        g_norm = g_two + nn(pre[r, :], wh_t[...])
        n_t[0:width, r] = low.T
        gs = g_norm * vec[4:5, :]
        g_res = inv_one * (gs - row_mean(gs) - hat_one * row_mean(gs * hat_one))
        g_one[r, :] = g_res
        out_low = g_res.astype(BF16)
        o_t[:, r] = out_low.T
        acc[3] += fold_rows(out_low.astype(F32))
        acc[4] += fold_rows(g_norm * hat_one)
        acc[5] += fold_rows(g_norm)
        return carry

    lax.fori_loop(0, tok // ROWS, tile, 0)
    for j in range(BLOCKS):
        c = slice(j * BLOCK, (j + 1) * BLOCK)
        g = nn(n_t[...], pre[:, c])
        for u in range(2):
            halves[u][pl.ds(j, width, stride=BLOCKS), :] = g[0:width, u * 128 : (u + 1) * 128]
        vec_grad[9 + j : 10 + j, :] = g[width : width + 1, :]
        at = first + FF + j * BLOCK
        gff[at : at + BLOCK, :] = nn(b_t[...], act[:, c]).T.astype(BF16)
    for u in range(2):
        gff[first : first + FF, u * 128 : (u + 1) * 128] = halves[u][...].astype(BF16)
    g = nn(o_t[...], attn[...]).T.astype(BF16)
    dwo[...] = g[0:first, :]
    gff[0:first, :] = g[first:, :]
    sums = jnp.sum(acc[...], axis=1)
    vec_grad[0:3, :] = jnp.zeros((3, width), F32)
    for row, at in ((3, 3), (4, 4), (5, 5), (6, 0), (7, 1), (8, 2)):
        vec_grad[row : row + 1, :] = sums[at : at + 1, :]
    if flat:
        res[5][...] = gff[...]
    else:
        split_cores(place, gff, res[5], res[6])


def split_cores(place, grads, keep, send):
    core = place[3]
    piece = keep.shape[1]
    for m in range(keep.shape[0]):
        keep[m] = grads[pl.ds(pl.multiple_of((2 * m + core) * piece, 16), piece), :]
        send[m] = grads[pl.ds(pl.multiple_of((2 * m + 1 - core) * piece, 16), piece), :]


def feed(flat, place, emb, attn, cot, vec, wa, pieces, ff_rows):
    tok, width = emb.shape
    piece = pieces[0].shape[-2]
    outs = [
        shape((tok, width), F32),
        shape((tok, width), F32),
        shape((width, width), BF16),
        shape(vec.shape, F32),
        shape((width // 2, width), BF16),
    ]
    if flat:
        outs += [shape((ff_rows, width), BF16)]
    else:
        outs += [shape((ff_rows // piece // 2, piece, width), BF16)] * 2
    return call(
        functools.partial(feed_kernel, flat, piece),
        outs,
        [place, emb, attn, cot, vec, wa, *pieces],
        [
            VMEM((ff_rows, width), BF16),
            VMEM((width, FF), BF16),
            VMEM((FF, width), BF16),
            VMEM((width, FF), BF16),
            VMEM((FF, 128), F32),
            VMEM((FF, 128), F32),
            VMEM((tok, FF), BF16),
            VMEM((tok, FF), BF16),
            VMEM((ROWS, FF), BF16),
            VMEM((width + 8, tok), BF16),
            VMEM((width, tok), BF16),
            VMEM((width, tok), BF16),
            VMEM((6, 8, width), F32),
            VMEM((ff_rows, width), BF16),
            pltpu.SemaphoreType.DMA((24,)),
        ],
        "feed_forward_both",
        14_000_000_000,
        [pltpu.SMEM] + [VMEM] * 5 + [pl.ANY] * len(pieces),
    )


def attention_back_kernel(g_one, q, k, v, p, w_out, ql, kl, vl, ag, k_t, ds_all, a_t, qm, am, dk, dv):
    tok, width = g_one.shape
    size = width // HEADS
    scale = size ** (-0.5)
    for i in range(tok // ROWS):
        r = pl.ds(i * ROWS, ROWS)
        ag[r, :] = nt(g_one[r, :].astype(BF16), w_out[...]).astype(BF16)
    k_t[...] = k[...].T
    dk[...] = jnp.zeros_like(dk)
    dv[...] = jnp.zeros_like(dv)
    a_t[...] = jnp.zeros_like(a_t)

    def tile(i, carry):
        rows = pl.ds(pl.multiple_of(i * TILE, TILE), TILE)
        win = pl.ds(pl.multiple_of(window_start(i, tok), TILE), WINDOW)
        own_q = q[rows, :]
        own_a = ag[rows, :]
        own_t = own_a.T
        vals = v[win, :]
        keys_t = k_t[:, win]
        for h in range(HEADS):
            lanes = head_lanes(h, TILE, width)
            d = slice(h * size, (h + 1) * size)
            c = slice(h * TILE, (h + 1) * TILE)
            a_t[d, c] = own_t[d, :]
            qm[c, :] = jnp.where(lanes, own_q, jnp.zeros_like(own_q))
            am[c, :] = jnp.where(lanes, own_a, jnp.zeros_like(own_a))
        parts = []
        for g in range(HEADS // 2):
            both = nn(vals, a_t[:, 2 * g * TILE : (2 * g + 2) * TILE])
            for u in range(2):
                h = 2 * g + u
                c = slice(h * TILE, (h + 1) * TILE)
                probs = p[i, :, c].astype(F32)
                dp = both[:, u * TILE : (u + 1) * TILE]
                inner = jnp.sum(dp * probs, axis=0, keepdims=True)
                ds = (probs * (dp - inner)).astype(BF16)
                ds_all[:, c] = ds
                parts.append(nn(keys_t[h * size : (h + 1) * size, :], ds))
        ql[rows, :] = (jnp.concatenate(parts, axis=0).T * scale).astype(BF16)
        dk[win, :] += nn(ds_all[...], qm[...])
        dv[win, :] += nn(p[i], am[...])
        return carry

    lax.fori_loop(0, tok // TILE, tile, 0, unroll=2)
    kl[...] = (dk[...] * scale).astype(BF16)
    vl[...] = dv[...].astype(BF16)


def attention_back(g_one, q, k, v, p, w_out):
    tok, width = g_one.shape
    return call(
        attention_back_kernel,
        [shape((tok, width), BF16)] * 3,
        [g_one, q, k, v, p, w_out],
        [
            VMEM((tok, width), BF16),
            VMEM((width, tok), BF16),
            VMEM((WINDOW, HEADS * TILE), BF16),
            VMEM((width, HEADS * TILE), BF16),
            VMEM((HEADS * TILE, width), BF16),
            VMEM((HEADS * TILE, width), BF16),
            VMEM((tok, width), F32),
            VMEM((tok, width), F32),
        ],
        "attention_backward",
        16_000_000_000,
    )


def project_back_kernel(flat, piece, place, feat, emb, src, g_one, ql, kl, vl, dwo, vg, wa, *rest):
    low_out = rest[0]
    outs, (grads,) = rest[1:-1], rest[-1:]
    tok, width = g_one.shape
    at = feat.shape[1]
    total = jnp.zeros((1, width), F32)
    for i in range(tok // ROWS):
        r = pl.ds(i * ROWS, ROWS)
        e = (
            g_one[r, :]
            + nt(ql[r, :], wa[at : at + width, :])
            + nt(kl[r, :], wa[at + width : at + 2 * width, :])
            + nt(vl[r, :], wa[at + 2 * width : at + 3 * width, :])
        )
        low = e.astype(BF16)
        low_out[r, :] = low
        total += column_sum(low)
    src_t = src[...].T
    grads[at : at + width, :] = nn(src_t, ql[...]).astype(BF16)
    grads[at + width : at + 2 * width, :] = nn(src_t, kl[...]).astype(BF16)
    grads[at + 2 * width : at + 3 * width, :] = nn(emb[...].astype(BF16).T, vl[...]).astype(BF16)
    grads[0:at, :] = nn(feat[...].T, low_out[...]).astype(BF16)
    grads[at + 3 * width :, :] = dwo[...]
    front = jnp.concatenate([total, column_sum(ql[...]), column_sum(vl[...])], axis=0)
    if flat:
        outs[0][...] = grads[...]
        outs[1][...] = vg[...]
        outs[1][0:3, :] = front
        return
    keep, send = outs
    core = place[3]
    for m in range(4):
        to = pl.ds(m * piece, piece)
        keep[to, :] = grads[pl.ds(pl.multiple_of((2 * m + core) * piece, 16), piece), :]
        send[to, :] = grads[pl.ds(pl.multiple_of((2 * m + 1 - core) * piece, 16), piece), :]
    rows = vg.shape[0]
    pad = jnp.zeros((VEC_PAD - rows, width), F32)
    tail = jnp.concatenate([front, vg[3:rows, :], pad], axis=0).astype(BF16)
    for ref in (keep, send):
        ref[4 * piece :, :] = tail


def project_back(flat, place, feat, emb, src, g_one, ql, kl, vl, dwo, vg, wa, piece):
    tok, width = g_one.shape
    outs = [shape((tok, width), BF16)]
    if flat:
        outs += [shape(wa.shape, BF16), shape(vg.shape, F32)]
    else:
        outs += [shape((4 * piece + VEC_PAD, width), BF16)] * 2
    return call(
        functools.partial(project_back_kernel, flat, piece),
        outs,
        [place, feat, emb, src, g_one, ql, kl, vl, dwo, vg, wa],
        [VMEM(wa.shape, BF16)],
        "project_backward",
        2_000_000_000,
        [pltpu.SMEM] + [VMEM] * 10,
    )


def feature_kernel(low, wa, out):
    for i in range(low.shape[0] // ROWS):
        r = pl.ds(i * ROWS, ROWS)
        out[r, :] = nt(low[r, :], wa[0 : out.shape[1], :])


def feature_back(low, wa, feat_dim):
    return call(
        feature_kernel,
        [shape((low.shape[0], feat_dim), F32)],
        [low, wa],
        [],
        "feature_gradient",
        300_000_000,
    )[0]


def plane_kernel(place, own, one, two, three, attn, rest):
    got = (own, one, two, three)
    z = place[0]
    for slot in range(4):

        @pl.when(z == slot)
        def _(slot=slot):
            attn[...] = got[slot][...]
            for plane in range(1, 4):
                rest[plane - 1] = got[slot ^ plane][...]


def pick_planes(place, own, one, two, three):
    return call(
        plane_kernel,
        [shape(own.shape, BF16), shape((3, *own.shape), BF16)],
        [place, own, one, two, three],
        [],
        "pick_planes",
        1_000_000,
        [pltpu.SMEM] + [VMEM] * 4,
    )


def ff_sum_kernel(place, keep, recv, *outs):
    yx = place[1]
    for slot in range(4):
        for plane in range(3):
            at = 4 * plane + (yx ^ slot)
            outs[slot][plane] = (keep[at].astype(F32) + recv[at].astype(F32)).astype(BF16)


def ff_sum(place, keep, recv):
    one = shape((3, *keep.shape[1:]), BF16)
    return call(
        ff_sum_kernel,
        [one] * 4,
        [place, keep, recv],
        [],
        "sum_cores_ff",
        1_000_000,
        [pltpu.SMEM] + [VMEM] * 2,
    )


def four_kernel(a, b, c, d, out):
    out[...] = (
        (a[...].astype(F32) + b[...].astype(F32)) + (c[...].astype(F32) + d[...].astype(F32))
    ).astype(BF16)


def four_sum(a, b, c, d):
    return call(four_kernel, [shape(a.shape, BF16)], [a, b, c, d], [], "sum_plane_ff", 1_000_000)[0]


def tail_sum_kernel(piece, place, keep, recv, *outs):
    yx = place[1]
    vec = keep[4 * piece :, :].astype(F32) + recv[4 * piece :, :].astype(F32)
    for slot in range(4):
        r = pl.ds(pl.multiple_of((yx ^ slot) * piece, 16), piece)
        outs[slot][0:piece, :] = (keep[r, :].astype(F32) + recv[r, :].astype(F32)).astype(BF16)
        outs[slot][piece:, :] = vec.astype(BF16)


def tail_sum(place, keep, recv, piece):
    return call(
        functools.partial(tail_sum_kernel, piece),
        [shape((piece + VEC_PAD, keep.shape[1]), BF16)] * 4,
        [place, keep, recv],
        [],
        "sum_cores_tail",
        1_000_000,
        [pltpu.SMEM] + [VMEM] * 2,
    )


def plane_sum_kernel(place, a, b, c, d, ff, *outs):
    z = place[0]
    total = (
        (a[...].astype(F32) + b[...].astype(F32)) + (c[...].astype(F32) + d[...].astype(F32))
    ).astype(BF16)
    piece = ff.shape[1]
    for slot in range(4):
        goal = z ^ slot
        outs[slot][piece:, :] = total[piece:, :]

        @pl.when(goal == 0)
        def _(slot=slot):
            outs[slot][0:piece, :] = total[0:piece, :]

        @pl.when(goal != 0)
        def _(slot=slot, goal=goal):
            outs[slot][0:piece, :] = ff[jnp.maximum(goal - 1, 0)]


def plane_sum(place, a, b, c, d, ff):
    return call(
        plane_sum_kernel,
        [shape(a.shape, BF16)] * 4,
        [place, a, b, c, d, ff],
        [],
        "sum_plane_tail",
        1_000_000,
        [pltpu.SMEM] + [VMEM] * 5,
    )


def adam_step(weight, moment_one, moment_two, gradient, step_rate, decay_rate):
    moment_one = BETA_ONE * moment_one + (1.0 - BETA_ONE) * gradient
    moment_two = BETA_TWO * moment_two + (1.0 - BETA_TWO) * gradient * gradient
    mean_hat = moment_one / (1.0 - BETA_ONE**STEP)
    square_hat = moment_two / (1.0 - BETA_TWO**STEP)
    weight = weight - step_rate * (
        mean_hat / (jnp.sqrt(square_hat) + ADAM_EPS) + decay_rate * weight
    )
    return (weight, moment_one, moment_two)


def adam_kernel(feat_dim, place, a, b, c, d, w, m, v, vw, vm, vv, *outs):
    total = (a[...].astype(F32) + b[...].astype(F32)) + (c[...].astype(F32) + d[...].astype(F32))
    piece = w.shape[0]
    rows = place[2] * piece + lax.broadcasted_iota(jnp.int32, w.shape, 0)
    rate = jnp.where(rows < feat_dim, 0.1 * RATE, RATE)
    new = adam_step(w[...], m[...], v[...], total[0:piece, :], rate, DECAY)
    for ref, value in zip(outs[:3], new):
        ref[...] = value
    outs[3][...] = new[0].astype(BF16)
    new = adam_step(vw[...], vm[...], vv[...], total[piece : piece + vw.shape[0], :], RATE, 0.0)
    for ref, value in zip(outs[4:], new):
        ref[...] = value


def adam(place, parts, mats, mats_m, mats_v, vecs, vecs_m, vecs_v, feat_dim):
    mat, vec = shape(mats.shape, F32), shape(vecs.shape, F32)
    return call(
        functools.partial(adam_kernel, feat_dim),
        [mat, mat, mat, shape(mats.shape, BF16), vec, vec, vec],
        [place, *parts, mats, mats_m, mats_v, vecs, vecs_m, vecs_v],
        [],
        "adam",
        10_000_000,
        [pltpu.SMEM] + [VMEM] * 10,
    )


def sine_table(within, model_width):
    half_width = model_width // 2
    frequency = jnp.exp(-jnp.log(10000.0) * jnp.arange(half_width, dtype=F32) / half_width)
    angles = within.astype(F32)[:, None] * frequency[None, :]
    return jnp.concatenate([jnp.sin(angles), jnp.cos(angles)], axis=1)


def window_mask(segment):
    tok = segment.shape[0]
    tiles = []
    for i in range(tok // TILE):
        start = min(max((i - 1) * TILE, 0), tok - WINDOW)
        keys = segment[start : start + WINDOW]
        tiles.append(keys[:, None] == segment[i * TILE : (i + 1) * TILE][None, :])
    return jnp.stack(tiles).astype(F32)


def grid_swap(dz, dyx):
    return [(4 * z + yx, 4 * (z ^ dz) + (yx ^ dyx)) for z in range(4) for yx in range(4)]


PAIR_SWAP = [(0, 1), (1, 0)]


def per_device(
    flat,
    features,
    cotangent,
    canvas_lengths,
    crop_ids,
    mats,
    mats_m,
    mats_v,
    vecs,
    vecs_m,
    vecs_v,
):
    tok = features.shape[0]
    feat_dim = features.shape[1]
    width = vecs.shape[1]
    attn_rows = feat_dim + 3 * width + width // 2
    ff_rows = width // 2 + 2 * FF
    piece = mats.shape[0]
    dp, core = lax.axis_index("dp"), lax.axis_index("pair")
    device = lax.axis_index(("dp", "pair"))
    place = jnp.stack([dp // 4, dp % 4, device, core]).astype(jnp.int32)

    position = jnp.arange(tok, dtype=jnp.int32)
    first_len = canvas_lengths[0, 0]
    canvas_id = (position >= first_len).astype(jnp.int32)
    within = position - first_len * canvas_id
    pos_table = sine_table(within, width)
    mask = window_mask(crop_ids * 2 + canvas_id)

    mats_low = mats.astype(BF16)
    if flat:
        gathered = lax.all_gather(mats_low, ("dp", "pair"), axis=0, tiled=True)
        attn_pieces = [gathered[:attn_rows]]
        ff_pieces = [gathered[attn_rows:]]
    else:
        planes = [lax.ppermute(mats_low, "dp", grid_swap(dz, 0)) for dz in (1, 2, 3)]
        one, three = pick_planes(place, mats_low, *planes)
        attn_pieces = [one] + [lax.ppermute(one, "dp", grid_swap(0, s)) for s in (1, 2, 3)]
        attn_pieces += [lax.ppermute(a, "pair", PAIR_SWAP) for a in attn_pieces]
        ff_pieces = [three] + [lax.ppermute(three, "dp", grid_swap(0, s)) for s in (1, 2, 3)]
        ff_pieces += [lax.ppermute(a, "pair", PAIR_SWAP) for a in ff_pieces]

    wa, emb, src, q, k, v, attn, probs = attention(
        flat, place, features, pos_table, mask, vecs, attn_pieces, attn_rows
    )
    output, g_one, w_out, vg, dwo, *ff_grads = feed(
        flat, place, emb, attn, cotangent, vecs, wa, ff_pieces, ff_rows
    )
    if not flat:
        keep, send = ff_grads
        sums = ff_sum(place, keep, lax.ppermute(send, "pair", PAIR_SWAP))
        ff_parts = [sums[0]] + [lax.ppermute(sums[s], "dp", grid_swap(0, s)) for s in (1, 2, 3)]
    ql, kl, vl = attention_back(g_one, q, k, v, probs, w_out)
    if not flat:
        ff = four_sum(*ff_parts)
    low, *tail = project_back(
        flat, place, features, emb, src, g_one, ql, kl, vl, dwo, vg, wa, piece
    )
    feature_grad = feature_back(low, wa, feat_dim)
    if flat:
        grads = jnp.concatenate([tail[0], ff_grads[0]], axis=0).astype(F32)
        total = lax.psum_scatter(grads, ("dp", "pair"), scatter_dimension=0, tiled=True)
        vec_total = lax.psum(tail[1], ("dp", "pair"))
        row_ids = device * piece + jnp.arange(piece, dtype=jnp.int32)
        rate = jnp.where(row_ids < feat_dim, 0.1 * RATE, RATE)[:, None]
        new = adam_step(mats, mats_m, mats_v, total, rate, DECAY)
        new_vec = adam_step(vecs, vecs_m, vecs_v, vec_total, RATE, 0.0)
        return (output, feature_grad, *new, new[0].astype(BF16), *new_vec)
    keep, send = tail
    sums = tail_sum(place, keep, lax.ppermute(send, "pair", PAIR_SWAP), piece)
    parts = [sums[0]] + [lax.ppermute(sums[s], "dp", grid_swap(0, s)) for s in (1, 2, 3)]
    sums = plane_sum(place, *parts, ff)
    parts = [sums[0]] + [lax.ppermute(sums[s], "dp", grid_swap(s, 0)) for s in (1, 2, 3)]
    new = adam(place, parts, mats, mats_m, mats_v, vecs, vecs_m, vecs_v, feat_dim)
    return (output, feature_grad, *new)


def solution(mesh):
    rows = P(("dp", "pair"), None)
    in_specs = (rows, rows, rows, P(("dp", "pair")), rows, rows, rows, P(), P(), P())
    out_specs = (rows, rows, rows, rows, rows, rows, P(), P(), P())
    flat = mesh.shape["dp"] != 16 or mesh.shape["pair"] != 2
    return jax.shard_map(
        functools.partial(per_device, flat),
        mesh=mesh,
        in_specs=in_specs,
        out_specs=out_specs,
        check_vma=False,
    )
```

```python
import functools

import jax
import jax.numpy as jnp
from jax import lax
from jax.experimental import pallas as pl
from jax.experimental.pallas import tpu as pltpu
from jax.sharding import PartitionSpec as P

HEADS = 8
FF = 2048
STEP = 10

EPS_NORM = 1e-05
RATE = 0.2
BETA_ONE = 0.9
BETA_TWO = 0.999
ADAM_EPS = 1e-08
DECAY = 0.0001
MASKED = -1000000000.0

TILE = 128
WINDOW = 384
ROWS = 256
BLOCK = 256
BLOCKS = FF // BLOCK
GELU_A = 0.7978845608028654
GELU_B = 0.044715
VEC_PAD = 32

F32 = jnp.float32
BF16 = jnp.bfloat16
VMEM = pltpu.VMEM


def nn(a, b):
    return lax.dot_general(a, b, (((1,), (0,)), ((), ())), preferred_element_type=F32)


def nt(a, b):
    return lax.dot_general(a, b, (((1,), (1,)), ((), ())), preferred_element_type=F32)


def row_mean(x):
    return jnp.sum(x, axis=1, keepdims=True) * (1.0 / x.shape[1])


def fold_rows(x):
    return jnp.sum(x.reshape(x.shape[0] // 8, 8, x.shape[1]), axis=0)


def column_sum(x):
    return jnp.sum(x.astype(F32), axis=0, keepdims=True)


def head_lanes(h, rows, width):
    lane = lax.broadcasted_iota(jnp.int32, (rows, width), 1)
    size = width // HEADS
    return (lane >= h * size) & (lane < (h + 1) * size)


def window_start(i, tok):
    return jnp.clip((i - 1) * TILE, 0, tok - WINDOW)


def call(kernel, outs, ins, scratch, name, flops, spaces=None, vmem=48):
    spaces = spaces or [VMEM] * len(ins)
    nbytes = sum(a.size * a.dtype.itemsize for a in ins) + sum(
        a.size * a.dtype.itemsize for a in outs
    )
    return pl.pallas_call(
        kernel,
        out_shape=tuple(outs),
        in_specs=[pl.BlockSpec(memory_space=s) for s in spaces],
        out_specs=tuple(pl.BlockSpec(memory_space=VMEM) for _ in outs),
        scratch_shapes=scratch,
        compiler_params=pltpu.CompilerParams(vmem_limit_bytes=vmem << 20),
        cost_estimate=pl.CostEstimate(flops=flops, bytes_accessed=nbytes, transcendentals=0),
        name=name,
    )(*ins)


def shape(dims, kind):
    return jax.ShapeDtypeStruct(dims, kind)


def load_pieces(refs, offsets, dst, sems):
    copies = []
    for ref, offs in zip(refs, offsets):
        if len(ref.shape) == 2:
            views = [ref]
        else:
            views = [ref.at[i] for i in range(ref.shape[0])]
        for view, off in zip(views, offs):
            copies.append(
                pltpu.make_async_copy(
                    view, dst.at[pl.ds(off, view.shape[0]), :], sems.at[len(copies)]
                )
            )
    for copy in copies:
        copy.start()
    for copy in copies:
        copy.wait()


def place_offsets(place, piece, planes):
    offsets = []
    for other in (0, 1):
        for slot in range(4):
            core = place[3] ^ other if other else place[3]
            inner = 2 * (place[1] ^ slot) + core
            offsets.append(
                [pl.multiple_of((8 * plane + inner) * piece, 16) for plane in range(planes)]
            )
    return offsets


def attention_kernel(flat, piece, place, feat, pos, seg_col, seg_row, vec, *rest):
    count = 1 if flat else 8
    pieces, rest = rest[:count], rest[count:]
    w, emb, src, q, k, v, attn, p, v_t, q_t, sems = rest
    tok, width = emb.shape
    feat_dim = feat.shape[1]
    size = width // HEADS
    scale = size ** (-0.5)
    offsets = [[0]] if flat else place_offsets(place, piece, 1)
    load_pieces(pieces, offsets, w, sems)
    for i in range(tok // ROWS):
        r = pl.ds(i * ROWS, ROWS)
        e = nn(feat[r, :], w[0:feat_dim, :]) + vec[0:1, :]
        emb[r, :] = e
        s = (e + pos[r, :]).astype(BF16)
        src[r, :] = s
        low = e.astype(BF16)
        at = feat_dim
        q[r, :] = (nn(s, w[at : at + width, :]) + vec[1:2, :]).astype(BF16)
        k[r, :] = nn(s, w[at + width : at + 2 * width, :]).astype(BF16)
        v[r, :] = (nn(low, w[at + 2 * width : at + 3 * width, :]) + vec[2:3, :]).astype(BF16)
    v_t[...] = v[...].T
    q_t[...] = jnp.zeros_like(q_t)
    masked = MASKED / scale

    def tile(i, carry):
        rows = pl.ds(pl.multiple_of(i * TILE, TILE), TILE)
        win = pl.ds(pl.multiple_of(window_start(i, tok), TILE), WINDOW)
        own_t = q[rows, :].T
        keys = k[win, :]
        vals_t = v_t[:, win]
        allowed = seg_col[win, :] == seg_row[pl.ds(i, 1), :]
        for h in range(HEADS):
            d = slice(h * size, (h + 1) * size)
            q_t[d, h * TILE : (h + 1) * TILE] = own_t[d, :]
        parts = []
        for g in range(HEADS // 2):
            both = nn(keys, q_t[:, 2 * g * TILE : (2 * g + 2) * TILE])
            for u in range(2):
                h = 2 * g + u
                s = jnp.where(allowed, both[:, u * TILE : (u + 1) * TILE], masked)
                top = jnp.max(s, axis=0, keepdims=True)
                e = jnp.exp((s - top) * scale)
                total = jnp.sum(e, axis=0, keepdims=True)
                probs = (e * (1.0 / total)).astype(BF16)
                p[i, :, h * TILE : (h + 1) * TILE] = probs
                parts.append(nn(vals_t[h * size : (h + 1) * size, :], probs))
        attn[rows, :] = jnp.concatenate(parts, axis=0).T.astype(BF16)
        return carry

    lax.fori_loop(0, tok // TILE, tile, 0, unroll=2)


def attention(flat, place, feat, pos, segment, vec, pieces, attn_rows):
    tok, width = feat.shape[0], vec.shape[1]
    piece = pieces[0].shape[0]
    low = shape((tok, width), BF16)
    outs = [
        shape((attn_rows, width), BF16),
        shape((tok, width), F32),
        low,
        low,
        low,
        low,
        low,
        shape((tok // TILE, WINDOW, HEADS * TILE), BF16),
    ]
    seg_col = jnp.broadcast_to(segment[:, None], (tok, TILE))
    ins = [place, feat, pos, seg_col, segment.reshape(-1, TILE), vec, *pieces]
    return call(
        functools.partial(attention_kernel, flat, piece),
        outs,
        ins,
        [
            VMEM((width, tok), BF16),
            VMEM((width, HEADS * TILE), BF16),
            pltpu.SemaphoreType.DMA((8,)),
        ],
        "attention_forward",
        12_000_000_000,
        [pltpu.SMEM] + [VMEM] * 5 + [pl.ANY] * len(pieces),
    )


def feed_kernel(flat, piece, place, emb, attn, cot, vec, wa, *rest):
    count = 1 if flat else 8
    pieces, rest = rest[:count], rest[count:]
    outs = 5 if flat else 6
    res, rest = rest[: outs + 1], rest[outs + 1 :]
    out, g_one, w_out, vec_grad, dwo = res[:5]
    (wf, wh, wh_t, wb_t, half_a, half_b, act, pre, slope, n_t, b_t, o_t, acc, gff, sems) = rest
    halves = (half_a, half_b)
    tok, width = emb.shape
    first = width // 2
    offsets = [[0]] if flat else place_offsets(place, piece, 3)
    load_pieces(pieces, offsets, wf, sems)
    for u in range(2):
        halves[u][...] = wf[first : first + FF, u * 128 : (u + 1) * 128].astype(F32)
    w_out[0:first, :] = wa[wa.shape[0] - first :, :]
    w_out[first:, :] = wf[0:first, :]
    for j in range(BLOCKS):
        c = slice(j * BLOCK, (j + 1) * BLOCK)
        w = jnp.concatenate(
            [halves[u][pl.ds(j, width, stride=BLOCKS), :] for u in range(2)], axis=1
        ).astype(BF16)
        wh[:, c] = w
        wh_t[c, :] = w.T
        wb_t[:, c] = wf[first + FF + j * BLOCK : first + FF + (j + 1) * BLOCK, :].T
    acc[...] = jnp.zeros_like(acc)
    n_t[width : width + 8, :] = jnp.ones((8, tok), BF16)

    def tile(i, carry):
        r = pl.ds(pl.multiple_of(i * ROWS, ROWS), ROWS)
        res_one = emb[r, :] + nn(attn[r, :], w_out[...]) + vec[3:4, :]
        cen = res_one - row_mean(res_one)
        inv_one = lax.rsqrt(row_mean(cen * cen) + EPS_NORM)
        hat_one = cen * inv_one
        normed = hat_one * vec[4:5, :] + vec[5:6, :]
        low = normed.astype(BF16)
        for j in range(BLOCKS):
            c = slice(j * BLOCK, (j + 1) * BLOCK)
            x = nn(low, wh[:, c]) + vec[9 + j : 10 + j, :]
            sq = x * x
            t = jnp.tanh(x * (GELU_A + (GELU_A * GELU_B) * sq))
            half = 0.5 + 0.5 * t
            act[r, c] = (x * half).astype(BF16)
            bend = x * ((2 * GELU_A) + (6 * GELU_A * GELU_B) * sq)
            slope[:, c] = (half + (half - half * half) * bend).astype(BF16)
        res_two = normed + nn(act[r, :], wf[first + FF : first + 2 * FF, :]) + vec[6:7, :]
        cen = res_two - row_mean(res_two)
        inv_two = lax.rsqrt(row_mean(cen * cen) + EPS_NORM)
        hat_two = cen * inv_two
        out[r, :] = hat_two * vec[7:8, :] + vec[8:9, :]
        ct = cot[r, :].astype(F32)
        gs = ct * vec[7:8, :]
        g_two = inv_two * (gs - row_mean(gs) - hat_two * row_mean(gs * hat_two))
        back = g_two.astype(BF16)
        b_t[:, r] = back.T
        acc[0] += fold_rows(back.astype(F32))
        acc[1] += fold_rows(ct * hat_two)
        acc[2] += fold_rows(ct)
        for j in range(BLOCKS):
            c = slice(j * BLOCK, (j + 1) * BLOCK)
            pre[r, c] = (nn(back, wb_t[:, c]) * slope[:, c].astype(F32)).astype(BF16)
        g_norm = g_two + nn(pre[r, :], wh_t[...])
        n_t[0:width, r] = low.T
        gs = g_norm * vec[4:5, :]
        g_res = inv_one * (gs - row_mean(gs) - hat_one * row_mean(gs * hat_one))
        g_one[r, :] = g_res
        out_low = g_res.astype(BF16)
        o_t[:, r] = out_low.T
        acc[3] += fold_rows(out_low.astype(F32))
        acc[4] += fold_rows(g_norm * hat_one)
        acc[5] += fold_rows(g_norm)
        return carry

    lax.fori_loop(0, tok // ROWS, tile, 0)
    for j in range(BLOCKS):
        c = slice(j * BLOCK, (j + 1) * BLOCK)
        g = nn(n_t[...], pre[:, c])
        for u in range(2):
            halves[u][pl.ds(j, width, stride=BLOCKS), :] = g[0:width, u * 128 : (u + 1) * 128]
        vec_grad[9 + j : 10 + j, :] = g[width : width + 1, :]
        at = first + FF + j * BLOCK
        gff[at : at + BLOCK, :] = nn(b_t[...], act[:, c]).T.astype(BF16)
    for u in range(2):
        gff[first : first + FF, u * 128 : (u + 1) * 128] = halves[u][...].astype(BF16)
    g = nn(o_t[...], attn[...]).T.astype(BF16)
    dwo[...] = g[0:first, :]
    gff[0:first, :] = g[first:, :]
    sums = jnp.sum(acc[...], axis=1)
    vec_grad[0:3, :] = jnp.zeros((3, width), F32)
    for row, at in ((3, 3), (4, 4), (5, 5), (6, 0), (7, 1), (8, 2)):
        vec_grad[row : row + 1, :] = sums[at : at + 1, :]
    if flat:
        res[5][...] = gff[...]
    else:
        split_cores(place, gff, res[5], res[6])


def split_cores(place, grads, keep, send):
    core = place[3]
    piece = keep.shape[1]
    for m in range(keep.shape[0]):
        keep[m] = grads[pl.ds(pl.multiple_of((2 * m + core) * piece, 16), piece), :]
        send[m] = grads[pl.ds(pl.multiple_of((2 * m + 1 - core) * piece, 16), piece), :]


def feed(flat, place, emb, attn, cot, vec, wa, pieces, ff_rows):
    tok, width = emb.shape
    piece = pieces[0].shape[-2]
    outs = [
        shape((tok, width), F32),
        shape((tok, width), F32),
        shape((width, width), BF16),
        shape(vec.shape, F32),
        shape((width // 2, width), BF16),
    ]
    if flat:
        outs += [shape((ff_rows, width), BF16)]
    else:
        outs += [shape((ff_rows // piece // 2, piece, width), BF16)] * 2
    return call(
        functools.partial(feed_kernel, flat, piece),
        outs,
        [place, emb, attn, cot, vec, wa, *pieces],
        [
            VMEM((ff_rows, width), BF16),
            VMEM((width, FF), BF16),
            VMEM((FF, width), BF16),
            VMEM((width, FF), BF16),
            VMEM((FF, 128), F32),
            VMEM((FF, 128), F32),
            VMEM((tok, FF), BF16),
            VMEM((tok, FF), BF16),
            VMEM((ROWS, FF), BF16),
            VMEM((width + 8, tok), BF16),
            VMEM((width, tok), BF16),
            VMEM((width, tok), BF16),
            VMEM((6, 8, width), F32),
            VMEM((ff_rows, width), BF16),
            pltpu.SemaphoreType.DMA((24,)),
        ],
        "feed_forward_both",
        14_000_000_000,
        [pltpu.SMEM] + [VMEM] * 5 + [pl.ANY] * len(pieces),
    )


def attention_back_kernel(g_one, q, k, v, p, w_out, ql, kl, vl, ag, k_t, ds_all, a_t, qm, am, dk, dv):
    tok, width = g_one.shape
    size = width // HEADS
    scale = size ** (-0.5)
    for i in range(tok // ROWS):
        r = pl.ds(i * ROWS, ROWS)
        ag[r, :] = nt(g_one[r, :].astype(BF16), w_out[...]).astype(BF16)
    k_t[...] = k[...].T
    dk[...] = jnp.zeros_like(dk)
    dv[...] = jnp.zeros_like(dv)
    a_t[...] = jnp.zeros_like(a_t)

    def tile(i, carry):
        rows = pl.ds(pl.multiple_of(i * TILE, TILE), TILE)
        win = pl.ds(pl.multiple_of(window_start(i, tok), TILE), WINDOW)
        own_q = q[rows, :]
        own_a = ag[rows, :]
        own_t = own_a.T
        vals = v[win, :]
        keys_t = k_t[:, win]
        for h in range(HEADS):
            lanes = head_lanes(h, TILE, width)
            d = slice(h * size, (h + 1) * size)
            c = slice(h * TILE, (h + 1) * TILE)
            a_t[d, c] = own_t[d, :]
            qm[c, :] = jnp.where(lanes, own_q, jnp.zeros_like(own_q))
            am[c, :] = jnp.where(lanes, own_a, jnp.zeros_like(own_a))
        parts = []
        for g in range(HEADS // 2):
            both = nn(vals, a_t[:, 2 * g * TILE : (2 * g + 2) * TILE])
            for u in range(2):
                h = 2 * g + u
                c = slice(h * TILE, (h + 1) * TILE)
                probs = p[i, :, c].astype(F32)
                dp = both[:, u * TILE : (u + 1) * TILE]
                inner = jnp.sum(dp * probs, axis=0, keepdims=True)
                ds = (probs * (dp - inner)).astype(BF16)
                ds_all[:, c] = ds
                parts.append(nn(keys_t[h * size : (h + 1) * size, :], ds))
        ql[rows, :] = (jnp.concatenate(parts, axis=0).T * scale).astype(BF16)
        dk[win, :] += nn(ds_all[...], qm[...])
        dv[win, :] += nn(p[i], am[...])
        return carry

    lax.fori_loop(0, tok // TILE, tile, 0, unroll=2)
    kl[...] = (dk[...] * scale).astype(BF16)
    vl[...] = dv[...].astype(BF16)


def attention_back(g_one, q, k, v, p, w_out):
    tok, width = g_one.shape
    return call(
        attention_back_kernel,
        [shape((tok, width), BF16)] * 3,
        [g_one, q, k, v, p, w_out],
        [
            VMEM((tok, width), BF16),
            VMEM((width, tok), BF16),
            VMEM((WINDOW, HEADS * TILE), BF16),
            VMEM((width, HEADS * TILE), BF16),
            VMEM((HEADS * TILE, width), BF16),
            VMEM((HEADS * TILE, width), BF16),
            VMEM((tok, width), F32),
            VMEM((tok, width), F32),
        ],
        "attention_backward",
        16_000_000_000,
    )


def project_back_kernel(flat, piece, place, feat, emb, src, g_one, ql, kl, vl, dwo, vg, wa, *rest):
    low_out = rest[0]
    outs, (grads,) = rest[1:-1], rest[-1:]
    tok, width = g_one.shape
    at = feat.shape[1]
    total = jnp.zeros((1, width), F32)
    for i in range(tok // ROWS):
        r = pl.ds(i * ROWS, ROWS)
        e = (
            g_one[r, :]
            + nt(ql[r, :], wa[at : at + width, :])
            + nt(kl[r, :], wa[at + width : at + 2 * width, :])
            + nt(vl[r, :], wa[at + 2 * width : at + 3 * width, :])
        )
        low = e.astype(BF16)
        low_out[r, :] = low
        total += column_sum(low)
    src_t = src[...].T
    grads[at : at + width, :] = nn(src_t, ql[...]).astype(BF16)
    grads[at + width : at + 2 * width, :] = nn(src_t, kl[...]).astype(BF16)
    grads[at + 2 * width : at + 3 * width, :] = nn(emb[...].astype(BF16).T, vl[...]).astype(BF16)
    grads[0:at, :] = nn(feat[...].T, low_out[...]).astype(BF16)
    grads[at + 3 * width :, :] = dwo[...]
    front = jnp.concatenate([total, column_sum(ql[...]), column_sum(vl[...])], axis=0)
    if flat:
        outs[0][...] = grads[...]
        outs[1][...] = vg[...]
        outs[1][0:3, :] = front
        return
    keep, send = outs
    core = place[3]
    for m in range(4):
        to = pl.ds(m * piece, piece)
        keep[to, :] = grads[pl.ds(pl.multiple_of((2 * m + core) * piece, 16), piece), :]
        send[to, :] = grads[pl.ds(pl.multiple_of((2 * m + 1 - core) * piece, 16), piece), :]
    rows = vg.shape[0]
    pad = jnp.zeros((VEC_PAD - rows, width), F32)
    tail = jnp.concatenate([front, vg[3:rows, :], pad], axis=0).astype(BF16)
    for ref in (keep, send):
        ref[4 * piece :, :] = tail


def project_back(flat, place, feat, emb, src, g_one, ql, kl, vl, dwo, vg, wa, piece):
    tok, width = g_one.shape
    outs = [shape((tok, width), BF16)]
    if flat:
        outs += [shape(wa.shape, BF16), shape(vg.shape, F32)]
    else:
        outs += [shape((4 * piece + VEC_PAD, width), BF16)] * 2
    return call(
        functools.partial(project_back_kernel, flat, piece),
        outs,
        [place, feat, emb, src, g_one, ql, kl, vl, dwo, vg, wa],
        [VMEM(wa.shape, BF16)],
        "project_backward",
        2_000_000_000,
        [pltpu.SMEM] + [VMEM] * 10,
    )


def feature_kernel(low, wa, out):
    for i in range(low.shape[0] // ROWS):
        r = pl.ds(i * ROWS, ROWS)
        out[r, :] = nt(low[r, :], wa[0 : out.shape[1], :])


def feature_back(low, wa, feat_dim):
    return call(
        feature_kernel,
        [shape((low.shape[0], feat_dim), F32)],
        [low, wa],
        [],
        "feature_gradient",
        300_000_000,
    )[0]


def plane_kernel(place, own, one, two, three, attn, rest):
    got = (own, one, two, three)
    z = place[0]
    for slot in range(4):

        @pl.when(z == slot)
        def _(slot=slot):
            attn[...] = got[slot][...]
            for plane in range(1, 4):
                rest[plane - 1] = got[slot ^ plane][...]


def pick_planes(place, own, one, two, three):
    return call(
        plane_kernel,
        [shape(own.shape, BF16), shape((3, *own.shape), BF16)],
        [place, own, one, two, three],
        [],
        "pick_planes",
        1_000_000,
        [pltpu.SMEM] + [VMEM] * 4,
    )


def ff_sum_kernel(place, keep, recv, *outs):
    yx = place[1]
    for slot in range(4):
        for plane in range(3):
            at = 4 * plane + (yx ^ slot)
            outs[slot][plane] = (keep[at].astype(F32) + recv[at].astype(F32)).astype(BF16)


def ff_sum(place, keep, recv):
    one = shape((3, *keep.shape[1:]), BF16)
    return call(
        ff_sum_kernel,
        [one] * 4,
        [place, keep, recv],
        [],
        "sum_cores_ff",
        1_000_000,
        [pltpu.SMEM] + [VMEM] * 2,
    )


def four_kernel(a, b, c, d, out):
    out[...] = (
        (a[...].astype(F32) + b[...].astype(F32)) + (c[...].astype(F32) + d[...].astype(F32))
    ).astype(BF16)


def four_sum(a, b, c, d):
    return call(four_kernel, [shape(a.shape, BF16)], [a, b, c, d], [], "sum_plane_ff", 1_000_000)[0]


def tail_sum_kernel(piece, place, keep, recv, *outs):
    yx = place[1]
    vec = keep[4 * piece :, :].astype(F32) + recv[4 * piece :, :].astype(F32)
    for slot in range(4):
        r = pl.ds(pl.multiple_of((yx ^ slot) * piece, 16), piece)
        outs[slot][0:piece, :] = (keep[r, :].astype(F32) + recv[r, :].astype(F32)).astype(BF16)
        outs[slot][piece:, :] = vec.astype(BF16)


def tail_sum(place, keep, recv, piece):
    return call(
        functools.partial(tail_sum_kernel, piece),
        [shape((piece + VEC_PAD, keep.shape[1]), BF16)] * 4,
        [place, keep, recv],
        [],
        "sum_cores_tail",
        1_000_000,
        [pltpu.SMEM] + [VMEM] * 2,
    )


def plane_sum_kernel(place, a, b, c, d, ff, *outs):
    z = place[0]
    total = (
        (a[...].astype(F32) + b[...].astype(F32)) + (c[...].astype(F32) + d[...].astype(F32))
    ).astype(BF16)
    piece = ff.shape[1]
    for slot in range(4):
        goal = z ^ slot
        outs[slot][piece:, :] = total[piece:, :]

        @pl.when(goal == 0)
        def _(slot=slot):
            outs[slot][0:piece, :] = total[0:piece, :]

        @pl.when(goal != 0)
        def _(slot=slot, goal=goal):
            outs[slot][0:piece, :] = ff[jnp.maximum(goal - 1, 0)]


def plane_sum(place, a, b, c, d, ff):
    return call(
        plane_sum_kernel,
        [shape(a.shape, BF16)] * 4,
        [place, a, b, c, d, ff],
        [],
        "sum_plane_tail",
        1_000_000,
        [pltpu.SMEM] + [VMEM] * 5,
    )


def adam_step(weight, moment_one, moment_two, gradient, step_rate, decay_rate):
    moment_one = BETA_ONE * moment_one + (1.0 - BETA_ONE) * gradient
    moment_two = BETA_TWO * moment_two + (1.0 - BETA_TWO) * gradient * gradient
    mean_hat = moment_one / (1.0 - BETA_ONE**STEP)
    square_hat = moment_two / (1.0 - BETA_TWO**STEP)
    weight = weight - step_rate * (
        mean_hat / (jnp.sqrt(square_hat) + ADAM_EPS) + decay_rate * weight
    )
    return (weight, moment_one, moment_two)


def adam_kernel(feat_dim, place, a, b, c, d, w, m, v, vw, vm, vv, *outs):
    total = (a[...].astype(F32) + b[...].astype(F32)) + (c[...].astype(F32) + d[...].astype(F32))
    piece = w.shape[0]
    rows = place[2] * piece + lax.broadcasted_iota(jnp.int32, w.shape, 0)
    rate = jnp.where(rows < feat_dim, 0.1 * RATE, RATE)
    new = adam_step(w[...], m[...], v[...], total[0:piece, :], rate, DECAY)
    for ref, value in zip(outs[:3], new):
        ref[...] = value
    outs[3][...] = new[0].astype(BF16)
    new = adam_step(vw[...], vm[...], vv[...], total[piece : piece + vw.shape[0], :], RATE, 0.0)
    for ref, value in zip(outs[4:], new):
        ref[...] = value


def adam(place, parts, mats, mats_m, mats_v, vecs, vecs_m, vecs_v, feat_dim):
    mat, vec = shape(mats.shape, F32), shape(vecs.shape, F32)
    return call(
        functools.partial(adam_kernel, feat_dim),
        [mat, mat, mat, shape(mats.shape, BF16), vec, vec, vec],
        [place, *parts, mats, mats_m, mats_v, vecs, vecs_m, vecs_v],
        [],
        "adam",
        10_000_000,
        [pltpu.SMEM] + [VMEM] * 10,
    )


def sine_table(within, model_width):
    half_width = model_width // 2
    frequency = jnp.exp(-jnp.log(10000.0) * jnp.arange(half_width, dtype=F32) / half_width)
    angles = within.astype(F32)[:, None] * frequency[None, :]
    return jnp.concatenate([jnp.sin(angles), jnp.cos(angles)], axis=1)


def grid_swap(dz, dyx):
    return [(4 * z + yx, 4 * (z ^ dz) + (yx ^ dyx)) for z in range(4) for yx in range(4)]


PAIR_SWAP = [(0, 1), (1, 0)]


def per_device(
    flat,
    features,
    cotangent,
    canvas_lengths,
    crop_ids,
    mats,
    mats_m,
    mats_v,
    vecs,
    vecs_m,
    vecs_v,
):
    tok = features.shape[0]
    feat_dim = features.shape[1]
    width = vecs.shape[1]
    attn_rows = feat_dim + 3 * width + width // 2
    ff_rows = width // 2 + 2 * FF
    piece = mats.shape[0]
    dp, core = lax.axis_index("dp"), lax.axis_index("pair")
    device = lax.axis_index(("dp", "pair"))
    place = jnp.stack([dp // 4, dp % 4, device, core]).astype(jnp.int32)

    position = jnp.arange(tok, dtype=jnp.int32)
    first_len = canvas_lengths[0, 0]
    canvas_id = (position >= first_len).astype(jnp.int32)
    within = position - first_len * canvas_id
    pos_table = sine_table(within, width)
    segment = crop_ids * 2 + canvas_id

    mats_low = mats.astype(BF16)
    if flat:
        gathered = lax.all_gather(mats_low, ("dp", "pair"), axis=0, tiled=True)
        attn_pieces = [gathered[:attn_rows]]
        ff_pieces = [gathered[attn_rows:]]
    else:
        planes = [lax.ppermute(mats_low, "dp", grid_swap(dz, 0)) for dz in (1, 2, 3)]
        one, three = pick_planes(place, mats_low, *planes)
        attn_pieces = [one] + [lax.ppermute(one, "dp", grid_swap(0, s)) for s in (1, 2, 3)]
        attn_pieces += [lax.ppermute(a, "pair", PAIR_SWAP) for a in attn_pieces]
        ff_pieces = [three] + [lax.ppermute(three, "dp", grid_swap(0, s)) for s in (1, 2, 3)]

    wa, emb, src, q, k, v, attn, probs = attention(
        flat, place, features, pos_table, segment, vecs, attn_pieces, attn_rows
    )
    if not flat:
        attn, *ff_pieces = lax.optimization_barrier((attn, *ff_pieces))
        ff_pieces += [lax.ppermute(a, "pair", PAIR_SWAP) for a in ff_pieces]
    output, g_one, w_out, vg, dwo, *ff_grads = feed(
        flat, place, emb, attn, cotangent, vecs, wa, ff_pieces, ff_rows
    )
    if not flat:
        keep, send = ff_grads
        sums = ff_sum(place, keep, lax.ppermute(send, "pair", PAIR_SWAP))
        g_one, *sums = lax.optimization_barrier((g_one, *sums))
        ff_parts = [sums[0]] + [lax.ppermute(sums[s], "dp", grid_swap(0, s)) for s in (1, 2, 3)]
    ql, kl, vl = attention_back(g_one, q, k, v, probs, w_out)
    if not flat:
        ql, kl, vl, *ff_parts = lax.optimization_barrier((ql, kl, vl, *ff_parts))
        ff = four_sum(*ff_parts)
    low, *tail = project_back(
        flat, place, features, emb, src, g_one, ql, kl, vl, dwo, vg, wa, piece
    )
    feature_grad = feature_back(low, wa, feat_dim)
    if flat:
        grads = jnp.concatenate([tail[0], ff_grads[0]], axis=0).astype(F32)
        total = lax.psum_scatter(grads, ("dp", "pair"), scatter_dimension=0, tiled=True)
        vec_total = lax.psum(tail[1], ("dp", "pair"))
        row_ids = device * piece + jnp.arange(piece, dtype=jnp.int32)
        rate = jnp.where(row_ids < feat_dim, 0.1 * RATE, RATE)[:, None]
        new = adam_step(mats, mats_m, mats_v, total, rate, DECAY)
        new_vec = adam_step(vecs, vecs_m, vecs_v, vec_total, RATE, 0.0)
        return (output, feature_grad, *new, new[0].astype(BF16), *new_vec)
    keep, send = tail
    sums = tail_sum(place, keep, lax.ppermute(send, "pair", PAIR_SWAP), piece)
    parts = [sums[0]] + [lax.ppermute(sums[s], "dp", grid_swap(0, s)) for s in (1, 2, 3)]
    sums = plane_sum(place, *parts, ff)
    parts = [sums[0]] + [lax.ppermute(sums[s], "dp", grid_swap(s, 0)) for s in (1, 2, 3)]
    new = adam(place, parts, mats, mats_m, mats_v, vecs, vecs_m, vecs_v, feat_dim)
    return (output, feature_grad, *new)


def solution(mesh):
    rows = P(("dp", "pair"), None)
    in_specs = (rows, rows, rows, P(("dp", "pair")), rows, rows, rows, P(), P(), P())
    out_specs = (rows, rows, rows, rows, rows, rows, P(), P(), P())
    flat = mesh.shape["dp"] != 16 or mesh.shape["pair"] != 2
    return jax.shard_map(
        functools.partial(per_device, flat),
        mesh=mesh,
        in_specs=in_specs,
        out_specs=out_specs,
        check_vma=False,
    )
```

```python
import functools

import jax
import jax.numpy as jnp
from jax import lax
from jax.experimental import pallas as pl
from jax.experimental.pallas import tpu as pltpu
from jax.sharding import PartitionSpec as P

HEADS = 8
FF = 2048
STEP = 10

EPS_NORM = 1e-05
RATE = 0.2
BETA_ONE = 0.9
BETA_TWO = 0.999
ADAM_EPS = 1e-08
DECAY = 0.0001
MASKED = -1000000000.0

TILE = 128
WINDOW = 384
ROWS = 256
BLOCK = 256
BLOCKS = FF // BLOCK
GELU_A = 0.7978845608028654
GELU_B = 0.044715
VEC_PAD = 32

F32 = jnp.float32
BF16 = jnp.bfloat16
VMEM = pltpu.VMEM


def nn(a, b):
    return lax.dot_general(a, b, (((1,), (0,)), ((), ())), preferred_element_type=F32)


def nt(a, b):
    return lax.dot_general(a, b, (((1,), (1,)), ((), ())), preferred_element_type=F32)


def row_mean(x):
    return jnp.sum(x, axis=1, keepdims=True) * (1.0 / x.shape[1])


def fold_rows(x):
    return jnp.sum(x.reshape(x.shape[0] // 8, 8, x.shape[1]), axis=0)


def column_sum(x):
    return jnp.sum(x.astype(F32), axis=0, keepdims=True)


def head_lanes(h, rows, width):
    lane = lax.broadcasted_iota(jnp.int32, (rows, width), 1)
    size = width // HEADS
    return (lane >= h * size) & (lane < (h + 1) * size)


def window_start(i, tok):
    return jnp.clip((i - 1) * TILE, 0, tok - WINDOW)


def call(kernel, outs, ins, scratch, name, flops, spaces=None, vmem=12):
    spaces = spaces or [VMEM] * len(ins)
    nbytes = sum(a.size * a.dtype.itemsize for a in ins) + sum(
        a.size * a.dtype.itemsize for a in outs
    )
    return pl.pallas_call(
        kernel,
        out_shape=tuple(outs),
        in_specs=[pl.BlockSpec(memory_space=s) for s in spaces],
        out_specs=tuple(pl.BlockSpec(memory_space=VMEM) for _ in outs),
        scratch_shapes=scratch,
        compiler_params=pltpu.CompilerParams(vmem_limit_bytes=vmem << 20),
        cost_estimate=pl.CostEstimate(flops=flops, bytes_accessed=nbytes, transcendentals=0),
        name=name,
    )(*ins)


def shape(dims, kind):
    return jax.ShapeDtypeStruct(dims, kind)


def load_pieces(refs, offsets, dst, sems):
    copies = []
    for ref, offs in zip(refs, offsets):
        if len(ref.shape) == 2:
            views = [ref]
        else:
            views = [ref.at[i] for i in range(ref.shape[0])]
        for view, off in zip(views, offs):
            copies.append(
                pltpu.make_async_copy(
                    view, dst.at[pl.ds(off, view.shape[0]), :], sems.at[len(copies)]
                )
            )
    for copy in copies:
        copy.start()
    for copy in copies:
        copy.wait()


def place_offsets(place, piece, planes):
    offsets = []
    for other in (0, 1):
        for slot in range(4):
            core = place[3] ^ other if other else place[3]
            inner = 2 * (place[1] ^ slot) + core
            offsets.append(
                [pl.multiple_of((8 * plane + inner) * piece, 16) for plane in range(planes)]
            )
    return offsets


def attention_kernel(flat, piece, place, feat, pos, seg_col, seg_row, vec, *rest):
    count = 1 if flat else 8
    pieces, rest = rest[:count], rest[count:]
    w, emb, src, q, k, v, attn, p, v_t, q_t, sems = rest
    tok, width = emb.shape
    feat_dim = feat.shape[1]
    size = width // HEADS
    scale = size ** (-0.5)
    offsets = [[0]] if flat else place_offsets(place, piece, 1)
    load_pieces(pieces, offsets, w, sems)
    for i in range(tok // ROWS):
        r = pl.ds(i * ROWS, ROWS)
        e = nn(feat[r, :], w[0:feat_dim, :]) + vec[0:1, :]
        emb[r, :] = e
        s = (e + pos[r, :]).astype(BF16)
        src[r, :] = s
        low = e.astype(BF16)
        at = feat_dim
        q[r, :] = (nn(s, w[at : at + width, :]) + vec[1:2, :]).astype(BF16)
        k[r, :] = nn(s, w[at + width : at + 2 * width, :]).astype(BF16)
        v[r, :] = (nn(low, w[at + 2 * width : at + 3 * width, :]) + vec[2:3, :]).astype(BF16)
    v_t[...] = v[...].T
    q_t[...] = jnp.zeros_like(q_t)
    masked = MASKED / scale

    def tile(i, carry):
        rows = pl.ds(pl.multiple_of(i * TILE, TILE), TILE)
        win = pl.ds(pl.multiple_of(window_start(i, tok), TILE), WINDOW)
        own_t = q[rows, :].T
        keys = k[win, :]
        vals_t = v_t[:, win]
        allowed = seg_col[win, :] == seg_row[pl.ds(i, 1), :]
        for h in range(HEADS):
            d = slice(h * size, (h + 1) * size)
            q_t[d, h * TILE : (h + 1) * TILE] = own_t[d, :]
        parts = []
        for g in range(HEADS // 2):
            both = nn(keys, q_t[:, 2 * g * TILE : (2 * g + 2) * TILE])
            for u in range(2):
                h = 2 * g + u
                s = jnp.where(allowed, both[:, u * TILE : (u + 1) * TILE], masked)
                top = jnp.max(s, axis=0, keepdims=True)
                e = jnp.exp((s - top) * scale)
                total = jnp.sum(e, axis=0, keepdims=True)
                probs = (e * (1.0 / total)).astype(BF16)
                p[i, :, h * TILE : (h + 1) * TILE] = probs
                parts.append(nn(vals_t[h * size : (h + 1) * size, :], probs))
        attn[rows, :] = jnp.concatenate(parts, axis=0).T.astype(BF16)
        return carry

    lax.fori_loop(0, tok // TILE, tile, 0, unroll=2)


def attention(flat, place, feat, pos, segment, vec, pieces, attn_rows):
    tok, width = feat.shape[0], vec.shape[1]
    piece = pieces[0].shape[0]
    low = shape((tok, width), BF16)
    outs = [
        shape((attn_rows, width), BF16),
        shape((tok, width), F32),
        low,
        low,
        low,
        low,
        low,
        shape((tok // TILE, WINDOW, HEADS * TILE), BF16),
    ]
    ins = [place, feat, pos, *segment, vec, *pieces]
    return call(
        functools.partial(attention_kernel, flat, piece),
        outs,
        ins,
        [
            VMEM((width, tok), BF16),
            VMEM((width, HEADS * TILE), BF16),
            pltpu.SemaphoreType.DMA((8,)),
        ],
        "attention_forward",
        12_000_000_000,
        [pltpu.SMEM] + [VMEM] * 5 + [pl.ANY] * len(pieces),
        vmem=20,
    )


def feed_kernel(flat, piece, place, emb, attn, cot, vec, wa, *rest):
    count = 1 if flat else 8
    pieces, rest = rest[:count], rest[count:]
    outs = 5 if flat else 6
    res, rest = rest[: outs + 1], rest[outs + 1 :]
    out, g_one, w_out, vec_grad, dwo = res[:5]
    (wf, wh, wh_t, wb_t, half_a, half_b, act, pre, slope, n_t, b_t, o_t, acc, gff, sems) = rest
    halves = (half_a, half_b)
    tok, width = emb.shape
    first = width // 2
    offsets = [[0]] if flat else place_offsets(place, piece, 3)
    load_pieces(pieces, offsets, wf, sems)
    for u in range(2):
        halves[u][...] = wf[first : first + FF, u * 128 : (u + 1) * 128].astype(F32)
    w_out[0:first, :] = wa[wa.shape[0] - first :, :]
    w_out[first:, :] = wf[0:first, :]
    for j in range(BLOCKS):
        c = slice(j * BLOCK, (j + 1) * BLOCK)
        w = jnp.concatenate(
            [halves[u][pl.ds(j, width, stride=BLOCKS), :] for u in range(2)], axis=1
        ).astype(BF16)
        wh[:, c] = w
        wh_t[c, :] = w.T
        wb_t[:, c] = wf[first + FF + j * BLOCK : first + FF + (j + 1) * BLOCK, :].T
    acc[...] = jnp.zeros_like(acc)
    n_t[width : width + 8, :] = jnp.ones((8, tok), BF16)

    def tile(i, carry):
        r = pl.ds(pl.multiple_of(i * ROWS, ROWS), ROWS)
        res_one = emb[r, :] + nn(attn[r, :], w_out[...]) + vec[3:4, :]
        cen = res_one - row_mean(res_one)
        inv_one = lax.rsqrt(row_mean(cen * cen) + EPS_NORM)
        hat_one = cen * inv_one
        normed = hat_one * vec[4:5, :] + vec[5:6, :]
        low = normed.astype(BF16)
        for j in range(BLOCKS):
            c = slice(j * BLOCK, (j + 1) * BLOCK)
            x = nn(low, wh[:, c]) + vec[9 + j : 10 + j, :]
            sq = x * x
            t = jnp.tanh(x * (GELU_A + (GELU_A * GELU_B) * sq))
            half = 0.5 + 0.5 * t
            act[r, c] = (x * half).astype(BF16)
            bend = x * ((2 * GELU_A) + (6 * GELU_A * GELU_B) * sq)
            slope[:, c] = (half + (half - half * half) * bend).astype(BF16)
        res_two = normed + nn(act[r, :], wf[first + FF : first + 2 * FF, :]) + vec[6:7, :]
        cen = res_two - row_mean(res_two)
        inv_two = lax.rsqrt(row_mean(cen * cen) + EPS_NORM)
        hat_two = cen * inv_two
        out[r, :] = hat_two * vec[7:8, :] + vec[8:9, :]
        ct = cot[r, :].astype(F32)
        gs = ct * vec[7:8, :]
        g_two = inv_two * (gs - row_mean(gs) - hat_two * row_mean(gs * hat_two))
        back = g_two.astype(BF16)
        b_t[:, r] = back.T
        acc[0] += fold_rows(back.astype(F32))
        acc[1] += fold_rows(ct * hat_two)
        acc[2] += fold_rows(ct)
        for j in range(BLOCKS):
            c = slice(j * BLOCK, (j + 1) * BLOCK)
            pre[r, c] = (nn(back, wb_t[:, c]) * slope[:, c].astype(F32)).astype(BF16)
        g_norm = g_two + nn(pre[r, :], wh_t[...])
        n_t[0:width, r] = low.T
        gs = g_norm * vec[4:5, :]
        g_res = inv_one * (gs - row_mean(gs) - hat_one * row_mean(gs * hat_one))
        g_one[r, :] = g_res
        out_low = g_res.astype(BF16)
        o_t[:, r] = out_low.T
        acc[3] += fold_rows(out_low.astype(F32))
        acc[4] += fold_rows(g_norm * hat_one)
        acc[5] += fold_rows(g_norm)
        return carry

    lax.fori_loop(0, tok // ROWS, tile, 0)
    for j in range(BLOCKS):
        c = slice(j * BLOCK, (j + 1) * BLOCK)
        g = nn(n_t[...], pre[:, c])
        for u in range(2):
            halves[u][pl.ds(j, width, stride=BLOCKS), :] = g[0:width, u * 128 : (u + 1) * 128]
        vec_grad[9 + j : 10 + j, :] = g[width : width + 1, :]
        at = first + FF + j * BLOCK
        gff[at : at + BLOCK, :] = nn(b_t[...], act[:, c]).T.astype(BF16)
    for u in range(2):
        gff[first : first + FF, u * 128 : (u + 1) * 128] = halves[u][...].astype(BF16)
    g = nn(o_t[...], attn[...]).T.astype(BF16)
    dwo[...] = g[0:first, :]
    gff[0:first, :] = g[first:, :]
    sums = jnp.sum(acc[...], axis=1)
    vec_grad[0:3, :] = jnp.zeros((3, width), F32)
    for row, at in ((3, 3), (4, 4), (5, 5), (6, 0), (7, 1), (8, 2)):
        vec_grad[row : row + 1, :] = sums[at : at + 1, :]
    if flat:
        res[5][...] = gff[...]
    else:
        split_cores(place, gff, res[5], res[6])


def split_cores(place, grads, keep, send):
    core = place[3]
    piece = keep.shape[1]
    for m in range(keep.shape[0]):
        keep[m] = grads[pl.ds(pl.multiple_of((2 * m + core) * piece, 16), piece), :]
        send[m] = grads[pl.ds(pl.multiple_of((2 * m + 1 - core) * piece, 16), piece), :]


def feed(flat, place, emb, attn, cot, vec, wa, pieces, ff_rows):
    tok, width = emb.shape
    piece = pieces[0].shape[-2]
    outs = [
        shape((tok, width), F32),
        shape((tok, width), F32),
        shape((width, width), BF16),
        shape(vec.shape, F32),
        shape((width // 2, width), BF16),
    ]
    if flat:
        outs += [shape((ff_rows, width), BF16)]
    else:
        outs += [shape((ff_rows // piece // 2, piece, width), BF16)] * 2
    return call(
        functools.partial(feed_kernel, flat, piece),
        outs,
        [place, emb, attn, cot, vec, wa, *pieces],
        [
            VMEM((ff_rows, width), BF16),
            VMEM((width, FF), BF16),
            VMEM((FF, width), BF16),
            VMEM((width, FF), BF16),
            VMEM((FF, 128), F32),
            VMEM((FF, 128), F32),
            VMEM((tok, FF), BF16),
            VMEM((tok, FF), BF16),
            VMEM((ROWS, FF), BF16),
            VMEM((width + 8, tok), BF16),
            VMEM((width, tok), BF16),
            VMEM((width, tok), BF16),
            VMEM((6, 8, width), F32),
            VMEM((ff_rows, width), BF16),
            pltpu.SemaphoreType.DMA((24,)),
        ],
        "feed_forward_both",
        14_000_000_000,
        [pltpu.SMEM] + [VMEM] * 5 + [pl.ANY] * len(pieces),
        vmem=34,
    )


def attention_back_kernel(g_one, q, k, v, p, w_out, ql, kl, vl, ag, k_t, ds_all, a_t, qm, am, dk, dv):
    tok, width = g_one.shape
    size = width // HEADS
    scale = size ** (-0.5)
    for i in range(tok // ROWS):
        r = pl.ds(i * ROWS, ROWS)
        ag[r, :] = nt(g_one[r, :].astype(BF16), w_out[...]).astype(BF16)
    k_t[...] = k[...].T
    dk[...] = jnp.zeros_like(dk)
    dv[...] = jnp.zeros_like(dv)
    a_t[...] = jnp.zeros_like(a_t)

    def tile(i, carry):
        rows = pl.ds(pl.multiple_of(i * TILE, TILE), TILE)
        win = pl.ds(pl.multiple_of(window_start(i, tok), TILE), WINDOW)
        own_q = q[rows, :]
        own_a = ag[rows, :]
        own_t = own_a.T
        vals = v[win, :]
        keys_t = k_t[:, win]
        for h in range(HEADS):
            lanes = head_lanes(h, TILE, width)
            d = slice(h * size, (h + 1) * size)
            c = slice(h * TILE, (h + 1) * TILE)
            a_t[d, c] = own_t[d, :]
            qm[c, :] = jnp.where(lanes, own_q, jnp.zeros_like(own_q))
            am[c, :] = jnp.where(lanes, own_a, jnp.zeros_like(own_a))
        parts = []
        for g in range(HEADS // 2):
            both = nn(vals, a_t[:, 2 * g * TILE : (2 * g + 2) * TILE])
            for u in range(2):
                h = 2 * g + u
                c = slice(h * TILE, (h + 1) * TILE)
                probs = p[i, :, c].astype(F32)
                dp = both[:, u * TILE : (u + 1) * TILE]
                inner = jnp.sum(dp * probs, axis=0, keepdims=True)
                ds = (probs * (dp - inner)).astype(BF16)
                ds_all[:, c] = ds
                parts.append(nn(keys_t[h * size : (h + 1) * size, :], ds))
        ql[rows, :] = (jnp.concatenate(parts, axis=0).T * scale).astype(BF16)
        dk[win, :] += nn(ds_all[...], qm[...])
        dv[win, :] += nn(p[i], am[...])
        return carry

    lax.fori_loop(0, tok // TILE, tile, 0, unroll=2)
    kl[...] = (dk[...] * scale).astype(BF16)
    vl[...] = dv[...].astype(BF16)


def attention_back(g_one, q, k, v, p, w_out):
    tok, width = g_one.shape
    return call(
        attention_back_kernel,
        [shape((tok, width), BF16)] * 3,
        [g_one, q, k, v, p, w_out],
        [
            VMEM((tok, width), BF16),
            VMEM((width, tok), BF16),
            VMEM((WINDOW, HEADS * TILE), BF16),
            VMEM((width, HEADS * TILE), BF16),
            VMEM((HEADS * TILE, width), BF16),
            VMEM((HEADS * TILE, width), BF16),
            VMEM((tok, width), F32),
            VMEM((tok, width), F32),
        ],
        "attention_backward",
        16_000_000_000,
        vmem=20,
    )


def project_back_kernel(flat, piece, place, feat, emb, src, g_one, ql, kl, vl, dwo, vg, wa, *rest):
    low_out = rest[0]
    outs, (grads,) = rest[1:-1], rest[-1:]
    tok, width = g_one.shape
    at = feat.shape[1]
    total = jnp.zeros((1, width), F32)
    for i in range(tok // ROWS):
        r = pl.ds(i * ROWS, ROWS)
        e = (
            g_one[r, :]
            + nt(ql[r, :], wa[at : at + width, :])
            + nt(kl[r, :], wa[at + width : at + 2 * width, :])
            + nt(vl[r, :], wa[at + 2 * width : at + 3 * width, :])
        )
        low = e.astype(BF16)
        low_out[r, :] = low
        total += column_sum(low)
    src_t = src[...].T
    grads[at : at + width, :] = nn(src_t, ql[...]).astype(BF16)
    grads[at + width : at + 2 * width, :] = nn(src_t, kl[...]).astype(BF16)
    grads[at + 2 * width : at + 3 * width, :] = nn(emb[...].astype(BF16).T, vl[...]).astype(BF16)
    grads[0:at, :] = nn(feat[...].T, low_out[...]).astype(BF16)
    grads[at + 3 * width :, :] = dwo[...]
    front = jnp.concatenate([total, column_sum(ql[...]), column_sum(vl[...])], axis=0)
    if flat:
        outs[0][...] = grads[...]
        outs[1][...] = vg[...]
        outs[1][0:3, :] = front
        return
    keep, send = outs
    core = place[3]
    for m in range(4):
        to = pl.ds(m * piece, piece)
        keep[to, :] = grads[pl.ds(pl.multiple_of((2 * m + core) * piece, 16), piece), :]
        send[to, :] = grads[pl.ds(pl.multiple_of((2 * m + 1 - core) * piece, 16), piece), :]
    rows = vg.shape[0]
    pad = jnp.zeros((VEC_PAD - rows, width), F32)
    tail = jnp.concatenate([front, vg[3:rows, :], pad], axis=0).astype(BF16)
    for ref in (keep, send):
        ref[4 * piece :, :] = tail


def project_back(flat, place, feat, emb, src, g_one, ql, kl, vl, dwo, vg, wa, piece):
    tok, width = g_one.shape
    outs = [shape((tok, width), BF16)]
    if flat:
        outs += [shape(wa.shape, BF16), shape(vg.shape, F32)]
    else:
        outs += [shape((4 * piece + VEC_PAD, width), BF16)] * 2
    return call(
        functools.partial(project_back_kernel, flat, piece),
        outs,
        [place, feat, emb, src, g_one, ql, kl, vl, dwo, vg, wa],
        [VMEM(wa.shape, BF16)],
        "project_backward",
        2_000_000_000,
        [pltpu.SMEM] + [VMEM] * 10,
        vmem=16,
    )


def feature_kernel(low, wa, out):
    for i in range(low.shape[0] // ROWS):
        r = pl.ds(i * ROWS, ROWS)
        out[r, :] = nt(low[r, :], wa[0 : out.shape[1], :])


def feature_back(low, wa, feat_dim):
    return call(
        feature_kernel,
        [shape((low.shape[0], feat_dim), F32)],
        [low, wa],
        [],
        "feature_gradient",
        300_000_000,
    )[0]


def plane_kernel(place, own, one, two, three, attn, rest):
    got = (own, one, two, three)
    z = place[0]
    for slot in range(4):

        @pl.when(z == slot)
        def _(slot=slot):
            attn[...] = got[slot][...]
            for plane in range(1, 4):
                rest[plane - 1] = got[slot ^ plane][...]


def pick_planes(place, own, one, two, three):
    return call(
        plane_kernel,
        [shape(own.shape, BF16), shape((3, *own.shape), BF16)],
        [place, own, one, two, three],
        [],
        "pick_planes",
        1_000_000,
        [pltpu.SMEM] + [VMEM] * 4,
    )


def ff_sum_kernel(place, keep, recv, *outs):
    yx = place[1]
    for slot in range(4):
        for plane in range(3):
            at = 4 * plane + (yx ^ slot)
            outs[slot][plane] = (keep[at].astype(F32) + recv[at].astype(F32)).astype(BF16)


def ff_sum(place, keep, recv):
    one = shape((3, *keep.shape[1:]), BF16)
    return call(
        ff_sum_kernel,
        [one] * 4,
        [place, keep, recv],
        [],
        "sum_cores_ff",
        1_000_000,
        [pltpu.SMEM] + [VMEM] * 2,
    )


def four_kernel(a, b, c, d, out):
    out[...] = (
        (a[...].astype(F32) + b[...].astype(F32)) + (c[...].astype(F32) + d[...].astype(F32))
    ).astype(BF16)


def four_sum(a, b, c, d):
    return call(four_kernel, [shape(a.shape, BF16)], [a, b, c, d], [], "sum_plane_ff", 1_000_000)[0]


def tail_sum_kernel(piece, place, keep, recv, *outs):
    yx = place[1]
    vec = keep[4 * piece :, :].astype(F32) + recv[4 * piece :, :].astype(F32)
    for slot in range(4):
        r = pl.ds(pl.multiple_of((yx ^ slot) * piece, 16), piece)
        outs[slot][0:piece, :] = (keep[r, :].astype(F32) + recv[r, :].astype(F32)).astype(BF16)
        outs[slot][piece:, :] = vec.astype(BF16)


def tail_sum(place, keep, recv, piece):
    return call(
        functools.partial(tail_sum_kernel, piece),
        [shape((piece + VEC_PAD, keep.shape[1]), BF16)] * 4,
        [place, keep, recv],
        [],
        "sum_cores_tail",
        1_000_000,
        [pltpu.SMEM] + [VMEM] * 2,
    )


def plane_sum_kernel(place, a, b, c, d, ff, *outs):
    z = place[0]
    total = (
        (a[...].astype(F32) + b[...].astype(F32)) + (c[...].astype(F32) + d[...].astype(F32))
    ).astype(BF16)
    piece = ff.shape[1]
    for slot in range(4):
        goal = z ^ slot
        outs[slot][piece:, :] = total[piece:, :]

        @pl.when(goal == 0)
        def _(slot=slot):
            outs[slot][0:piece, :] = total[0:piece, :]

        @pl.when(goal != 0)
        def _(slot=slot, goal=goal):
            outs[slot][0:piece, :] = ff[jnp.maximum(goal - 1, 0)]


def plane_sum(place, a, b, c, d, ff):
    return call(
        plane_sum_kernel,
        [shape(a.shape, BF16)] * 4,
        [place, a, b, c, d, ff],
        [],
        "sum_plane_tail",
        1_000_000,
        [pltpu.SMEM] + [VMEM] * 5,
    )


def adam_step(weight, moment_one, moment_two, gradient, step_rate, decay_rate):
    moment_one = BETA_ONE * moment_one + (1.0 - BETA_ONE) * gradient
    moment_two = BETA_TWO * moment_two + (1.0 - BETA_TWO) * gradient * gradient
    mean_hat = moment_one / (1.0 - BETA_ONE**STEP)
    square_hat = moment_two / (1.0 - BETA_TWO**STEP)
    weight = weight - step_rate * (
        mean_hat / (jnp.sqrt(square_hat) + ADAM_EPS) + decay_rate * weight
    )
    return (weight, moment_one, moment_two)


def adam_kernel(feat_dim, place, a, b, c, d, w, m, v, vw, vm, vv, *outs):
    total = (a[...].astype(F32) + b[...].astype(F32)) + (c[...].astype(F32) + d[...].astype(F32))
    piece = w.shape[0]
    rows = place[2] * piece + lax.broadcasted_iota(jnp.int32, w.shape, 0)
    rate = jnp.where(rows < feat_dim, 0.1 * RATE, RATE)
    new = adam_step(w[...], m[...], v[...], total[0:piece, :], rate, DECAY)
    for ref, value in zip(outs[:3], new):
        ref[...] = value
    outs[3][...] = new[0].astype(BF16)
    new = adam_step(vw[...], vm[...], vv[...], total[piece : piece + vw.shape[0], :], RATE, 0.0)
    for ref, value in zip(outs[4:], new):
        ref[...] = value


def adam(place, parts, mats, mats_m, mats_v, vecs, vecs_m, vecs_v, feat_dim):
    mat, vec = shape(mats.shape, F32), shape(vecs.shape, F32)
    return call(
        functools.partial(adam_kernel, feat_dim),
        [mat, mat, mat, shape(mats.shape, BF16), vec, vec, vec],
        [place, *parts, mats, mats_m, mats_v, vecs, vecs_m, vecs_v],
        [],
        "adam",
        10_000_000,
        [pltpu.SMEM] + [VMEM] * 10,
    )


def sine_table(within, model_width):
    half_width = model_width // 2
    frequency = jnp.exp(-jnp.log(10000.0) * jnp.arange(half_width, dtype=F32) / half_width)
    angles = within.astype(F32)[:, None] * frequency[None, :]
    return jnp.concatenate([jnp.sin(angles), jnp.cos(angles)], axis=1)


def grid_swap(dz, dyx):
    return [(4 * z + yx, 4 * (z ^ dz) + (yx ^ dyx)) for z in range(4) for yx in range(4)]


PAIR_SWAP = [(0, 1), (1, 0)]


def per_device(
    flat,
    features,
    cotangent,
    canvas_lengths,
    crop_ids,
    mats,
    mats_m,
    mats_v,
    vecs,
    vecs_m,
    vecs_v,
):
    tok = features.shape[0]
    feat_dim = features.shape[1]
    width = vecs.shape[1]
    attn_rows = feat_dim + 3 * width + width // 2
    ff_rows = width // 2 + 2 * FF
    piece = mats.shape[0]
    dp, core = lax.axis_index("dp"), lax.axis_index("pair")
    device = lax.axis_index(("dp", "pair"))
    place = jnp.stack([dp // 4, dp % 4, device, core]).astype(jnp.int32)

    position = jnp.arange(tok, dtype=jnp.int32)
    first_len = canvas_lengths[0, 0]
    canvas_id = (position >= first_len).astype(jnp.int32)
    within = position - first_len * canvas_id
    pos_table = sine_table(within, width)
    segment = crop_ids * 2 + canvas_id
    segment = (jnp.broadcast_to(segment[:, None], (tok, TILE)), segment.reshape(-1, TILE))

    mats_low = mats.astype(BF16)
    if flat:
        gathered = lax.all_gather(mats_low, ("dp", "pair"), axis=0, tiled=True)
        attn_pieces = [gathered[:attn_rows]]
        ff_pieces = [gathered[attn_rows:]]
    else:
        planes = [lax.ppermute(mats_low, "dp", grid_swap(dz, 0)) for dz in (1, 2, 3)]
        pos_table, segment, planes = lax.optimization_barrier((pos_table, segment, planes))
        one, three = pick_planes(place, mats_low, *planes)
        attn_pieces = [one] + [lax.ppermute(one, "dp", grid_swap(0, s)) for s in (1, 2, 3)]
        attn_pieces += [lax.ppermute(a, "pair", PAIR_SWAP) for a in attn_pieces]
        ff_pieces = [three] + [lax.ppermute(three, "dp", grid_swap(0, s)) for s in (1, 2, 3)]

    wa, emb, src, q, k, v, attn, probs = attention(
        flat, place, features, pos_table, segment, vecs, attn_pieces, attn_rows
    )
    if not flat:
        attn, *ff_pieces = lax.optimization_barrier((attn, *ff_pieces))
        ff_pieces += [lax.ppermute(a, "pair", PAIR_SWAP) for a in ff_pieces]
    output, g_one, w_out, vg, dwo, *ff_grads = feed(
        flat, place, emb, attn, cotangent, vecs, wa, ff_pieces, ff_rows
    )
    if not flat:
        keep, send = ff_grads
        sums = ff_sum(place, keep, lax.ppermute(send, "pair", PAIR_SWAP))
        g_one, *sums = lax.optimization_barrier((g_one, *sums))
        ff_parts = [sums[0]] + [lax.ppermute(sums[s], "dp", grid_swap(0, s)) for s in (1, 2, 3)]
    ql, kl, vl = attention_back(g_one, q, k, v, probs, w_out)
    if not flat:
        ql, kl, vl, *ff_parts = lax.optimization_barrier((ql, kl, vl, *ff_parts))
        ff = four_sum(*ff_parts)
    low, *tail = project_back(
        flat, place, features, emb, src, g_one, ql, kl, vl, dwo, vg, wa, piece
    )
    feature_grad = feature_back(low, wa, feat_dim)
    if flat:
        grads = jnp.concatenate([tail[0], ff_grads[0]], axis=0).astype(F32)
        total = lax.psum_scatter(grads, ("dp", "pair"), scatter_dimension=0, tiled=True)
        vec_total = lax.psum(tail[1], ("dp", "pair"))
        row_ids = device * piece + jnp.arange(piece, dtype=jnp.int32)
        rate = jnp.where(row_ids < feat_dim, 0.1 * RATE, RATE)[:, None]
        new = adam_step(mats, mats_m, mats_v, total, rate, DECAY)
        new_vec = adam_step(vecs, vecs_m, vecs_v, vec_total, RATE, 0.0)
        return (output, feature_grad, *new, new[0].astype(BF16), *new_vec)
    keep, send = tail
    sums = tail_sum(place, keep, lax.ppermute(send, "pair", PAIR_SWAP), piece)
    parts = [sums[0]] + [lax.ppermute(sums[s], "dp", grid_swap(0, s)) for s in (1, 2, 3)]
    sums = plane_sum(place, *parts, ff)
    parts = [sums[0]] + [lax.ppermute(sums[s], "dp", grid_swap(s, 0)) for s in (1, 2, 3)]
    new = adam(place, parts, mats, mats_m, mats_v, vecs, vecs_m, vecs_v, feat_dim)
    return (output, feature_grad, *new)


def solution(mesh):
    rows = P(("dp", "pair"), None)
    in_specs = (rows, rows, rows, P(("dp", "pair")), rows, rows, rows, P(), P(), P())
    out_specs = (rows, rows, rows, rows, rows, rows, P(), P(), P())
    flat = mesh.shape["dp"] != 16 or mesh.shape["pair"] != 2
    return jax.shard_map(
        functools.partial(per_device, flat),
        mesh=mesh,
        in_specs=in_specs,
        out_specs=out_specs,
        check_vma=False,
    )
```

```python
import functools

import jax
import jax.numpy as jnp
from jax import lax
from jax.experimental import pallas as pl
from jax.experimental.pallas import tpu as pltpu
from jax.sharding import PartitionSpec as P

HEADS = 8
FF = 2048
STEP = 10

EPS_NORM = 1e-05
RATE = 0.2
BETA_ONE = 0.9
BETA_TWO = 0.999
ADAM_EPS = 1e-08
DECAY = 0.0001
MASKED = -1000000000.0

TILE = 128
WINDOW = 384
ROWS = 512
BLOCK = 256
BLOCKS = FF // BLOCK
GELU_A = 0.7978845608028654
GELU_B = 0.044715
LOG2_E = 1.4426950408889634
VEC_PAD = 32

F32 = jnp.float32
BF16 = jnp.bfloat16
VMEM = pltpu.VMEM


def nn(a, b):
    return lax.dot_general(a, b, (((1,), (0,)), ((), ())), preferred_element_type=F32)


def nt(a, b):
    return lax.dot_general(a, b, (((1,), (1,)), ((), ())), preferred_element_type=F32)


def tn(a, b):
    return lax.dot_general(a, b, (((0,), (0,)), ((), ())), preferred_element_type=F32)


def row_mean(x):
    return jnp.sum(x, axis=1, keepdims=True) * (1.0 / x.shape[1])


def fold_rows(x):
    return jnp.sum(x.reshape(x.shape[0] // 8, 8, x.shape[1]), axis=0)


def column_sum(x):
    return jnp.sum(x.astype(F32), axis=0, keepdims=True)


def head_lanes(h, rows, width):
    lane = lax.broadcasted_iota(jnp.int32, (rows, width), 1)
    size = width // HEADS
    return (lane >= h * size) & (lane < (h + 1) * size)


def window_start(i, tok):
    return jnp.clip((i - 1) * TILE, 0, tok - WINDOW)


def call(kernel, outs, ins, scratch, name, flops, spaces=None, vmem=12):
    spaces = spaces or [VMEM] * len(ins)
    nbytes = sum(a.size * a.dtype.itemsize for a in ins) + sum(
        a.size * a.dtype.itemsize for a in outs
    )
    return pl.pallas_call(
        kernel,
        out_shape=tuple(outs),
        in_specs=[pl.BlockSpec(memory_space=s) for s in spaces],
        out_specs=tuple(pl.BlockSpec(memory_space=VMEM) for _ in outs),
        scratch_shapes=scratch,
        compiler_params=pltpu.CompilerParams(vmem_limit_bytes=vmem << 20),
        cost_estimate=pl.CostEstimate(flops=flops, bytes_accessed=nbytes, transcendentals=0),
        name=name,
    )(*ins)


def shape(dims, kind):
    return jax.ShapeDtypeStruct(dims, kind)


def load_pieces(refs, offsets, dst):
    for ref, offs in zip(refs, offsets):
        if len(ref.shape) == 2:
            dst[pl.ds(offs[0], ref.shape[0]), :] = ref[...]
        else:
            for i, off in enumerate(offs):
                dst[pl.ds(off, ref.shape[1]), :] = ref[i]


def place_offsets(place, piece, planes):
    offsets = []
    for other in (0, 1):
        for slot in range(4):
            core = place[3] ^ other if other else place[3]
            inner = 2 * (place[1] ^ slot) + core
            offsets.append(
                [pl.multiple_of((8 * plane + inner) * piece, 16) for plane in range(planes)]
            )
    return offsets


def attention_kernel(flat, piece, place, feat, pos, seg_col, seg_row, vec, *rest):
    count = 1 if flat else 8
    pieces, rest = rest[:count], rest[count:]
    w, emb, src, q, k, v, attn_t, p, scale_inv, v_t, q_t = rest
    tok, width = emb.shape
    feat_dim = feat.shape[1]
    size = width // HEADS
    scale = size ** (-0.5)
    offsets = [[0]] if flat else place_offsets(place, piece, 1)
    load_pieces(pieces, offsets, w)
    for i in range(tok // ROWS):
        r = pl.ds(i * ROWS, ROWS)
        e = nn(feat[r, :], w[0:feat_dim, :]) + vec[0:1, :]
        emb[r, :] = e
        s = (e + pos[r, :]).astype(BF16)
        src[r, :] = s
        low = e.astype(BF16)
        at = feat_dim
        q[r, :] = (nn(s, w[at : at + width, :]) + vec[1:2, :]).astype(BF16)
        k[r, :] = nn(s, w[at + width : at + 2 * width, :]).astype(BF16)
        v[r, :] = (nn(low, w[at + 2 * width : at + 3 * width, :]) + vec[2:3, :]).astype(BF16)
    pad = v_t.shape[0] // HEADS
    vals = v[...].T
    for h in range(HEADS):
        v_t[h * pad : h * pad + size, :] = vals[h * size : (h + 1) * size, :]
        v_t[h * pad + size : (h + 1) * pad, :] = jnp.ones((pad - size, tok), BF16)
    q_t[...] = jnp.zeros_like(q_t)
    masked = MASKED / scale
    factor = scale * LOG2_E

    def tile(i, carry):
        rows = pl.ds(pl.multiple_of(i * TILE, TILE), TILE)
        win = pl.ds(pl.multiple_of(window_start(i, tok), TILE), WINDOW)
        own_t = q[rows, :].T
        keys = k[win, :]
        vals_t = v_t[:, win]
        allowed = seg_col[win, :] == seg_row[pl.ds(i, 1), :]
        for h in range(HEADS):
            d = slice(h * size, (h + 1) * size)
            q_t[d, h * TILE : (h + 1) * TILE] = own_t[d, :]
        for g in range(HEADS // 2):
            both = nn(keys, q_t[:, 2 * g * TILE : (2 * g + 2) * TILE])
            for u in range(2):
                h = 2 * g + u
                s = jnp.where(allowed, both[:, u * TILE : (u + 1) * TILE], masked)
                top = jnp.max(s, axis=0, keepdims=True)
                e = jnp.exp2((s - top) * factor).astype(BF16)
                p[i, :, h * TILE : (h + 1) * TILE] = e
                o = nn(vals_t[h * pad : (h + 1) * pad, :], e)
                inv = 1.0 / o[size : size + 1, :]
                scale_inv[i, h : h + 1, :] = inv
                attn_t[h * size : (h + 1) * size, rows] = (o[0:size, :] * inv).astype(BF16)
        return carry

    lax.fori_loop(0, tok // TILE, tile, 0, unroll=4)


def attention(flat, place, feat, pos, segment, vec, pieces, attn_rows):
    tok, width = feat.shape[0], vec.shape[1]
    piece = pieces[0].shape[0]
    low = shape((tok, width), BF16)
    outs = [
        shape((attn_rows, width), BF16),
        shape((tok, width), F32),
        low,
        low,
        low,
        low,
        shape((width, tok), BF16),
        shape((tok // TILE, WINDOW, HEADS * TILE), BF16),
        shape((tok // TILE, HEADS, TILE), F32),
    ]
    ins = [place, feat, pos, *segment, vec, *pieces]
    return call(
        functools.partial(attention_kernel, flat, piece),
        outs,
        ins,
        [
            VMEM((width + 16 * HEADS, tok), BF16),
            VMEM((width, HEADS * TILE), BF16),
        ],
        "attention_forward",
        12_000_000_000,
        [pltpu.SMEM] + [VMEM] * (5 + len(pieces)),
        vmem=20,
    )


def feed_kernel(flat, piece, place, emb, attn_t, cot, vec, wa, *rest):
    count = 1 if flat else 8
    pieces, rest = rest[:count], rest[count:]
    outs = 5 if flat else 6
    res, rest = rest[: outs + 1], rest[outs + 1 :]
    out, g_one, w_out, vec_grad, dwo = res[:5]
    (wf, wh, wh_t, wb_t, half_a, half_b, act, pre, slope, n_t, b_t, out_all, acc, gff) = rest
    halves = (half_a, half_b)
    tok, width = emb.shape
    first = width // 2
    offsets = [[0]] if flat else place_offsets(place, piece, 3)
    load_pieces(pieces, offsets, wf)
    for u in range(2):
        halves[u][...] = wf[first : first + FF, u * 128 : (u + 1) * 128].astype(F32)
    w_out[0:first, :] = wa[wa.shape[0] - first :, :]
    w_out[first:, :] = wf[0:first, :]
    for j in range(BLOCKS):
        c = slice(j * BLOCK, (j + 1) * BLOCK)
        w = jnp.concatenate(
            [halves[u][pl.ds(j, width, stride=BLOCKS), :] for u in range(2)], axis=1
        ).astype(BF16)
        wh[:, c] = w
        wh_t[c, :] = w.T
        wb_t[:, c] = wf[first + FF + j * BLOCK : first + FF + (j + 1) * BLOCK, :].T
    acc[...] = jnp.zeros_like(acc)
    n_t[width : width + 8, :] = jnp.ones((8, tok), BF16)

    def tile(i, carry):
        r = pl.ds(pl.multiple_of(i * ROWS, ROWS), ROWS)
        res_one = emb[r, :] + tn(attn_t[:, r], w_out[...]) + vec[3:4, :]
        cen = res_one - row_mean(res_one)
        inv_one = lax.rsqrt(row_mean(cen * cen) + EPS_NORM)
        hat_one = cen * inv_one
        normed = hat_one * vec[4:5, :] + vec[5:6, :]
        low = normed.astype(BF16)
        for j in range(BLOCKS):
            c = slice(j * BLOCK, (j + 1) * BLOCK)
            x = nn(low, wh[:, c]) + vec[9 + j : 10 + j, :]
            sq = x * x
            t = jnp.tanh(x * (GELU_A + (GELU_A * GELU_B) * sq))
            half = 0.5 + 0.5 * t
            act[r, c] = (x * half).astype(BF16)
            bend = x * ((2 * GELU_A) + (6 * GELU_A * GELU_B) * sq)
            slope[r, c] = (half + (half - half * half) * bend).astype(BF16)
        res_two = normed + nn(act[r, :], wf[first + FF : first + 2 * FF, :]) + vec[6:7, :]
        cen = res_two - row_mean(res_two)
        inv_two = lax.rsqrt(row_mean(cen * cen) + EPS_NORM)
        hat_two = cen * inv_two
        out[r, :] = hat_two * vec[7:8, :] + vec[8:9, :]
        ct = cot[r, :].astype(F32)
        gs = ct * vec[7:8, :]
        g_two = inv_two * (gs - row_mean(gs) - hat_two * row_mean(gs * hat_two))
        back = g_two.astype(BF16)
        b_t[:, r] = back.T
        acc[0] += fold_rows(back.astype(F32))
        acc[1] += fold_rows(ct * hat_two)
        acc[2] += fold_rows(ct)
        for j in range(BLOCKS):
            c = slice(j * BLOCK, (j + 1) * BLOCK)
            pre[r, c] = (nn(back, wb_t[:, c]) * slope[r, c].astype(F32)).astype(BF16)
        g_norm = g_two + nn(pre[r, :], wh_t[...])
        n_t[0:width, r] = low.T
        gs = g_norm * vec[4:5, :]
        g_res = inv_one * (gs - row_mean(gs) - hat_one * row_mean(gs * hat_one))
        g_one[r, :] = g_res
        out_low = g_res.astype(BF16)
        out_all[r, :] = out_low
        acc[3] += fold_rows(out_low.astype(F32))
        acc[4] += fold_rows(g_norm * hat_one)
        acc[5] += fold_rows(g_norm)
        return carry

    lax.fori_loop(0, tok // ROWS, tile, 0, unroll=2)
    for j in range(BLOCKS):
        c = slice(j * BLOCK, (j + 1) * BLOCK)
        g = nn(n_t[...], pre[:, c])
        for u in range(2):
            halves[u][pl.ds(j, width, stride=BLOCKS), :] = g[0:width, u * 128 : (u + 1) * 128]
        vec_grad[9 + j : 10 + j, :] = g[width : width + 1, :]
        at = first + FF + j * BLOCK
        gff[at : at + BLOCK, :] = nn(b_t[...], act[:, c]).T.astype(BF16)
    for u in range(2):
        gff[first : first + FF, u * 128 : (u + 1) * 128] = halves[u][...].astype(BF16)
    g = nn(attn_t[...], out_all[...]).astype(BF16)
    dwo[...] = g[0:first, :]
    gff[0:first, :] = g[first:, :]
    sums = jnp.sum(acc[...], axis=1)
    vec_grad[0:3, :] = jnp.zeros((3, width), F32)
    for row, at in ((3, 3), (4, 4), (5, 5), (6, 0), (7, 1), (8, 2)):
        vec_grad[row : row + 1, :] = sums[at : at + 1, :]
    if flat:
        res[5][...] = gff[...]
    else:
        split_cores(place, gff, res[5], res[6])


def split_cores(place, grads, keep, send):
    core = place[3]
    piece = keep.shape[1]
    for m in range(keep.shape[0]):
        keep[m] = grads[pl.ds(pl.multiple_of((2 * m + core) * piece, 16), piece), :]
        send[m] = grads[pl.ds(pl.multiple_of((2 * m + 1 - core) * piece, 16), piece), :]


def feed(flat, place, emb, attn_t, cot, vec, wa, pieces, ff_rows):
    tok, width = emb.shape
    piece = pieces[0].shape[-2]
    outs = [
        shape((tok, width), F32),
        shape((tok, width), F32),
        shape((width, width), BF16),
        shape(vec.shape, F32),
        shape((width // 2, width), BF16),
    ]
    if flat:
        outs += [shape((ff_rows, width), BF16)]
    else:
        outs += [shape((ff_rows // piece // 2, piece, width), BF16)] * 2
    return call(
        functools.partial(feed_kernel, flat, piece),
        outs,
        [place, emb, attn_t, cot, vec, wa, *pieces],
        [
            VMEM((ff_rows, width), BF16),
            VMEM((width, FF), BF16),
            VMEM((FF, width), BF16),
            VMEM((width, FF), BF16),
            VMEM((FF, 128), F32),
            VMEM((FF, 128), F32),
            VMEM((tok, FF), BF16),
            VMEM((tok, FF), BF16),
            VMEM((tok, FF), BF16),
            VMEM((width + 8, tok), BF16),
            VMEM((width, tok), BF16),
            VMEM((tok, width), BF16),
            VMEM((6, 8, width), F32),
            VMEM((ff_rows, width), BF16),
        ],
        "feed_forward_both",
        14_000_000_000,
        [pltpu.SMEM] + [VMEM] * (5 + len(pieces)),
        vmem=34,
    )


def attention_back_kernel(g_one, q, k, v, p, scale_inv, attn_t, w_out, *rest):
    ql, kl, vl, ag, k_t, ds_all, a_t, scaled, qm, am, dk, dv = rest
    tok, width = g_one.shape
    size = width // HEADS
    scale = size ** (-0.5)
    for i in range(tok // ROWS):
        r = pl.ds(i * ROWS, ROWS)
        ag[r, :] = nt(g_one[r, :].astype(BF16), w_out[...]).astype(BF16)
    k_t[...] = k[...].T
    dk[...] = jnp.zeros_like(dk)
    dv[...] = jnp.zeros_like(dv)
    a_t[...] = jnp.zeros_like(a_t)

    def tile(i, carry):
        rows = pl.ds(pl.multiple_of(i * TILE, TILE), TILE)
        win = pl.ds(pl.multiple_of(window_start(i, tok), TILE), WINDOW)
        own_q = q[rows, :]
        own_t = ag[rows, :].T
        vals = v[win, :]
        keys_t = k_t[:, win]
        inner = []
        for h in range(HEADS):
            d = slice(h * size, (h + 1) * size)
            grad = own_t[d, :].astype(F32) * scale_inv[i, h : h + 1, :]
            inner.append(jnp.sum(grad * attn_t[d, rows].astype(F32), axis=0, keepdims=True))
            a_t[d, h * TILE : (h + 1) * TILE] = grad.astype(BF16)
            scaled[d, :] = grad.astype(BF16)
        own_a = scaled[...].T
        for h in range(HEADS):
            lanes = head_lanes(h, TILE, width)
            c = slice(h * TILE, (h + 1) * TILE)
            qm[c, :] = jnp.where(lanes, own_q, jnp.zeros_like(own_q))
            am[c, :] = jnp.where(lanes, own_a, jnp.zeros_like(own_a))
        parts = []
        for g in range(HEADS // 2):
            both = nn(vals, a_t[:, 2 * g * TILE : (2 * g + 2) * TILE])
            for u in range(2):
                h = 2 * g + u
                c = slice(h * TILE, (h + 1) * TILE)
                dp = both[:, u * TILE : (u + 1) * TILE]
                ds = (p[i, :, c].astype(F32) * (dp - inner[h])).astype(BF16)
                ds_all[:, c] = ds
                parts.append(nn(keys_t[h * size : (h + 1) * size, :], ds))
        ql[rows, :] = (jnp.concatenate(parts, axis=0).T * scale).astype(BF16)
        dk[win, :] += nn(ds_all[...], qm[...])
        dv[win, :] += nn(p[i], am[...])
        return carry

    lax.fori_loop(0, tok // TILE, tile, 0, unroll=2)
    kl[...] = (dk[...] * scale).astype(BF16)
    vl[...] = dv[...].astype(BF16)


def attention_back(g_one, q, k, v, p, scale_inv, attn_t, w_out):
    tok, width = g_one.shape
    return call(
        attention_back_kernel,
        [shape((tok, width), BF16)] * 3,
        [g_one, q, k, v, p, scale_inv, attn_t, w_out],
        [
            VMEM((tok, width), BF16),
            VMEM((width, tok), BF16),
            VMEM((WINDOW, HEADS * TILE), BF16),
            VMEM((width, HEADS * TILE), BF16),
            VMEM((width, TILE), BF16),
            VMEM((HEADS * TILE, width), BF16),
            VMEM((HEADS * TILE, width), BF16),
            VMEM((tok, width), F32),
            VMEM((tok, width), F32),
        ],
        "attention_backward",
        16_000_000_000,
        vmem=20,
    )


def project_back_kernel(flat, piece, place, feat, emb, src, g_one, ql, kl, vl, dwo, vg, wa, *rest):
    low_out = rest[0]
    outs, (grads,) = rest[1:-1], rest[-1:]
    tok, width = g_one.shape
    at = feat.shape[1]
    total = jnp.zeros((1, width), F32)
    for i in range(tok // ROWS):
        r = pl.ds(i * ROWS, ROWS)
        e = (
            g_one[r, :]
            + nt(ql[r, :], wa[at : at + width, :])
            + nt(kl[r, :], wa[at + width : at + 2 * width, :])
            + nt(vl[r, :], wa[at + 2 * width : at + 3 * width, :])
        )
        low = e.astype(BF16)
        low_out[r, :] = low
        total += column_sum(low)
    src_t = src[...].T
    grads[at : at + width, :] = nn(src_t, ql[...]).astype(BF16)
    grads[at + width : at + 2 * width, :] = nn(src_t, kl[...]).astype(BF16)
    grads[at + 2 * width : at + 3 * width, :] = nn(emb[...].astype(BF16).T, vl[...]).astype(BF16)
    grads[0:at, :] = nn(feat[...].T, low_out[...]).astype(BF16)
    grads[at + 3 * width :, :] = dwo[...]
    front = jnp.concatenate([total, column_sum(ql[...]), column_sum(vl[...])], axis=0)
    if flat:
        outs[0][...] = grads[...]
        outs[1][...] = vg[...]
        outs[1][0:3, :] = front
        return
    keep, send = outs
    core = place[3]
    for m in range(4):
        to = pl.ds(m * piece, piece)
        keep[to, :] = grads[pl.ds(pl.multiple_of((2 * m + core) * piece, 16), piece), :]
        send[to, :] = grads[pl.ds(pl.multiple_of((2 * m + 1 - core) * piece, 16), piece), :]
    rows = vg.shape[0]
    pad = jnp.zeros((VEC_PAD - rows, width), F32)
    tail = jnp.concatenate([front, vg[3:rows, :], pad], axis=0).astype(BF16)
    for ref in (keep, send):
        ref[4 * piece :, :] = tail


def project_back(flat, place, feat, emb, src, g_one, ql, kl, vl, dwo, vg, wa, piece):
    tok, width = g_one.shape
    outs = [shape((tok, width), BF16)]
    if flat:
        outs += [shape(wa.shape, BF16), shape(vg.shape, F32)]
    else:
        outs += [shape((4 * piece + VEC_PAD, width), BF16)] * 2
    return call(
        functools.partial(project_back_kernel, flat, piece),
        outs,
        [place, feat, emb, src, g_one, ql, kl, vl, dwo, vg, wa],
        [VMEM(wa.shape, BF16)],
        "project_backward",
        2_000_000_000,
        [pltpu.SMEM] + [VMEM] * 10,
        vmem=16,
    )


def feature_kernel(low, wa, out):
    for i in range(low.shape[0] // ROWS):
        r = pl.ds(i * ROWS, ROWS)
        out[r, :] = nt(low[r, :], wa[0 : out.shape[1], :])


def feature_back(low, wa, feat_dim):
    return call(
        feature_kernel,
        [shape((low.shape[0], feat_dim), F32)],
        [low, wa],
        [],
        "feature_gradient",
        300_000_000,
    )[0]


def plane_kernel(place, own, one, two, three, attn, rest):
    got = (own, one, two, three)
    z = place[0]
    for slot in range(4):

        @pl.when(z == slot)
        def _(slot=slot):
            attn[...] = got[slot][...]
            for plane in range(1, 4):
                rest[plane - 1] = got[slot ^ plane][...]


def pick_planes(place, own, one, two, three):
    return call(
        plane_kernel,
        [shape(own.shape, BF16), shape((3, *own.shape), BF16)],
        [place, own, one, two, three],
        [],
        "pick_planes",
        1_000_000,
        [pltpu.SMEM] + [VMEM] * 4,
    )


def ff_sum_kernel(place, keep, recv, *outs):
    yx = place[1]
    for slot in range(4):
        for plane in range(3):
            at = 4 * plane + (yx ^ slot)
            outs[slot][plane] = (keep[at].astype(F32) + recv[at].astype(F32)).astype(BF16)


def ff_sum(place, keep, recv):
    one = shape((3, *keep.shape[1:]), BF16)
    return call(
        ff_sum_kernel,
        [one] * 4,
        [place, keep, recv],
        [],
        "sum_cores_ff",
        1_000_000,
        [pltpu.SMEM] + [VMEM] * 2,
    )


def four_kernel(a, b, c, d, out):
    out[...] = (
        (a[...].astype(F32) + b[...].astype(F32)) + (c[...].astype(F32) + d[...].astype(F32))
    ).astype(BF16)


def four_sum(a, b, c, d):
    return call(four_kernel, [shape(a.shape, BF16)], [a, b, c, d], [], "sum_plane_ff", 1_000_000)[0]


def tail_sum_kernel(piece, place, keep, recv, *outs):
    yx = place[1]
    vec = keep[4 * piece :, :].astype(F32) + recv[4 * piece :, :].astype(F32)
    for slot in range(4):
        r = pl.ds(pl.multiple_of((yx ^ slot) * piece, 16), piece)
        outs[slot][0:piece, :] = (keep[r, :].astype(F32) + recv[r, :].astype(F32)).astype(BF16)
        outs[slot][piece:, :] = vec.astype(BF16)


def tail_sum(place, keep, recv, piece):
    return call(
        functools.partial(tail_sum_kernel, piece),
        [shape((piece + VEC_PAD, keep.shape[1]), BF16)] * 4,
        [place, keep, recv],
        [],
        "sum_cores_tail",
        1_000_000,
        [pltpu.SMEM] + [VMEM] * 2,
    )


def plane_sum_kernel(place, a, b, c, d, ff, *outs):
    z = place[0]
    total = (
        (a[...].astype(F32) + b[...].astype(F32)) + (c[...].astype(F32) + d[...].astype(F32))
    ).astype(BF16)
    piece = ff.shape[1]
    for slot in range(4):
        goal = z ^ slot
        outs[slot][piece:, :] = total[piece:, :]

        @pl.when(goal == 0)
        def _(slot=slot):
            outs[slot][0:piece, :] = total[0:piece, :]

        @pl.when(goal != 0)
        def _(slot=slot, goal=goal):
            outs[slot][0:piece, :] = ff[jnp.maximum(goal - 1, 0)]


def plane_sum(place, a, b, c, d, ff):
    return call(
        plane_sum_kernel,
        [shape(a.shape, BF16)] * 4,
        [place, a, b, c, d, ff],
        [],
        "sum_plane_tail",
        1_000_000,
        [pltpu.SMEM] + [VMEM] * 5,
    )


def adam_step(weight, moment_one, moment_two, gradient, step_rate, decay_rate):
    moment_one = BETA_ONE * moment_one + (1.0 - BETA_ONE) * gradient
    moment_two = BETA_TWO * moment_two + (1.0 - BETA_TWO) * gradient * gradient
    mean_hat = moment_one / (1.0 - BETA_ONE**STEP)
    square_hat = moment_two / (1.0 - BETA_TWO**STEP)
    weight = weight - step_rate * (
        mean_hat / (jnp.sqrt(square_hat) + ADAM_EPS) + decay_rate * weight
    )
    return (weight, moment_one, moment_two)


def adam_kernel(feat_dim, place, a, b, c, d, w, m, v, vw, vm, vv, *outs):
    total = (a[...].astype(F32) + b[...].astype(F32)) + (c[...].astype(F32) + d[...].astype(F32))
    piece = w.shape[0]
    rows = place[2] * piece + lax.broadcasted_iota(jnp.int32, w.shape, 0)
    rate = jnp.where(rows < feat_dim, 0.1 * RATE, RATE)
    new = adam_step(w[...], m[...], v[...], total[0:piece, :], rate, DECAY)
    for ref, value in zip(outs[:3], new):
        ref[...] = value
    outs[3][...] = new[0].astype(BF16)
    new = adam_step(vw[...], vm[...], vv[...], total[piece : piece + vw.shape[0], :], RATE, 0.0)
    for ref, value in zip(outs[4:], new):
        ref[...] = value


def adam(place, parts, mats, mats_m, mats_v, vecs, vecs_m, vecs_v, feat_dim):
    mat, vec = shape(mats.shape, F32), shape(vecs.shape, F32)
    return call(
        functools.partial(adam_kernel, feat_dim),
        [mat, mat, mat, shape(mats.shape, BF16), vec, vec, vec],
        [place, *parts, mats, mats_m, mats_v, vecs, vecs_m, vecs_v],
        [],
        "adam",
        10_000_000,
        [pltpu.SMEM] + [VMEM] * 10,
    )


def sine_table(within, model_width):
    half_width = model_width // 2
    frequency = jnp.exp(-jnp.log(10000.0) * jnp.arange(half_width, dtype=F32) / half_width)
    angles = within.astype(F32)[:, None] * frequency[None, :]
    return jnp.concatenate([jnp.sin(angles), jnp.cos(angles)], axis=1)


def grid_swap(dz, dyx):
    return [(4 * z + yx, 4 * (z ^ dz) + (yx ^ dyx)) for z in range(4) for yx in range(4)]


PAIR_SWAP = [(0, 1), (1, 0)]


def per_device(
    flat,
    features,
    cotangent,
    canvas_lengths,
    crop_ids,
    mats,
    mats_m,
    mats_v,
    vecs,
    vecs_m,
    vecs_v,
):
    tok = features.shape[0]
    feat_dim = features.shape[1]
    width = vecs.shape[1]
    attn_rows = feat_dim + 3 * width + width // 2
    ff_rows = width // 2 + 2 * FF
    piece = mats.shape[0]
    dp, core = lax.axis_index("dp"), lax.axis_index("pair")
    device = lax.axis_index(("dp", "pair"))
    place = jnp.stack([dp // 4, dp % 4, device, core]).astype(jnp.int32)

    position = jnp.arange(tok, dtype=jnp.int32)
    first_len = canvas_lengths[0, 0]
    canvas_id = (position >= first_len).astype(jnp.int32)
    within = position - first_len * canvas_id
    pos_table = sine_table(within, width)
    segment = crop_ids * 2 + canvas_id
    segment = (jnp.broadcast_to(segment[:, None], (tok, TILE)), segment.reshape(-1, TILE))

    mats_low = mats.astype(BF16)
    if flat:
        gathered = lax.all_gather(mats_low, ("dp", "pair"), axis=0, tiled=True)
        attn_pieces = [gathered[:attn_rows]]
        ff_pieces = [gathered[attn_rows:]]
    else:
        planes = [lax.ppermute(mats_low, "dp", grid_swap(dz, 0)) for dz in (1, 2, 3)]
        pos_table, segment, planes = lax.optimization_barrier((pos_table, segment, planes))
        one, three = pick_planes(place, mats_low, *planes)
        attn_pieces = [one] + [lax.ppermute(one, "dp", grid_swap(0, s)) for s in (1, 2, 3)]
        attn_pieces += [lax.ppermute(a, "pair", PAIR_SWAP) for a in attn_pieces]
        ff_pieces = [three] + [lax.ppermute(three, "dp", grid_swap(0, s)) for s in (1, 2, 3)]

    wa, emb, src, q, k, v, attn_t, probs, scale_inv = attention(
        flat, place, features, pos_table, segment, vecs, attn_pieces, attn_rows
    )
    if not flat:
        attn_t, *ff_pieces = lax.optimization_barrier((attn_t, *ff_pieces))
        ff_pieces += [lax.ppermute(a, "pair", PAIR_SWAP) for a in ff_pieces]
    output, g_one, w_out, vg, dwo, *ff_grads = feed(
        flat, place, emb, attn_t, cotangent, vecs, wa, ff_pieces, ff_rows
    )
    if not flat:
        keep, send = ff_grads
        sums = ff_sum(place, keep, lax.ppermute(send, "pair", PAIR_SWAP))
        g_one, *sums = lax.optimization_barrier((g_one, *sums))
        ff_parts = [sums[0]] + [lax.ppermute(sums[s], "dp", grid_swap(0, s)) for s in (1, 2, 3)]
    ql, kl, vl = attention_back(g_one, q, k, v, probs, scale_inv, attn_t, w_out)
    if not flat:
        ql, kl, vl, *ff_parts = lax.optimization_barrier((ql, kl, vl, *ff_parts))
        ff = four_sum(*ff_parts)
    low, *tail = project_back(
        flat, place, features, emb, src, g_one, ql, kl, vl, dwo, vg, wa, piece
    )
    feature_grad = feature_back(low, wa, feat_dim)
    if flat:
        grads = jnp.concatenate([tail[0], ff_grads[0]], axis=0).astype(F32)
        total = lax.psum_scatter(grads, ("dp", "pair"), scatter_dimension=0, tiled=True)
        vec_total = lax.psum(tail[1], ("dp", "pair"))
        row_ids = device * piece + jnp.arange(piece, dtype=jnp.int32)
        rate = jnp.where(row_ids < feat_dim, 0.1 * RATE, RATE)[:, None]
        new = adam_step(mats, mats_m, mats_v, total, rate, DECAY)
        new_vec = adam_step(vecs, vecs_m, vecs_v, vec_total, RATE, 0.0)
        return (output, feature_grad, *new, new[0].astype(BF16), *new_vec)
    keep, send = tail
    sums = tail_sum(place, keep, lax.ppermute(send, "pair", PAIR_SWAP), piece)
    parts = [sums[0]] + [lax.ppermute(sums[s], "dp", grid_swap(0, s)) for s in (1, 2, 3)]
    sums = plane_sum(place, *parts, ff)
    parts = [sums[0]] + [lax.ppermute(sums[s], "dp", grid_swap(s, 0)) for s in (1, 2, 3)]
    new = adam(place, parts, mats, mats_m, mats_v, vecs, vecs_m, vecs_v, feat_dim)
    return (output, feature_grad, *new)


def solution(mesh):
    rows = P(("dp", "pair"), None)
    in_specs = (rows, rows, rows, P(("dp", "pair")), rows, rows, rows, P(), P(), P())
    out_specs = (rows, rows, rows, rows, rows, rows, P(), P(), P())
    flat = mesh.shape["dp"] != 16 or mesh.shape["pair"] != 2
    return jax.shard_map(
        functools.partial(per_device, flat),
        mesh=mesh,
        in_specs=in_specs,
        out_specs=out_specs,
        check_vma=False,
    )
```

```python
import functools
import math

import jax
import jax.numpy as jnp
from jax import lax
from jax.experimental import pallas as pl
from jax.experimental.pallas import tpu as pltpu
from jax.sharding import PartitionSpec as P

HEADS = 8
FF = 2048
STEP = 10

EPS_NORM = 1e-05
RATE = 0.2
BETA_ONE = 0.9
BETA_TWO = 0.999
ADAM_EPS = 1e-08
DECAY = 0.0001
MASKED = -1000000000.0

TILE = 128
WINDOW = 384
ROWS = 512
BLOCK = 256
BLOCKS = FF // BLOCK
GELU_A = 0.7978845608028654
GELU_B = 0.044715
LOG2_E = 1.4426950408889634
VEC_PAD = 32

F32 = jnp.float32
BF16 = jnp.bfloat16
VMEM = pltpu.VMEM


def nn(a, b):
    return lax.dot_general(a, b, (((1,), (0,)), ((), ())), preferred_element_type=F32)


def nt(a, b):
    return lax.dot_general(a, b, (((1,), (1,)), ((), ())), preferred_element_type=F32)


def tn(a, b):
    return lax.dot_general(a, b, (((0,), (0,)), ((), ())), preferred_element_type=F32)


def row_mean(x):
    return jnp.sum(x, axis=1, keepdims=True) * (1.0 / x.shape[1])


def fold_rows(x):
    return jnp.sum(x.reshape(x.shape[0] // 8, 8, x.shape[1]), axis=0)


def column_sum(x):
    return jnp.sum(x.astype(F32), axis=0, keepdims=True)


def head_lanes(h, rows, width):
    lane = lax.broadcasted_iota(jnp.int32, (rows, width), 1)
    size = width // HEADS
    return (lane >= h * size) & (lane < (h + 1) * size)


def window_start(i, tok):
    return jnp.clip((i - 1) * TILE, 0, tok - WINDOW)


def call(kernel, outs, ins, scratch, name, flops, spaces=None, vmem=12):
    spaces = spaces or [VMEM] * len(ins)
    nbytes = 0 * sum(a.size * a.dtype.itemsize for a in ins) + sum(
        a.size * a.dtype.itemsize for a in outs
    )
    return pl.pallas_call(
        kernel,
        out_shape=tuple(outs),
        in_specs=[pl.BlockSpec(memory_space=s) for s in spaces],
        out_specs=tuple(pl.BlockSpec(memory_space=VMEM) for _ in outs),
        scratch_shapes=scratch,
        compiler_params=pltpu.CompilerParams(vmem_limit_bytes=vmem << 20),
        cost_estimate=pl.CostEstimate(flops=flops, bytes_accessed=nbytes, transcendentals=0),
        name=name,
    )(*ins)


def shape(dims, kind):
    return jax.ShapeDtypeStruct(dims, kind)


def load_pieces(refs, offsets, dst):
    for ref, offs in zip(refs, offsets):
        if len(ref.shape) == 2:
            dst[pl.ds(offs[0], ref.shape[0]), :] = ref[...]
        else:
            for i, off in enumerate(offs):
                dst[pl.ds(off, ref.shape[1]), :] = ref[i]


def place_offsets(place, piece, planes):
    offsets = []
    for other in (0, 1):
        for slot in range(4):
            core = place[3] ^ other if other else place[3]
            inner = 2 * (place[1] ^ slot) + core
            offsets.append(
                [pl.multiple_of((8 * plane + inner) * piece, 16) for plane in range(planes)]
            )
    return offsets


def prepare_kernel(lens, crops, feat, vec, pos, seg_col, seg_row, feat_near, vec_near):
    feat_near[...] = feat[...]
    vec_near[...] = vec[...]
    tok, width = pos.shape
    half = width // 2
    first = lens[0, 0]
    lane = lax.broadcasted_iota(jnp.int32, (TILE, half), 1)
    frequency = jnp.exp(lane.astype(F32) * (-math.log(10000.0) / half))
    at = lax.broadcasted_iota(jnp.int32, (tok // TILE, TILE), 0) * TILE
    at = at + lax.broadcasted_iota(jnp.int32, (tok // TILE, TILE), 1)
    seg_row[...] = (2 * crops[...] + (at >= first).astype(jnp.int32)).astype(F32)
    for i in range(tok // TILE):
        r = slice(i * TILE, (i + 1) * TILE)
        row = lax.broadcasted_iota(jnp.int32, (TILE, half), 0) + i * TILE
        angle = (row - jnp.where(row >= first, first, 0)).astype(F32) * frequency
        pos[r, 0:half] = jnp.sin(angle)
        pos[r, half:width] = jnp.cos(angle)
        seg_col[r, :] = jnp.broadcast_to(seg_row[i : i + 1, :], (TILE, TILE)).T


def prepare(lens, crops, feat, vec):
    tok, width = crops.shape[0], vec.shape[1]
    crops = crops.reshape(-1, TILE)
    return call(
        prepare_kernel,
        [
            shape((tok, width), F32),
            shape((tok, TILE), F32),
            shape(crops.shape, F32),
            shape(feat.shape, BF16),
            shape(vec.shape, F32),
        ],
        [lens, crops, feat, vec],
        [],
        "positions_segments",
        1_000_000,
        [pltpu.SMEM, VMEM, VMEM, VMEM],
    )


def attention_kernel(flat, piece, place, feat, pos, seg_col, seg_row, vec, *rest):
    count = 1 if flat else 8
    pieces, rest = rest[:count], rest[count:]
    w, emb, src, q, k, v, attn_t, p, scale_inv, v_t, q_t = rest
    tok, width = emb.shape
    feat_dim = feat.shape[1]
    size = width // HEADS
    scale = size ** (-0.5)
    offsets = [[0]] if flat else place_offsets(place, piece, 1)
    load_pieces(pieces, offsets, w)
    for i in range(tok // ROWS):
        r = pl.ds(i * ROWS, ROWS)
        e = nn(feat[r, :], w[0:feat_dim, :]) + vec[0:1, :]
        emb[r, :] = e
        s = (e + pos[r, :]).astype(BF16)
        src[r, :] = s
        low = e.astype(BF16)
        at = feat_dim
        q[r, :] = (nn(s, w[at : at + width, :]) + vec[1:2, :]).astype(BF16)
        k[r, :] = nn(s, w[at + width : at + 2 * width, :]).astype(BF16)
        v[r, :] = (nn(low, w[at + 2 * width : at + 3 * width, :]) + vec[2:3, :]).astype(BF16)
    pad = v_t.shape[0] // HEADS
    vals = v[...].T
    for h in range(HEADS):
        v_t[h * pad : h * pad + size, :] = vals[h * size : (h + 1) * size, :]
        v_t[h * pad + size : (h + 1) * pad, :] = jnp.ones((pad - size, tok), BF16)
    q_t[...] = jnp.zeros_like(q_t)
    masked = MASKED / scale
    factor = scale * LOG2_E

    def tile(i, carry):
        rows = pl.ds(pl.multiple_of(i * TILE, TILE), TILE)
        win = pl.ds(pl.multiple_of(window_start(i, tok), TILE), WINDOW)
        own_t = q[rows, :].T
        keys = k[win, :]
        vals_t = v_t[:, win]
        allowed = seg_col[win, :] == seg_row[pl.ds(i, 1), :]
        for h in range(HEADS):
            d = slice(h * size, (h + 1) * size)
            q_t[d, h * TILE : (h + 1) * TILE] = own_t[d, :]
        for g in range(HEADS // 8):
            both = nn(keys, q_t[:, 8 * g * TILE : (8 * g + 8) * TILE])
            for u in range(8):
                h = 8 * g + u
                s = jnp.where(allowed, both[:, u * TILE : (u + 1) * TILE], masked)
                top = jnp.max(s, axis=0, keepdims=True)
                e = jnp.exp2((s - top) * factor).astype(BF16)
                p[i, :, h * TILE : (h + 1) * TILE] = e
        for g in range(HEADS // 2):
            o = nn(
                vals_t[2 * g * pad : (2 * g + 2) * pad, :],
                p[i, :, 2 * g * TILE : (2 * g + 2) * TILE],
            )
            for u in range(2):
                h = 2 * g + u
                own = o[u * pad : (u + 1) * pad, u * TILE : (u + 1) * TILE]
                inv = 1.0 / own[size : size + 1, :]
                scale_inv[i, h : h + 1, :] = inv
                attn_t[h * size : (h + 1) * size, rows] = (own[0:size, :] * inv).astype(BF16)
        return carry

    lax.fori_loop(0, tok // TILE, tile, 0, unroll=8)


def attention(flat, place, feat, pos, segment, vec, pieces, attn_rows):
    tok, width = feat.shape[0], vec.shape[1]
    piece = pieces[0].shape[0]
    low = shape((tok, width), BF16)
    outs = [
        shape((attn_rows, width), BF16),
        shape((tok, width), F32),
        low,
        low,
        low,
        low,
        shape((width, tok), BF16),
        shape((tok // TILE, WINDOW, HEADS * TILE), BF16),
        shape((tok // TILE, HEADS, TILE), F32),
    ]
    ins = [place, feat, pos, *segment, vec, *pieces]
    return call(
        functools.partial(attention_kernel, flat, piece),
        outs,
        ins,
        [
            VMEM((width + 16 * HEADS, tok), BF16),
            VMEM((width, HEADS * TILE), BF16),
        ],
        "attention_forward",
        1_200_000_000,
        [pltpu.SMEM] + [VMEM] * (5 + len(pieces)),
        vmem=20,
    )


def feed_kernel(flat, piece, place, emb, attn_t, cot, vec, wa, *rest):
    count = 1 if flat else 8
    pieces, rest = rest[:count], rest[count:]
    outs = 5 if flat else 6
    res, rest = rest[: outs + 1], rest[outs + 1 :]
    out, g_one, w_out, vec_grad, dwo = res[:5]
    (wf, wh, wh_t, wb_t, half_a, half_b, act, pre, slope, n_t, b_t, out_all, acc, gff) = rest
    halves = (half_a, half_b)
    tok, width = emb.shape
    first = width // 2
    offsets = [[0]] if flat else place_offsets(place, piece, 3)
    load_pieces(pieces, offsets, wf)
    for u in range(2):
        halves[u][...] = wf[first : first + FF, u * 128 : (u + 1) * 128].astype(F32)
    w_out[0:first, :] = wa[wa.shape[0] - first :, :]
    w_out[first:, :] = wf[0:first, :]
    for j in range(BLOCKS):
        c = slice(j * BLOCK, (j + 1) * BLOCK)
        w = jnp.concatenate(
            [halves[u][pl.ds(j, width, stride=BLOCKS), :] for u in range(2)], axis=1
        ).astype(BF16)
        wh[:, c] = w
        wh_t[c, :] = w.T
        wb_t[:, c] = wf[first + FF + j * BLOCK : first + FF + (j + 1) * BLOCK, :].T
    acc[...] = jnp.zeros_like(acc)
    n_t[width : width + 8, :] = jnp.ones((8, tok), BF16)

    def tile(i, carry):
        r = pl.ds(pl.multiple_of(i * ROWS, ROWS), ROWS)
        res_one = emb[r, :] + tn(attn_t[:, r], w_out[...]) + vec[3:4, :]
        cen = res_one - row_mean(res_one)
        inv_one = lax.rsqrt(row_mean(cen * cen) + EPS_NORM)
        hat_one = cen * inv_one
        normed = hat_one * vec[4:5, :] + vec[5:6, :]
        low = normed.astype(BF16)
        for j in range(BLOCKS):
            c = slice(j * BLOCK, (j + 1) * BLOCK)
            x = nn(low, wh[:, c]) + vec[9 + j : 10 + j, :]
            sq = x * x
            t = jnp.tanh(x * (GELU_A + (GELU_A * GELU_B) * sq))
            half = 0.5 + 0.5 * t
            act[r, c] = (x * half).astype(BF16)
            bend = x * ((2 * GELU_A) + (6 * GELU_A * GELU_B) * sq)
            slope[r, c] = (half + (half - half * half) * bend).astype(BF16)
        res_two = normed + nn(act[r, :], wf[first + FF : first + 2 * FF, :]) + vec[6:7, :]
        cen = res_two - row_mean(res_two)
        inv_two = lax.rsqrt(row_mean(cen * cen) + EPS_NORM)
        hat_two = cen * inv_two
        out[r, :] = hat_two * vec[7:8, :] + vec[8:9, :]
        ct = cot[r, :].astype(F32)
        gs = ct * vec[7:8, :]
        g_two = inv_two * (gs - row_mean(gs) - hat_two * row_mean(gs * hat_two))
        back = g_two.astype(BF16)
        b_t[:, r] = back.T
        acc[0] += fold_rows(back.astype(F32))
        acc[1] += fold_rows(ct * hat_two)
        acc[2] += fold_rows(ct)
        for j in range(BLOCKS):
            c = slice(j * BLOCK, (j + 1) * BLOCK)
            pre[r, c] = (nn(back, wb_t[:, c]) * slope[r, c].astype(F32)).astype(BF16)
        g_norm = g_two + nn(pre[r, :], wh_t[...])
        n_t[0:width, r] = low.T
        gs = g_norm * vec[4:5, :]
        g_res = inv_one * (gs - row_mean(gs) - hat_one * row_mean(gs * hat_one))
        g_one[r, :] = g_res
        out_low = g_res.astype(BF16)
        out_all[r, :] = out_low
        acc[3] += fold_rows(out_low.astype(F32))
        acc[4] += fold_rows(g_norm * hat_one)
        acc[5] += fold_rows(g_norm)
        return carry

    lax.fori_loop(0, tok // ROWS, tile, 0, unroll=2)
    for j in range(BLOCKS):
        c = slice(j * BLOCK, (j + 1) * BLOCK)
        g = nn(n_t[...], pre[:, c])
        for u in range(2):
            halves[u][pl.ds(j, width, stride=BLOCKS), :] = g[0:width, u * 128 : (u + 1) * 128]
        vec_grad[9 + j : 10 + j, :] = g[width : width + 1, :]
        at = first + FF + j * BLOCK
        gff[at : at + BLOCK, :] = nn(b_t[...], act[:, c]).T.astype(BF16)
    for u in range(2):
        gff[first : first + FF, u * 128 : (u + 1) * 128] = halves[u][...].astype(BF16)
    g = nn(attn_t[...], out_all[...]).astype(BF16)
    dwo[...] = g[0:first, :]
    gff[0:first, :] = g[first:, :]
    sums = jnp.sum(acc[...], axis=1)
    vec_grad[0:3, :] = jnp.zeros((3, width), F32)
    for row, at in ((3, 3), (4, 4), (5, 5), (6, 0), (7, 1), (8, 2)):
        vec_grad[row : row + 1, :] = sums[at : at + 1, :]
    if flat:
        res[5][...] = gff[...]
    else:
        split_cores(place, gff, res[5], res[6])


def split_cores(place, grads, keep, send):
    core = place[3]
    piece = keep.shape[1]
    for m in range(keep.shape[0]):
        keep[m] = grads[pl.ds(pl.multiple_of((2 * m + core) * piece, 16), piece), :]
        send[m] = grads[pl.ds(pl.multiple_of((2 * m + 1 - core) * piece, 16), piece), :]


def feed(flat, place, emb, attn_t, cot, vec, wa, pieces, ff_rows):
    tok, width = emb.shape
    piece = pieces[0].shape[-2]
    outs = [
        shape((tok, width), F32),
        shape((tok, width), F32),
        shape((width, width), BF16),
        shape(vec.shape, F32),
        shape((width // 2, width), BF16),
    ]
    if flat:
        outs += [shape((ff_rows, width), BF16)]
    else:
        outs += [shape((ff_rows // piece // 2, piece, width), BF16)] * 2
    return call(
        functools.partial(feed_kernel, flat, piece),
        outs,
        [place, emb, attn_t, cot, vec, wa, *pieces],
        [
            VMEM((ff_rows, width), BF16),
            VMEM((width, FF), BF16),
            VMEM((FF, width), BF16),
            VMEM((width, FF), BF16),
            VMEM((FF, 128), F32),
            VMEM((FF, 128), F32),
            VMEM((tok, FF), BF16),
            VMEM((tok, FF), BF16),
            VMEM((tok, FF), BF16),
            VMEM((width + 8, tok), BF16),
            VMEM((width, tok), BF16),
            VMEM((tok, width), BF16),
            VMEM((6, 8, width), F32),
            VMEM((ff_rows, width), BF16),
        ],
        "feed_forward_both",
        14_000_000_000,
        [pltpu.SMEM] + [VMEM] * (5 + len(pieces)),
        vmem=34,
    )


def attention_back(g_one, q, k, v, p, scale_inv, attn_t, w_out, ql, kl, vl, *scratch):
    ag, k_t, ds_all, a_t, scaled, qm, am, dk, dv = scratch
    tok, width = g_one.shape
    size = width // HEADS
    scale = size ** (-0.5)
    for i in range(tok // ROWS):
        r = pl.ds(i * ROWS, ROWS)
        ag[r, :] = nt(g_one[r, :].astype(BF16), w_out[...]).astype(BF16)
    k_t[...] = k[...].T
    dk[...] = jnp.zeros_like(dk)
    dv[...] = jnp.zeros_like(dv)
    a_t[...] = jnp.zeros_like(a_t)

    def tile(i, carry):
        rows = pl.ds(pl.multiple_of(i * TILE, TILE), TILE)
        win = pl.ds(pl.multiple_of(window_start(i, tok), TILE), WINDOW)
        own_q = q[rows, :]
        own_t = ag[rows, :].T
        vals = v[win, :]
        keys_t = k_t[:, win]
        inner = []
        for h in range(HEADS):
            d = slice(h * size, (h + 1) * size)
            grad = own_t[d, :].astype(F32) * scale_inv[i, h : h + 1, :]
            inner.append(jnp.sum(grad * attn_t[d, rows].astype(F32), axis=0, keepdims=True))
            a_t[d, h * TILE : (h + 1) * TILE] = grad.astype(BF16)
            scaled[d, :] = grad.astype(BF16)
        own_a = scaled[...].T
        for h in range(HEADS):
            lanes = head_lanes(h, TILE, width)
            c = slice(h * TILE, (h + 1) * TILE)
            qm[c, :] = jnp.where(lanes, own_q, jnp.zeros_like(own_q))
            am[c, :] = jnp.where(lanes, own_a, jnp.zeros_like(own_a))
        parts = []
        for g in range(HEADS // 8):
            both = nn(vals, a_t[:, 8 * g * TILE : (8 * g + 8) * TILE])
            for u in range(8):
                h = 8 * g + u
                c = slice(h * TILE, (h + 1) * TILE)
                dp = both[:, u * TILE : (u + 1) * TILE]
                ds = (p[i, :, c].astype(F32) * (dp - inner[h])).astype(BF16)
                ds_all[:, c] = ds
        for g in range(HEADS // 2):
            o = nn(
                keys_t[2 * g * size : (2 * g + 2) * size, :],
                ds_all[:, 2 * g * TILE : (2 * g + 2) * TILE],
            )
            parts += [o[0:size, 0:TILE], o[size : 2 * size, TILE : 2 * TILE]]
        ql[rows, :] = (jnp.concatenate(parts, axis=0).T * scale).astype(BF16)
        dk[win, :] += nn(ds_all[...], qm[...])
        dv[win, :] += nn(p[i], am[...])
        return carry

    lax.fori_loop(0, tok // TILE, tile, 0, unroll=8)
    kl[...] = (dk[...] * scale).astype(BF16)
    vl[...] = dv[...].astype(BF16)


def backward_kernel(flat, piece, place, g_one, q, k, v, p, scale_inv, attn_t, w_out, *rest):
    feat, emb, src, dwo, vg, wa, low_out, *outs = rest[:9]
    grads, ql, kl, vl, *scratch = rest[9:]
    attention_back(g_one, q, k, v, p, scale_inv, attn_t, w_out, ql, kl, vl, *scratch)
    tok, width = g_one.shape
    at = feat.shape[1]
    total = jnp.zeros((1, width), F32)
    for i in range(tok // ROWS):
        r = pl.ds(i * ROWS, ROWS)
        e = (
            g_one[r, :]
            + nt(ql[r, :], wa[at : at + width, :])
            + nt(kl[r, :], wa[at + width : at + 2 * width, :])
            + nt(vl[r, :], wa[at + 2 * width : at + 3 * width, :])
        )
        low = e.astype(BF16)
        low_out[r, :] = low
        total += column_sum(low)
    src_t = src[...].T
    grads[at : at + width, :] = nn(src_t, ql[...]).astype(BF16)
    grads[at + width : at + 2 * width, :] = nn(src_t, kl[...]).astype(BF16)
    grads[at + 2 * width : at + 3 * width, :] = nn(emb[...].astype(BF16).T, vl[...]).astype(BF16)
    grads[0:at, :] = nn(feat[...].T, low_out[...]).astype(BF16)
    grads[at + 3 * width :, :] = dwo[...]
    front = jnp.concatenate([total, column_sum(ql[...]), column_sum(vl[...])], axis=0)
    if flat:
        outs[0][...] = grads[...]
        outs[1][...] = vg[...]
        outs[1][0:3, :] = front
        return
    keep, send = outs
    core = place[3]
    for m in range(4):
        to = pl.ds(m * piece, piece)
        keep[to, :] = grads[pl.ds(pl.multiple_of((2 * m + core) * piece, 16), piece), :]
        send[to, :] = grads[pl.ds(pl.multiple_of((2 * m + 1 - core) * piece, 16), piece), :]
    rows = vg.shape[0]
    pad = jnp.zeros((VEC_PAD - rows, width), F32)
    tail = jnp.concatenate([front, vg[3:rows, :], pad], axis=0).astype(BF16)
    for ref in (keep, send):
        ref[4 * piece :, :] = tail


def backward(flat, place, g_one, q, k, v, p, scale_inv, attn_t, w_out, feat, emb, src, *rest):
    dwo, vg, wa, piece = rest
    tok, width = g_one.shape
    outs = [shape((tok, width), BF16)]
    if flat:
        outs += [shape(wa.shape, BF16), shape(vg.shape, F32)]
    else:
        outs += [shape((4 * piece + VEC_PAD, width), BF16)] * 2
    ins = [place, g_one, q, k, v, p, scale_inv, attn_t, w_out, feat, emb, src, dwo, vg, wa]
    low = VMEM((tok, width), BF16)
    return call(
        functools.partial(backward_kernel, flat, piece),
        outs,
        ins,
        [
            VMEM(wa.shape, BF16),
            low,
            low,
            low,
            low,
            VMEM((width, tok), BF16),
            VMEM((WINDOW, HEADS * TILE), BF16),
            VMEM((width, HEADS * TILE), BF16),
            VMEM((width, TILE), BF16),
            VMEM((HEADS * TILE, width), BF16),
            VMEM((HEADS * TILE, width), BF16),
            VMEM((tok, width), F32),
            VMEM((tok, width), F32),
        ],
        "attention_backward",
        16_000_000_000,
        [pltpu.SMEM] + [VMEM] * (len(ins) - 1),
        vmem=24,
    )


def feature_kernel(low, wa, out):
    for i in range(low.shape[0] // ROWS):
        r = pl.ds(i * ROWS, ROWS)
        out[r, :] = nt(low[r, :], wa[0 : out.shape[1], :])


def feature_back(low, wa, feat_dim):
    return call(
        feature_kernel,
        [shape((low.shape[0], feat_dim), F32)],
        [low, wa],
        [],
        "feature_gradient",
        300_000_000,
    )[0]


def plane_kernel(place, own, one, two, three, attn, rest):
    got = (own, one, two, three)
    z = place[0]
    for slot in range(4):

        @pl.when(z == slot)
        def _(slot=slot):
            attn[...] = got[slot][...]
            for plane in range(1, 4):
                rest[plane - 1] = got[slot ^ plane][...]


def pick_planes(place, own, one, two, three):
    return call(
        plane_kernel,
        [shape(own.shape, BF16), shape((3, *own.shape), BF16)],
        [place, own, one, two, three],
        [],
        "pick_planes",
        1_000_000,
        [pltpu.SMEM] + [VMEM] * 4,
    )


def ff_sum_kernel(place, keep, recv, *outs):
    yx = place[1]
    for slot in range(4):
        for plane in range(3):
            at = 4 * plane + (yx ^ slot)
            outs[slot][plane] = (keep[at].astype(F32) + recv[at].astype(F32)).astype(BF16)


def ff_sum(place, keep, recv):
    one = shape((3, *keep.shape[1:]), BF16)
    return call(
        ff_sum_kernel,
        [one] * 4,
        [place, keep, recv],
        [],
        "sum_cores_ff",
        1_000_000,
        [pltpu.SMEM] + [VMEM] * 2,
    )


def four_kernel(a, b, c, d, out):
    out[...] = (
        (a[...].astype(F32) + b[...].astype(F32)) + (c[...].astype(F32) + d[...].astype(F32))
    ).astype(BF16)


def four_sum(a, b, c, d):
    return call(four_kernel, [shape(a.shape, BF16)], [a, b, c, d], [], "sum_plane_ff", 1_000_000)[0]


def tail_sum_kernel(piece, place, keep, recv, *outs):
    yx = place[1]
    vec = keep[4 * piece :, :].astype(F32) + recv[4 * piece :, :].astype(F32)
    for slot in range(4):
        r = pl.ds(pl.multiple_of((yx ^ slot) * piece, 16), piece)
        outs[slot][0:piece, :] = (keep[r, :].astype(F32) + recv[r, :].astype(F32)).astype(BF16)
        outs[slot][piece:, :] = vec.astype(BF16)


def tail_sum(place, keep, recv, piece):
    return call(
        functools.partial(tail_sum_kernel, piece),
        [shape((piece + VEC_PAD, keep.shape[1]), BF16)] * 4,
        [place, keep, recv],
        [],
        "sum_cores_tail",
        1_000_000,
        [pltpu.SMEM] + [VMEM] * 2,
    )


def plane_sum_kernel(place, a, b, c, d, ff, *outs):
    z = place[0]
    total = (
        (a[...].astype(F32) + b[...].astype(F32)) + (c[...].astype(F32) + d[...].astype(F32))
    ).astype(BF16)
    piece = ff.shape[1]
    for slot in range(4):
        goal = z ^ slot
        outs[slot][piece:, :] = total[piece:, :]

        @pl.when(goal == 0)
        def _(slot=slot):
            outs[slot][0:piece, :] = total[0:piece, :]

        @pl.when(goal != 0)
        def _(slot=slot, goal=goal):
            outs[slot][0:piece, :] = ff[jnp.maximum(goal - 1, 0)]


def plane_sum(place, a, b, c, d, ff):
    return call(
        plane_sum_kernel,
        [shape(a.shape, BF16)] * 4,
        [place, a, b, c, d, ff],
        [],
        "sum_plane_tail",
        1_000_000,
        [pltpu.SMEM] + [VMEM] * 5,
    )


def adam_step(weight, moment_one, moment_two, gradient, step_rate, decay_rate):
    moment_one = BETA_ONE * moment_one + (1.0 - BETA_ONE) * gradient
    moment_two = BETA_TWO * moment_two + (1.0 - BETA_TWO) * gradient * gradient
    mean_hat = moment_one / (1.0 - BETA_ONE**STEP)
    square_hat = moment_two / (1.0 - BETA_TWO**STEP)
    weight = weight - step_rate * (
        mean_hat / (jnp.sqrt(square_hat) + ADAM_EPS) + decay_rate * weight
    )
    return (weight, moment_one, moment_two)


def adam_kernel(feat_dim, place, a, b, c, d, w, m, v, vw, vm, vv, *outs):
    total = (a[...].astype(F32) + b[...].astype(F32)) + (c[...].astype(F32) + d[...].astype(F32))
    piece = w.shape[0]
    rows = place[2] * piece + lax.broadcasted_iota(jnp.int32, w.shape, 0)
    rate = jnp.where(rows < feat_dim, 0.1 * RATE, RATE)
    new = adam_step(w[...], m[...], v[...], total[0:piece, :], rate, DECAY)
    for ref, value in zip(outs[:3], new):
        ref[...] = value
    outs[3][...] = new[0].astype(BF16)
    new = adam_step(vw[...], vm[...], vv[...], total[piece : piece + vw.shape[0], :], RATE, 0.0)
    for ref, value in zip(outs[4:], new):
        ref[...] = value


def adam(place, parts, mats, mats_m, mats_v, vecs, vecs_m, vecs_v, feat_dim):
    mat, vec = shape(mats.shape, F32), shape(vecs.shape, F32)
    return call(
        functools.partial(adam_kernel, feat_dim),
        [mat, mat, mat, shape(mats.shape, BF16), vec, vec, vec],
        [place, *parts, mats, mats_m, mats_v, vecs, vecs_m, vecs_v],
        [],
        "adam",
        10_000_000,
        [pltpu.SMEM] + [VMEM] * 10,
    )


def grid_swap(dz, dyx):
    return [(4 * z + yx, 4 * (z ^ dz) + (yx ^ dyx)) for z in range(4) for yx in range(4)]


PAIR_SWAP = [(0, 1), (1, 0)]


def per_device(
    flat,
    features,
    cotangent,
    canvas_lengths,
    crop_ids,
    mats,
    mats_m,
    mats_v,
    vecs,
    vecs_m,
    vecs_v,
):
    tok = features.shape[0]
    feat_dim = features.shape[1]
    width = vecs.shape[1]
    attn_rows = feat_dim + 3 * width + width // 2
    ff_rows = width // 2 + 2 * FF
    piece = mats.shape[0]
    dp, core = lax.axis_index("dp"), lax.axis_index("pair")
    device = lax.axis_index(("dp", "pair"))
    place = jnp.stack([dp // 4, dp % 4, device, core]).astype(jnp.int32)

    near = prepare(canvas_lengths, crop_ids, features, vecs)
    mats_low = mats.astype(BF16)
    if flat:
        gathered = lax.all_gather(mats_low, ("dp", "pair"), axis=0, tiled=True)
        attn_pieces = [gathered[:attn_rows]]
        ff_pieces = [gathered[attn_rows:]]
    else:
        planes = [lax.ppermute(mats_low, "dp", grid_swap(dz, 0)) for dz in (1, 2, 3)]
        near, planes = lax.optimization_barrier((near, planes))
        one, three = pick_planes(place, mats_low, *planes)
        attn_pieces = [one] + [lax.ppermute(one, "dp", grid_swap(0, s)) for s in (1, 2, 3)]
        attn_pieces += [lax.ppermute(a, "pair", PAIR_SWAP) for a in attn_pieces]
        ff_pieces = [three] + [lax.ppermute(three, "dp", grid_swap(0, s)) for s in (1, 2, 3)]

    pos_table, seg_col, seg_row, features, vec = near
    wa, emb, src, q, k, v, attn_t, probs, scale_inv = attention(
        flat, place, features, pos_table, (seg_col, seg_row), vec, attn_pieces, attn_rows
    )
    if not flat:
        own_swap = lax.ppermute(ff_pieces[0], "pair", PAIR_SWAP)
        attn_t, *moved = lax.optimization_barrier((attn_t, *ff_pieces[1:]))
        moved_swap = [lax.ppermute(a, "pair", PAIR_SWAP) for a in moved]
        ff_pieces = [ff_pieces[0], *moved, own_swap, *moved_swap]
    output, g_one, w_out, vg, dwo, *ff_grads = feed(
        flat, place, emb, attn_t, cotangent, vec, wa, ff_pieces, ff_rows
    )
    if not flat:
        keep, send = ff_grads
        sums = ff_sum(place, keep, lax.ppermute(send, "pair", PAIR_SWAP))
        g_one, *sums = lax.optimization_barrier((g_one, *sums))
        ff_parts = [sums[0]] + [lax.ppermute(sums[s], "dp", grid_swap(0, s)) for s in (1, 2, 3)]
    low, *tail = backward(
        flat,
        place,
        g_one,
        q,
        k,
        v,
        probs,
        scale_inv,
        attn_t,
        w_out,
        features,
        emb,
        src,
        dwo,
        vg,
        wa,
        piece,
    )
    feature_grad = feature_back(low, wa, feat_dim)
    if flat:
        grads = jnp.concatenate([tail[0], ff_grads[0]], axis=0).astype(F32)
        total = lax.psum_scatter(grads, ("dp", "pair"), scatter_dimension=0, tiled=True)
        vec_total = lax.psum(tail[1], ("dp", "pair"))
        row_ids = device * piece + jnp.arange(piece, dtype=jnp.int32)
        rate = jnp.where(row_ids < feat_dim, 0.1 * RATE, RATE)[:, None]
        new = adam_step(mats, mats_m, mats_v, total, rate, DECAY)
        new_vec = adam_step(vecs, vecs_m, vecs_v, vec_total, RATE, 0.0)
        return (output, feature_grad, *new, new[0].astype(BF16), *new_vec)
    keep, send, *ff_parts = lax.optimization_barrier((*tail, *ff_parts))
    ff = four_sum(*ff_parts)
    sums = tail_sum(place, keep, lax.ppermute(send, "pair", PAIR_SWAP), piece)
    parts = [sums[0]] + [lax.ppermute(sums[s], "dp", grid_swap(0, s)) for s in (1, 2, 3)]
    sums = plane_sum(place, *parts, ff)
    parts = [sums[0]] + [lax.ppermute(sums[s], "dp", grid_swap(s, 0)) for s in (1, 2, 3)]
    new = adam(place, parts, mats, mats_m, mats_v, vecs, vecs_m, vecs_v, feat_dim)
    return (output, feature_grad, *new)


def solution(mesh):
    rows = P(("dp", "pair"), None)
    in_specs = (rows, rows, rows, P(("dp", "pair")), rows, rows, rows, P(), P(), P())
    out_specs = (rows, rows, rows, rows, rows, rows, P(), P(), P())
    flat = mesh.shape["dp"] != 16 or mesh.shape["pair"] != 2
    return jax.shard_map(
        functools.partial(per_device, flat),
        mesh=mesh,
        in_specs=in_specs,
        out_specs=out_specs,
        check_vma=False,
    )
```

```python
import functools
import math

import jax
import jax.numpy as jnp
from jax import lax
from jax.experimental import pallas as pl
from jax.experimental.pallas import tpu as pltpu
from jax.sharding import PartitionSpec as P

HEADS = 8
FF = 2048
STEP = 10

EPS_NORM = 1e-05
RATE = 0.2
BETA_ONE = 0.9
BETA_TWO = 0.999
ADAM_EPS = 1e-08
DECAY = 0.0001
MASKED = -1000000000.0

TILE = 128
WINDOW = 384
ROWS = 512
FEED_ROWS = 1024
BLOCK = 256
BLOCKS = FF // BLOCK
GELU_A = 0.7978845608028654
GELU_B = 0.044715
LOG2_E = 1.4426950408889634
VEC_PAD = 32

F32 = jnp.float32
BF16 = jnp.bfloat16
VMEM = pltpu.VMEM


def nn(a, b):
    return lax.dot_general(a, b, (((1,), (0,)), ((), ())), preferred_element_type=F32)


def nt(a, b):
    return lax.dot_general(a, b, (((1,), (1,)), ((), ())), preferred_element_type=F32)


def tn(a, b):
    return lax.dot_general(a, b, (((0,), (0,)), ((), ())), preferred_element_type=F32)


def row_mean(x):
    return jnp.sum(x, axis=1, keepdims=True) * (1.0 / x.shape[1])


def fold_rows(x):
    return jnp.sum(x.reshape(x.shape[0] // 8, 8, x.shape[1]), axis=0)


def column_sum(x):
    return jnp.sum(x.astype(F32), axis=0, keepdims=True)


def head_lanes(h, rows, width):
    lane = lax.broadcasted_iota(jnp.int32, (rows, width), 1)
    size = width // HEADS
    return (lane >= h * size) & (lane < (h + 1) * size)


def window_start(i, tok):
    return jnp.clip((i - 1) * TILE, 0, tok - WINDOW)


def call(kernel, outs, ins, scratch, name, flops, spaces=None, vmem=12):
    spaces = spaces or [VMEM] * len(ins)
    nbytes = 0 * sum(a.size * a.dtype.itemsize for a in ins) + sum(
        a.size * a.dtype.itemsize for a in outs
    )
    return pl.pallas_call(
        kernel,
        out_shape=tuple(outs),
        in_specs=[pl.BlockSpec(memory_space=s) for s in spaces],
        out_specs=tuple(pl.BlockSpec(memory_space=VMEM) for _ in outs),
        scratch_shapes=scratch,
        compiler_params=pltpu.CompilerParams(vmem_limit_bytes=vmem << 20),
        cost_estimate=pl.CostEstimate(flops=flops, bytes_accessed=nbytes, transcendentals=0),
        name=name,
    )(*ins)


def shape(dims, kind):
    return jax.ShapeDtypeStruct(dims, kind)


def load_pieces(refs, offsets, dst):
    for ref, offs in zip(refs, offsets):
        if len(ref.shape) == 2:
            dst[pl.ds(offs[0], ref.shape[0]), :] = ref[...]
        else:
            for i, off in enumerate(offs):
                dst[pl.ds(off, ref.shape[1]), :] = ref[i]


def place_offsets(place, piece, planes):
    offsets = []
    for other in (0, 1):
        for slot in range(4):
            core = place[3] ^ other if other else place[3]
            inner = 2 * (place[1] ^ slot) + core
            offsets.append(
                [pl.multiple_of((8 * plane + inner) * piece, 16) for plane in range(planes)]
            )
    return offsets


def prepare_kernel(lens, crops, feat, vec, pos, seg_col, seg_row, feat_near, vec_near):
    feat_near[...] = feat[...]
    vec_near[...] = vec[...]
    tok, width = pos.shape
    half = width // 2
    first = lens[0, 0]
    lane = lax.broadcasted_iota(jnp.int32, (TILE, half), 1)
    frequency = jnp.exp(lane.astype(F32) * (-math.log(10000.0) / half))
    at = lax.broadcasted_iota(jnp.int32, (tok // TILE, TILE), 0) * TILE
    at = at + lax.broadcasted_iota(jnp.int32, (tok // TILE, TILE), 1)
    seg_row[...] = (2 * crops[...] + (at >= first).astype(jnp.int32)).astype(F32)
    for i in range(tok // TILE):
        r = slice(i * TILE, (i + 1) * TILE)
        row = lax.broadcasted_iota(jnp.int32, (TILE, half), 0) + i * TILE
        angle = (row - jnp.where(row >= first, first, 0)).astype(F32) * frequency
        pos[r, 0:half] = jnp.sin(angle)
        pos[r, half:width] = jnp.cos(angle)
        seg_col[r, :] = jnp.broadcast_to(seg_row[i : i + 1, :], (TILE, TILE)).T


def prepare(lens, crops, feat, vec):
    tok, width = crops.shape[0], vec.shape[1]
    crops = crops.reshape(-1, TILE)
    return call(
        prepare_kernel,
        [
            shape((tok, width), F32),
            shape((tok, TILE), F32),
            shape(crops.shape, F32),
            shape(feat.shape, BF16),
            shape(vec.shape, F32),
        ],
        [lens, crops, feat, vec],
        [],
        "positions_segments",
        1_000_000,
        [pltpu.SMEM, VMEM, VMEM, VMEM],
    )


def attention_kernel(flat, piece, place, feat, pos, seg_col, seg_row, vec, *rest):
    count = 1 if flat else 8
    pieces, rest = rest[:count], rest[count:]
    w, emb, src, q, k, v, attn_t, p, scale_inv, v_t, q_t = rest
    tok, width = emb.shape
    feat_dim = feat.shape[1]
    size = width // HEADS
    scale = size ** (-0.5)
    offsets = [[0]] if flat else place_offsets(place, piece, 1)
    load_pieces(pieces, offsets, w)
    for i in range(tok // ROWS):
        r = pl.ds(i * ROWS, ROWS)
        e = nn(feat[r, :], w[0:feat_dim, :]) + vec[0:1, :]
        emb[r, :] = e
        s = (e + pos[r, :]).astype(BF16)
        src[r, :] = s
        low = e.astype(BF16)
        at = feat_dim
        q[r, :] = (nn(s, w[at : at + width, :]) + vec[1:2, :]).astype(BF16)
        k[r, :] = nn(s, w[at + width : at + 2 * width, :]).astype(BF16)
        v[r, :] = (nn(low, w[at + 2 * width : at + 3 * width, :]) + vec[2:3, :]).astype(BF16)
    pad = v_t.shape[0] // HEADS
    vals = v[...].T
    for h in range(HEADS):
        v_t[h * pad : h * pad + size, :] = vals[h * size : (h + 1) * size, :]
        v_t[h * pad + size : (h + 1) * pad, :] = jnp.ones((pad - size, tok), BF16)
    q_t[...] = jnp.zeros_like(q_t)
    masked = MASKED / scale
    factor = scale * LOG2_E

    def tile(i, carry):
        rows = pl.ds(pl.multiple_of(i * TILE, TILE), TILE)
        win = pl.ds(pl.multiple_of(window_start(i, tok), TILE), WINDOW)
        own_t = q[rows, :].T
        keys = k[win, :]
        vals_t = v_t[:, win]
        allowed = seg_col[win, :] == seg_row[pl.ds(i, 1), :]
        for h in range(HEADS):
            d = slice(h * size, (h + 1) * size)
            q_t[d, h * TILE : (h + 1) * TILE] = own_t[d, :]
        for g in range(HEADS // 8):
            both = nn(keys, q_t[:, 8 * g * TILE : (8 * g + 8) * TILE])
            for u in range(8):
                h = 8 * g + u
                s = jnp.where(allowed, both[:, u * TILE : (u + 1) * TILE], masked)
                top = jnp.max(s, axis=0, keepdims=True)
                e = jnp.exp2((s - top) * factor).astype(BF16)
                p[i, :, h * TILE : (h + 1) * TILE] = e
        for g in range(HEADS // 2):
            o = nn(
                vals_t[2 * g * pad : (2 * g + 2) * pad, :],
                p[i, :, 2 * g * TILE : (2 * g + 2) * TILE],
            )
            for u in range(2):
                h = 2 * g + u
                own = o[u * pad : (u + 1) * pad, u * TILE : (u + 1) * TILE]
                inv = 1.0 / own[size : size + 1, :]
                scale_inv[i, h : h + 1, :] = inv
                attn_t[h * size : (h + 1) * size, rows] = (own[0:size, :] * inv).astype(BF16)
        return carry

    lax.fori_loop(0, tok // TILE, tile, 0, unroll=8)


def attention(flat, place, feat, pos, segment, vec, pieces, attn_rows):
    tok, width = feat.shape[0], vec.shape[1]
    piece = pieces[0].shape[0]
    low = shape((tok, width), BF16)
    outs = [
        shape((attn_rows, width), BF16),
        shape((tok, width), F32),
        low,
        low,
        low,
        low,
        shape((width, tok), BF16),
        shape((tok // TILE, WINDOW, HEADS * TILE), BF16),
        shape((tok // TILE, HEADS, TILE), F32),
    ]
    ins = [place, feat, pos, *segment, vec, *pieces]
    return call(
        functools.partial(attention_kernel, flat, piece),
        outs,
        ins,
        [
            VMEM((width + 16 * HEADS, tok), BF16),
            VMEM((width, HEADS * TILE), BF16),
        ],
        "attention_forward",
        1_200_000_000,
        [pltpu.SMEM] + [VMEM] * (5 + len(pieces)),
        vmem=20,
    )


def feed_kernel(flat, piece, place, emb, attn_t, cot, vec, wa, *rest):
    count = 1 if flat else 8
    pieces, rest = rest[:count], rest[count:]
    outs = 5 if flat else 6
    res, rest = rest[: outs + 1], rest[outs + 1 :]
    out, g_one, w_out, vec_grad, dwo = res[:5]
    (wf, wh, wh_t, wb_t, half_a, half_b, act, slope, n_t, b_t, out_all, acc, gff) = rest
    halves = (half_a, half_b)
    tok, width = emb.shape
    first = width // 2
    offsets = [[0]] if flat else place_offsets(place, piece, 3)
    load_pieces(pieces, offsets, wf)
    for u in range(2):
        halves[u][...] = wf[first : first + FF, u * 128 : (u + 1) * 128].astype(F32)
    w_out[0:first, :] = wa[wa.shape[0] - first :, :]
    w_out[first:, :] = wf[0:first, :]
    for j in range(BLOCKS):
        c = slice(j * BLOCK, (j + 1) * BLOCK)
        w = jnp.concatenate(
            [halves[u][pl.ds(j, width, stride=BLOCKS), :] for u in range(2)], axis=1
        ).astype(BF16)
        wh[:, c] = w
        wh_t[c, :] = w.T
        wb_t[:, c] = wf[first + FF + j * BLOCK : first + FF + (j + 1) * BLOCK, :].T
    acc[...] = jnp.zeros_like(acc)
    n_t[width : width + 8, :] = jnp.ones((8, tok), BF16)

    r = slice(0, tok)
    res_one = emb[r, :] + tn(attn_t[:, r], w_out[...]) + vec[3:4, :]
    cen = res_one - row_mean(res_one)
    inv_one = lax.rsqrt(row_mean(cen * cen) + EPS_NORM)
    hat_one = cen * inv_one
    normed = hat_one * vec[4:5, :] + vec[5:6, :]
    low = normed.astype(BF16)
    res_two = normed + vec[6:7, :]
    for j in range(BLOCKS):
        c = slice(j * BLOCK, (j + 1) * BLOCK)
        at = first + FF + j * BLOCK
        x = nn(low, wh[:, c]) + vec[9 + j : 10 + j, :]
        sq = x * x
        t = jnp.tanh((x * (GELU_A + (GELU_A * GELU_B) * sq)).astype(BF16))
        half = t * jnp.bfloat16(0.5) + jnp.bfloat16(0.5)
        act[r, c] = x.astype(BF16) * half
        bend = (x * ((2 * GELU_A) + (6 * GELU_A * GELU_B) * sq)).astype(BF16)
        slope[r, c] = half + (half - half * half) * bend
        res_two += nn(act[r, c], wf[at : at + BLOCK, :])
    cen = res_two - row_mean(res_two)
    inv_two = lax.rsqrt(row_mean(cen * cen) + EPS_NORM)
    hat_two = cen * inv_two
    out[r, :] = hat_two * vec[7:8, :] + vec[8:9, :]
    ct = cot[r, :].astype(F32)
    gs = ct * vec[7:8, :]
    g_two = inv_two * (gs - row_mean(gs) - hat_two * row_mean(gs * hat_two))
    back = g_two.astype(BF16)
    b_t[:, r] = back.T
    acc[0] += fold_rows(back.astype(F32))
    acc[1] += fold_rows(ct * hat_two)
    acc[2] += fold_rows(ct)
    n_t[0:width, r] = low.T
    g_norm = g_two
    for j in range(BLOCKS):
        c = slice(j * BLOCK, (j + 1) * BLOCK)
        part = (nn(back, wb_t[:, c]) * slope[r, c].astype(F32)).astype(BF16)
        g_norm += nn(part, wh_t[c, :])
        g = nn(n_t[...], part)
        for u in range(2):
            halves[u][pl.ds(j, width, stride=BLOCKS), :] = g[0:width, u * 128 : (u + 1) * 128]
        vec_grad[9 + j : 10 + j, :] = g[width : width + 1, :]
        at = first + FF + j * BLOCK
        gff[at : at + BLOCK, :] = nn(b_t[...], act[:, c]).T.astype(BF16)
    gs = g_norm * vec[4:5, :]
    g_res = inv_one * (gs - row_mean(gs) - hat_one * row_mean(gs * hat_one))
    g_one[r, :] = g_res
    out_low = g_res.astype(BF16)
    out_all[r, :] = out_low
    acc[3] += fold_rows(out_low.astype(F32))
    acc[4] += fold_rows(g_norm * hat_one)
    acc[5] += fold_rows(g_norm)

    for u in range(2):
        gff[first : first + FF, u * 128 : (u + 1) * 128] = halves[u][...].astype(BF16)
    g = nn(attn_t[...], out_all[...]).astype(BF16)
    dwo[...] = g[0:first, :]
    gff[0:first, :] = g[first:, :]
    sums = jnp.sum(acc[...], axis=1)
    vec_grad[0:3, :] = jnp.zeros((3, width), F32)
    for row, at in ((3, 3), (4, 4), (5, 5), (6, 0), (7, 1), (8, 2)):
        vec_grad[row : row + 1, :] = sums[at : at + 1, :]
    if flat:
        res[5][...] = gff[...]
    else:
        split_cores(place, gff, res[5], res[6])


def split_cores(place, grads, keep, send):
    core = place[3]
    piece = keep.shape[1]
    for m in range(keep.shape[0]):
        keep[m] = grads[pl.ds(pl.multiple_of((2 * m + core) * piece, 16), piece), :]
        send[m] = grads[pl.ds(pl.multiple_of((2 * m + 1 - core) * piece, 16), piece), :]


def feed(flat, place, emb, attn_t, cot, vec, wa, pieces, ff_rows):
    tok, width = emb.shape
    piece = pieces[0].shape[-2]
    outs = [
        shape((tok, width), F32),
        shape((tok, width), F32),
        shape((width, width), BF16),
        shape(vec.shape, F32),
        shape((width // 2, width), BF16),
    ]
    if flat:
        outs += [shape((ff_rows, width), BF16)]
    else:
        outs += [shape((ff_rows // piece // 2, piece, width), BF16)] * 2
    return call(
        functools.partial(feed_kernel, flat, piece),
        outs,
        [place, emb, attn_t, cot, vec, wa, *pieces],
        [
            VMEM((ff_rows, width), BF16),
            VMEM((width, FF), BF16),
            VMEM((FF, width), BF16),
            VMEM((width, FF), BF16),
            VMEM((FF, 128), F32),
            VMEM((FF, 128), F32),
            VMEM((tok, FF), BF16),
            VMEM((tok, FF), BF16),
            VMEM((width + 8, tok), BF16),
            VMEM((width, tok), BF16),
            VMEM((tok, width), BF16),
            VMEM((6, 8, width), F32),
            VMEM((ff_rows, width), BF16),
        ],
        "feed_forward_both",
        14_000_000_000,
        [pltpu.SMEM] + [VMEM] * (5 + len(pieces)),
        vmem=34,
    )


def attention_back(g_one, q, k, v, p, scale_inv, attn_t, w_out, ql, kl, vl, *scratch):
    ag, k_t, ds_all, a_t, scaled, qm, am, dk, dv = scratch
    tok, width = g_one.shape
    size = width // HEADS
    scale = size ** (-0.5)
    for i in range(tok // ROWS):
        r = pl.ds(i * ROWS, ROWS)
        ag[r, :] = nt(g_one[r, :].astype(BF16), w_out[...]).astype(BF16)
    k_t[...] = k[...].T
    dk[...] = jnp.zeros_like(dk)
    dv[...] = jnp.zeros_like(dv)
    a_t[...] = jnp.zeros_like(a_t)

    def tile(i, carry):
        rows = pl.ds(pl.multiple_of(i * TILE, TILE), TILE)
        win = pl.ds(pl.multiple_of(window_start(i, tok), TILE), WINDOW)
        own_q = q[rows, :]
        own_t = ag[rows, :].T
        vals = v[win, :]
        keys_t = k_t[:, win]
        inner = []
        for h in range(HEADS):
            d = slice(h * size, (h + 1) * size)
            grad = own_t[d, :].astype(F32) * scale_inv[i, h : h + 1, :]
            inner.append(jnp.sum(grad * attn_t[d, rows].astype(F32), axis=0, keepdims=True))
            a_t[d, h * TILE : (h + 1) * TILE] = grad.astype(BF16)
            scaled[d, :] = grad.astype(BF16)
        own_a = scaled[...].T
        for h in range(HEADS):
            lanes = head_lanes(h, TILE, width)
            c = slice(h * TILE, (h + 1) * TILE)
            qm[c, :] = jnp.where(lanes, own_q, jnp.zeros_like(own_q))
            am[c, :] = jnp.where(lanes, own_a, jnp.zeros_like(own_a))
        parts = []
        for g in range(HEADS // 8):
            both = nn(vals, a_t[:, 8 * g * TILE : (8 * g + 8) * TILE])
            for u in range(8):
                h = 8 * g + u
                c = slice(h * TILE, (h + 1) * TILE)
                dp = both[:, u * TILE : (u + 1) * TILE]
                ds = (p[i, :, c].astype(F32) * (dp - inner[h])).astype(BF16)
                ds_all[:, c] = ds
        for g in range(HEADS // 2):
            o = nn(
                keys_t[2 * g * size : (2 * g + 2) * size, :],
                ds_all[:, 2 * g * TILE : (2 * g + 2) * TILE],
            )
            parts += [o[0:size, 0:TILE], o[size : 2 * size, TILE : 2 * TILE]]
        ql[rows, :] = (jnp.concatenate(parts, axis=0).T * scale).astype(BF16)
        dk[win, :] += nn(ds_all[...], qm[...])
        dv[win, :] += nn(p[i], am[...])
        return carry

    lax.fori_loop(0, tok // TILE, tile, 0, unroll=8)
    kl[...] = (dk[...] * scale).astype(BF16)
    vl[...] = dv[...].astype(BF16)


def backward_kernel(flat, piece, place, g_one, q, k, v, p, scale_inv, attn_t, w_out, *rest):
    feat, emb, src, dwo, vg, wa, low_out, *outs = rest[:9]
    grads, ql, kl, vl, *scratch = rest[9:]
    attention_back(g_one, q, k, v, p, scale_inv, attn_t, w_out, ql, kl, vl, *scratch)
    tok, width = g_one.shape
    at = feat.shape[1]
    total = jnp.zeros((1, width), F32)
    for i in range(tok // ROWS):
        r = pl.ds(i * ROWS, ROWS)
        e = (
            g_one[r, :]
            + nt(ql[r, :], wa[at : at + width, :])
            + nt(kl[r, :], wa[at + width : at + 2 * width, :])
            + nt(vl[r, :], wa[at + 2 * width : at + 3 * width, :])
        )
        low = e.astype(BF16)
        low_out[r, :] = low
        total += column_sum(low)
    src_t = src[...].T
    grads[at : at + width, :] = nn(src_t, ql[...]).astype(BF16)
    grads[at + width : at + 2 * width, :] = nn(src_t, kl[...]).astype(BF16)
    grads[at + 2 * width : at + 3 * width, :] = nn(emb[...].astype(BF16).T, vl[...]).astype(BF16)
    grads[0:at, :] = nn(feat[...].T, low_out[...]).astype(BF16)
    grads[at + 3 * width :, :] = dwo[...]
    front = jnp.concatenate([total, column_sum(ql[...]), column_sum(vl[...])], axis=0)
    if flat:
        outs[0][...] = grads[...]
        outs[1][...] = vg[...]
        outs[1][0:3, :] = front
        return
    keep, send = outs
    core = place[3]
    for m in range(4):
        to = pl.ds(m * piece, piece)
        keep[to, :] = grads[pl.ds(pl.multiple_of((2 * m + core) * piece, 16), piece), :]
        send[to, :] = grads[pl.ds(pl.multiple_of((2 * m + 1 - core) * piece, 16), piece), :]
    rows = vg.shape[0]
    pad = jnp.zeros((VEC_PAD - rows, width), F32)
    tail = jnp.concatenate([front, vg[3:rows, :], pad], axis=0).astype(BF16)
    for ref in (keep, send):
        ref[4 * piece :, :] = tail


def backward(flat, place, g_one, q, k, v, p, scale_inv, attn_t, w_out, feat, emb, src, *rest):
    dwo, vg, wa, piece = rest
    tok, width = g_one.shape
    outs = [shape((tok, width), BF16)]
    if flat:
        outs += [shape(wa.shape, BF16), shape(vg.shape, F32)]
    else:
        outs += [shape((4 * piece + VEC_PAD, width), BF16)] * 2
    ins = [place, g_one, q, k, v, p, scale_inv, attn_t, w_out, feat, emb, src, dwo, vg, wa]
    low = VMEM((tok, width), BF16)
    return call(
        functools.partial(backward_kernel, flat, piece),
        outs,
        ins,
        [
            VMEM(wa.shape, BF16),
            low,
            low,
            low,
            low,
            VMEM((width, tok), BF16),
            VMEM((WINDOW, HEADS * TILE), BF16),
            VMEM((width, HEADS * TILE), BF16),
            VMEM((width, TILE), BF16),
            VMEM((HEADS * TILE, width), BF16),
            VMEM((HEADS * TILE, width), BF16),
            VMEM((tok, width), F32),
            VMEM((tok, width), F32),
        ],
        "attention_backward",
        16_000_000_000,
        [pltpu.SMEM] + [VMEM] * (len(ins) - 1),
        vmem=24,
    )


def feature_kernel(low, wa, out):
    for i in range(low.shape[0] // ROWS):
        r = pl.ds(i * ROWS, ROWS)
        out[r, :] = nt(low[r, :], wa[0 : out.shape[1], :])


def feature_back(low, wa, feat_dim):
    return call(
        feature_kernel,
        [shape((low.shape[0], feat_dim), F32)],
        [low, wa],
        [],
        "feature_gradient",
        300_000_000,
    )[0]


def plane_kernel(place, own, one, two, three, attn, rest):
    got = (own, one, two, three)
    z = place[0]
    for slot in range(4):

        @pl.when(z == slot)
        def _(slot=slot):
            attn[...] = got[slot][...]
            for plane in range(1, 4):
                rest[plane - 1] = got[slot ^ plane][...]


def pick_planes(place, own, one, two, three):
    return call(
        plane_kernel,
        [shape(own.shape, BF16), shape((3, *own.shape), BF16)],
        [place, own, one, two, three],
        [],
        "pick_planes",
        1_000_000,
        [pltpu.SMEM] + [VMEM] * 4,
    )


def ff_sum_kernel(place, keep, recv, *outs):
    yx = place[1]
    for slot in range(4):
        for plane in range(3):
            at = 4 * plane + (yx ^ slot)
            outs[slot][plane] = (keep[at].astype(F32) + recv[at].astype(F32)).astype(BF16)


def ff_sum(place, keep, recv):
    one = shape((3, *keep.shape[1:]), BF16)
    return call(
        ff_sum_kernel,
        [one] * 4,
        [place, keep, recv],
        [],
        "sum_cores_ff",
        1_000_000,
        [pltpu.SMEM] + [VMEM] * 2,
    )


def four_kernel(a, b, c, d, out):
    out[...] = (
        (a[...].astype(F32) + b[...].astype(F32)) + (c[...].astype(F32) + d[...].astype(F32))
    ).astype(BF16)


def four_sum(a, b, c, d):
    return call(four_kernel, [shape(a.shape, BF16)], [a, b, c, d], [], "sum_plane_ff", 1_000_000)[0]


def tail_sum_kernel(piece, place, keep, recv, *outs):
    yx = place[1]
    vec = keep[4 * piece :, :].astype(F32) + recv[4 * piece :, :].astype(F32)
    for slot in range(4):
        r = pl.ds(pl.multiple_of((yx ^ slot) * piece, 16), piece)
        outs[slot][0:piece, :] = (keep[r, :].astype(F32) + recv[r, :].astype(F32)).astype(BF16)
        outs[slot][piece:, :] = vec.astype(BF16)


def tail_sum(place, keep, recv, piece):
    return call(
        functools.partial(tail_sum_kernel, piece),
        [shape((piece + VEC_PAD, keep.shape[1]), BF16)] * 4,
        [place, keep, recv],
        [],
        "sum_cores_tail",
        1_000_000,
        [pltpu.SMEM] + [VMEM] * 2,
    )


def plane_sum_kernel(place, a, b, c, d, ff, *outs):
    z = place[0]
    total = (
        (a[...].astype(F32) + b[...].astype(F32)) + (c[...].astype(F32) + d[...].astype(F32))
    ).astype(BF16)
    piece = ff.shape[1]
    for slot in range(4):
        goal = z ^ slot
        outs[slot][piece:, :] = total[piece:, :]

        @pl.when(goal == 0)
        def _(slot=slot):
            outs[slot][0:piece, :] = total[0:piece, :]

        @pl.when(goal != 0)
        def _(slot=slot, goal=goal):
            outs[slot][0:piece, :] = ff[jnp.maximum(goal - 1, 0)]


def plane_sum(place, a, b, c, d, ff):
    return call(
        plane_sum_kernel,
        [shape(a.shape, BF16)] * 4,
        [place, a, b, c, d, ff],
        [],
        "sum_plane_tail",
        1_000_000,
        [pltpu.SMEM] + [VMEM] * 5,
    )


def adam_step(weight, moment_one, moment_two, gradient, step_rate, decay_rate):
    moment_one = BETA_ONE * moment_one + (1.0 - BETA_ONE) * gradient
    moment_two = BETA_TWO * moment_two + (1.0 - BETA_TWO) * gradient * gradient
    mean_hat = moment_one / (1.0 - BETA_ONE**STEP)
    square_hat = moment_two / (1.0 - BETA_TWO**STEP)
    weight = weight - step_rate * (
        mean_hat / (jnp.sqrt(square_hat) + ADAM_EPS) + decay_rate * weight
    )
    return (weight, moment_one, moment_two)


def adam_kernel(feat_dim, place, a, b, c, d, w, m, v, vw, vm, vv, *outs):
    total = (a[...].astype(F32) + b[...].astype(F32)) + (c[...].astype(F32) + d[...].astype(F32))
    piece = w.shape[0]
    rows = place[2] * piece + lax.broadcasted_iota(jnp.int32, w.shape, 0)
    rate = jnp.where(rows < feat_dim, 0.1 * RATE, RATE)
    new = adam_step(w[...], m[...], v[...], total[0:piece, :], rate, DECAY)
    for ref, value in zip(outs[:3], new):
        ref[...] = value
    outs[3][...] = new[0].astype(BF16)
    new = adam_step(vw[...], vm[...], vv[...], total[piece : piece + vw.shape[0], :], RATE, 0.0)
    for ref, value in zip(outs[4:], new):
        ref[...] = value


def adam(place, parts, mats, mats_m, mats_v, vecs, vecs_m, vecs_v, feat_dim):
    mat, vec = shape(mats.shape, F32), shape(vecs.shape, F32)
    return call(
        functools.partial(adam_kernel, feat_dim),
        [mat, mat, mat, shape(mats.shape, BF16), vec, vec, vec],
        [place, *parts, mats, mats_m, mats_v, vecs, vecs_m, vecs_v],
        [],
        "adam",
        10_000_000,
        [pltpu.SMEM] + [VMEM] * 10,
    )


def grid_swap(dz, dyx):
    return [(4 * z + yx, 4 * (z ^ dz) + (yx ^ dyx)) for z in range(4) for yx in range(4)]


PAIR_SWAP = [(0, 1), (1, 0)]


def per_device(
    flat,
    features,
    cotangent,
    canvas_lengths,
    crop_ids,
    mats,
    mats_m,
    mats_v,
    vecs,
    vecs_m,
    vecs_v,
):
    tok = features.shape[0]
    feat_dim = features.shape[1]
    width = vecs.shape[1]
    attn_rows = feat_dim + 3 * width + width // 2
    ff_rows = width // 2 + 2 * FF
    piece = mats.shape[0]
    dp, core = lax.axis_index("dp"), lax.axis_index("pair")
    device = lax.axis_index(("dp", "pair"))
    place = jnp.stack([dp // 4, dp % 4, device, core]).astype(jnp.int32)

    near = prepare(canvas_lengths, crop_ids, features, vecs)
    mats_low = mats.astype(BF16)
    if flat:
        gathered = lax.all_gather(mats_low, ("dp", "pair"), axis=0, tiled=True)
        attn_pieces = [gathered[:attn_rows]]
        ff_pieces = [gathered[attn_rows:]]
    else:
        planes = [lax.ppermute(mats_low, "dp", grid_swap(dz, 0)) for dz in (1, 2, 3)]
        near, planes = lax.optimization_barrier((near, planes))
        one, three = pick_planes(place, mats_low, *planes)
        attn_pieces = [one] + [lax.ppermute(one, "dp", grid_swap(0, s)) for s in (1, 2, 3)]
        attn_pieces += [lax.ppermute(a, "pair", PAIR_SWAP) for a in attn_pieces]
        ff_pieces = [three] + [lax.ppermute(three, "dp", grid_swap(0, s)) for s in (1, 2, 3)]

    pos_table, seg_col, seg_row, features, vec = near
    wa, emb, src, q, k, v, attn_t, probs, scale_inv = attention(
        flat, place, features, pos_table, (seg_col, seg_row), vec, attn_pieces, attn_rows
    )
    if not flat:
        own_swap = lax.ppermute(ff_pieces[0], "pair", PAIR_SWAP)
        attn_t, *moved = lax.optimization_barrier((attn_t, *ff_pieces[1:]))
        moved_swap = [lax.ppermute(a, "pair", PAIR_SWAP) for a in moved]
        ff_pieces = [ff_pieces[0], *moved, own_swap, *moved_swap]
    output, g_one, w_out, vg, dwo, *ff_grads = feed(
        flat, place, emb, attn_t, cotangent, vec, wa, ff_pieces, ff_rows
    )
    if not flat:
        keep, send = ff_grads
        sums = ff_sum(place, keep, lax.ppermute(send, "pair", PAIR_SWAP))
        g_one, *sums = lax.optimization_barrier((g_one, *sums))
        ff_parts = [sums[0]] + [lax.ppermute(sums[s], "dp", grid_swap(0, s)) for s in (1, 2, 3)]
    low, *tail = backward(
        flat,
        place,
        g_one,
        q,
        k,
        v,
        probs,
        scale_inv,
        attn_t,
        w_out,
        features,
        emb,
        src,
        dwo,
        vg,
        wa,
        piece,
    )
    feature_grad = feature_back(low, wa, feat_dim)
    if flat:
        grads = jnp.concatenate([tail[0], ff_grads[0]], axis=0).astype(F32)
        total = lax.psum_scatter(grads, ("dp", "pair"), scatter_dimension=0, tiled=True)
        vec_total = lax.psum(tail[1], ("dp", "pair"))
        row_ids = device * piece + jnp.arange(piece, dtype=jnp.int32)
        rate = jnp.where(row_ids < feat_dim, 0.1 * RATE, RATE)[:, None]
        new = adam_step(mats, mats_m, mats_v, total, rate, DECAY)
        new_vec = adam_step(vecs, vecs_m, vecs_v, vec_total, RATE, 0.0)
        return (output, feature_grad, *new, new[0].astype(BF16), *new_vec)
    keep, send, *ff_parts = lax.optimization_barrier((*tail, *ff_parts))
    ff = four_sum(*ff_parts)
    sums = tail_sum(place, keep, lax.ppermute(send, "pair", PAIR_SWAP), piece)
    parts = [sums[0]] + [lax.ppermute(sums[s], "dp", grid_swap(0, s)) for s in (1, 2, 3)]
    sums = plane_sum(place, *parts, ff)
    parts = [sums[0]] + [lax.ppermute(sums[s], "dp", grid_swap(s, 0)) for s in (1, 2, 3)]
    new = adam(place, parts, mats, mats_m, mats_v, vecs, vecs_m, vecs_v, feat_dim)
    return (output, feature_grad, *new)


def solution(mesh):
    rows = P(("dp", "pair"), None)
    in_specs = (rows, rows, rows, P(("dp", "pair")), rows, rows, rows, P(), P(), P())
    out_specs = (rows, rows, rows, rows, rows, rows, P(), P(), P())
    flat = mesh.shape["dp"] != 16 or mesh.shape["pair"] != 2
    return jax.shard_map(
        functools.partial(per_device, flat),
        mesh=mesh,
        in_specs=in_specs,
        out_specs=out_specs,
        check_vma=False,
    )
```

```python
import functools
import math

import jax
import jax.numpy as jnp
from jax import lax
from jax.experimental import pallas as pl
from jax.experimental.pallas import tpu as pltpu
from jax.sharding import PartitionSpec as P

HEADS = 8
FF = 2048
STEP = 10

EPS_NORM = 1e-05
RATE = 0.2
BETA_ONE = 0.9
BETA_TWO = 0.999
ADAM_EPS = 1e-08
DECAY = 0.0001
MASKED = -1000000000.0

TILE = 128
WINDOW = 384
ROWS = 512
FEED_ROWS = 1024
BLOCK = 256
BLOCKS = FF // BLOCK
GELU_A = 0.7978845608028654
GELU_B = 0.044715
LOG2_E = 1.4426950408889634
VEC_PAD = 32

F32 = jnp.float32
BF16 = jnp.bfloat16
VMEM = pltpu.VMEM


def nn(a, b):
    return lax.dot_general(a, b, (((1,), (0,)), ((), ())), preferred_element_type=F32)


def nt(a, b):
    return lax.dot_general(a, b, (((1,), (1,)), ((), ())), preferred_element_type=F32)


def tn(a, b):
    return lax.dot_general(a, b, (((0,), (0,)), ((), ())), preferred_element_type=F32)


def row_mean(x):
    return jnp.sum(x, axis=1, keepdims=True) * (1.0 / x.shape[1])


def fold_rows(x):
    return jnp.sum(x.reshape(x.shape[0] // 8, 8, x.shape[1]), axis=0)


def column_sum(x):
    return jnp.sum(x.astype(F32), axis=0, keepdims=True)


def head_lanes(h, rows, width):
    lane = lax.broadcasted_iota(jnp.int32, (rows, width), 1)
    size = width // HEADS
    return (lane >= h * size) & (lane < (h + 1) * size)


def window_start(i, tok):
    return jnp.clip((i - 1) * TILE, 0, tok - WINDOW)


def call(kernel, outs, ins, scratch, name, flops, spaces=None, vmem=12):
    spaces = spaces or [VMEM] * len(ins)
    nbytes = 0 * sum(a.size * a.dtype.itemsize for a in ins) + sum(
        a.size * a.dtype.itemsize for a in outs
    )
    return pl.pallas_call(
        kernel,
        out_shape=tuple(outs),
        in_specs=[pl.BlockSpec(memory_space=s) for s in spaces],
        out_specs=tuple(pl.BlockSpec(memory_space=VMEM) for _ in outs),
        scratch_shapes=scratch,
        compiler_params=pltpu.CompilerParams(vmem_limit_bytes=vmem << 20),
        cost_estimate=pl.CostEstimate(flops=flops, bytes_accessed=nbytes, transcendentals=0),
        name=name,
    )(*ins)


def shape(dims, kind):
    return jax.ShapeDtypeStruct(dims, kind)


def load_pieces(refs, offsets, dst):
    for ref, offs in zip(refs, offsets):
        if len(ref.shape) == 2:
            dst[pl.ds(offs[0], ref.shape[0]), :] = ref[...]
        else:
            for i, off in enumerate(offs):
                dst[pl.ds(off, ref.shape[1]), :] = ref[i]


def place_offsets(place, piece, planes):
    offsets = []
    for other in (0, 1):
        for slot in range(4):
            core = place[3] ^ other if other else place[3]
            inner = 2 * (place[1] ^ slot) + core
            offsets.append(
                [pl.multiple_of((8 * plane + inner) * piece, 16) for plane in range(planes)]
            )
    return offsets


def prepare_kernel(lens, crops, feat, vec, pos, seg_col, seg_row, feat_near, vec_near):
    feat_near[...] = feat[...]
    vec_near[...] = vec[...]
    tok, width = pos.shape
    half = width // 2
    first = lens[0, 0]
    lane = lax.broadcasted_iota(jnp.int32, (TILE, half), 1)
    frequency = jnp.exp(lane.astype(F32) * (-math.log(10000.0) / half))
    at = lax.broadcasted_iota(jnp.int32, (tok // TILE, TILE), 0) * TILE
    at = at + lax.broadcasted_iota(jnp.int32, (tok // TILE, TILE), 1)
    seg_row[...] = (2 * crops[...] + (at >= first).astype(jnp.int32)).astype(F32)
    for i in range(tok // TILE):
        r = slice(i * TILE, (i + 1) * TILE)
        row = lax.broadcasted_iota(jnp.int32, (TILE, half), 0) + i * TILE
        angle = (row - jnp.where(row >= first, first, 0)).astype(F32) * frequency
        pos[r, 0:half] = jnp.sin(angle)
        pos[r, half:width] = jnp.cos(angle)
        seg_col[r, :] = jnp.broadcast_to(seg_row[i : i + 1, :], (TILE, TILE)).T


def prepare(lens, crops, feat, vec):
    tok, width = crops.shape[0], vec.shape[1]
    crops = crops.reshape(-1, TILE)
    return call(
        prepare_kernel,
        [
            shape((tok, width), F32),
            shape((tok, TILE), F32),
            shape(crops.shape, F32),
            shape(feat.shape, BF16),
            shape(vec.shape, F32),
        ],
        [lens, crops, feat, vec],
        [],
        "positions_segments",
        1_000_000,
        [pltpu.SMEM, VMEM, VMEM, VMEM],
    )


def attention_kernel(flat, piece, place, feat, pos, seg_col, seg_row, vec, *rest):
    count = 1 if flat else 8
    pieces, rest = rest[:count], rest[count:]
    w, emb, src, q, k, v, attn_t, p, scale_inv, v_t, q_t = rest
    tok, width = emb.shape
    feat_dim = feat.shape[1]
    size = width // HEADS
    scale = size ** (-0.5)
    offsets = [[0]] if flat else place_offsets(place, piece, 1)
    load_pieces(pieces, offsets, w)
    for i in range(tok // ROWS):
        r = pl.ds(i * ROWS, ROWS)
        e = nn(feat[r, :], w[0:feat_dim, :]) + vec[0:1, :]
        emb[r, :] = e
        s = (e + pos[r, :]).astype(BF16)
        src[r, :] = s
        low = e.astype(BF16)
        at = feat_dim
        q[r, :] = (nn(s, w[at : at + width, :]) + vec[1:2, :]).astype(BF16)
        k[r, :] = nn(s, w[at + width : at + 2 * width, :]).astype(BF16)
        v[r, :] = (nn(low, w[at + 2 * width : at + 3 * width, :]) + vec[2:3, :]).astype(BF16)
    pad = v_t.shape[0] // HEADS
    vals = v[...].T
    for h in range(HEADS):
        v_t[h * pad : h * pad + size, :] = vals[h * size : (h + 1) * size, :]
        v_t[h * pad + size : (h + 1) * pad, :] = jnp.ones((pad - size, tok), BF16)
    q_t[...] = jnp.zeros_like(q_t)
    masked = MASKED / scale
    factor = scale * LOG2_E

    def tile(i, carry):
        rows = pl.ds(pl.multiple_of(i * TILE, TILE), TILE)
        win = pl.ds(pl.multiple_of(window_start(i, tok), TILE), WINDOW)
        own_t = q[rows, :].T
        keys = k[win, :]
        vals_t = v_t[:, win]
        allowed = seg_col[win, :] == seg_row[pl.ds(i, 1), :]
        for h in range(HEADS):
            d = slice(h * size, (h + 1) * size)
            q_t[d, h * TILE : (h + 1) * TILE] = own_t[d, :]
        for g in range(HEADS // 8):
            both = nn(keys, q_t[:, 8 * g * TILE : (8 * g + 8) * TILE])
            for u in range(8):
                h = 8 * g + u
                s = jnp.where(allowed, both[:, u * TILE : (u + 1) * TILE], masked)
                top = jnp.max(s, axis=0, keepdims=True)
                e = jnp.exp2((s - top) * factor).astype(BF16)
                p[i, :, h * TILE : (h + 1) * TILE] = e
        for g in range(HEADS // 2):
            o = nn(
                vals_t[2 * g * pad : (2 * g + 2) * pad, :],
                p[i, :, 2 * g * TILE : (2 * g + 2) * TILE],
            )
            for u in range(2):
                h = 2 * g + u
                own = o[u * pad : (u + 1) * pad, u * TILE : (u + 1) * TILE]
                inv = 1.0 / own[size : size + 1, :]
                scale_inv[i, h : h + 1, :] = inv
                attn_t[h * size : (h + 1) * size, rows] = (own[0:size, :] * inv).astype(BF16)
        return carry

    lax.fori_loop(0, tok // TILE, tile, 0, unroll=8)


def attention(flat, place, feat, pos, segment, vec, pieces, attn_rows):
    tok, width = feat.shape[0], vec.shape[1]
    piece = pieces[0].shape[0]
    low = shape((tok, width), BF16)
    outs = [
        shape((attn_rows, width), BF16),
        shape((tok, width), F32),
        low,
        low,
        low,
        low,
        shape((width, tok), BF16),
        shape((tok // TILE, WINDOW, HEADS * TILE), BF16),
        shape((tok // TILE, HEADS, TILE), F32),
    ]
    ins = [place, feat, pos, *segment, vec, *pieces]
    return call(
        functools.partial(attention_kernel, flat, piece),
        outs,
        ins,
        [
            VMEM((width + 16 * HEADS, tok), BF16),
            VMEM((width, HEADS * TILE), BF16),
        ],
        "attention_forward",
        1_200_000_000,
        [pltpu.SMEM] + [VMEM] * (5 + len(pieces)),
        vmem=20,
    )


def feed_kernel(flat, piece, place, emb, attn_t, cot, vec, wa, *rest):
    count = 1 if flat else 8
    pieces, rest = rest[:count], rest[count:]
    outs = 5 if flat else 6
    res, rest = rest[: outs + 1], rest[outs + 1 :]
    out, g_one, w_out, vec_grad, dwo = res[:5]
    (wf, wh, wh_t, wb_t, half_a, half_b, act, slope, n_t, b_t, out_all, acc, gff) = rest
    halves = (half_a, half_b)
    tok, width = emb.shape
    first = width // 2
    offsets = [[0]] if flat else place_offsets(place, piece, 3)
    load_pieces(pieces, offsets, wf)
    for u in range(2):
        halves[u][...] = wf[first : first + FF, u * 128 : (u + 1) * 128].astype(F32)
    w_out[0:first, :] = wa[wa.shape[0] - first :, :]
    w_out[first:, :] = wf[0:first, :]
    for j in range(BLOCKS):
        c = slice(j * BLOCK, (j + 1) * BLOCK)
        w = jnp.concatenate(
            [halves[u][pl.ds(j, width, stride=BLOCKS), :] for u in range(2)], axis=1
        ).astype(BF16)
        wh[:, c] = w
        wh_t[c, :] = w.T
        wb_t[:, c] = wf[first + FF + j * BLOCK : first + FF + (j + 1) * BLOCK, :].T
    acc[...] = jnp.zeros_like(acc)
    n_t[width : width + 8, :] = jnp.ones((8, tok), BF16)

    r = slice(0, tok)
    res_one = emb[r, :] + tn(attn_t[:, r], w_out[...]) + vec[3:4, :]
    cen = res_one - row_mean(res_one)
    inv_one = lax.rsqrt(row_mean(cen * cen) + EPS_NORM)
    hat_one = cen * inv_one
    normed = hat_one * vec[4:5, :] + vec[5:6, :]
    low = normed.astype(BF16)
    res_two = normed + vec[6:7, :]
    for j in range(BLOCKS):
        c = slice(j * BLOCK, (j + 1) * BLOCK)
        at = first + FF + j * BLOCK
        x = nn(low, wh[:, c]) + vec[9 + j : 10 + j, :]
        sq = x * x
        t = jnp.tanh((x * (GELU_A + (GELU_A * GELU_B) * sq)).astype(BF16))
        half = t * jnp.bfloat16(0.5) + jnp.bfloat16(0.5)
        act[r, c] = x.astype(BF16) * half
        bend = (x * ((2 * GELU_A) + (6 * GELU_A * GELU_B) * sq)).astype(BF16)
        slope[r, c] = half + (half - half * half) * bend
        res_two += nn(act[r, c], wf[at : at + BLOCK, :])
    cen = res_two - row_mean(res_two)
    inv_two = lax.rsqrt(row_mean(cen * cen) + EPS_NORM)
    hat_two = cen * inv_two
    out[r, :] = hat_two * vec[7:8, :] + vec[8:9, :]
    ct = cot[r, :].astype(F32)
    gs = ct * vec[7:8, :]
    g_two = inv_two * (gs - row_mean(gs) - hat_two * row_mean(gs * hat_two))
    back = g_two.astype(BF16)
    b_t[:, r] = back.T
    acc[0] += fold_rows(back.astype(F32))
    acc[1] += fold_rows(ct * hat_two)
    acc[2] += fold_rows(ct)
    n_t[0:width, r] = low.T
    g_norm = g_two
    for j in range(BLOCKS):
        c = slice(j * BLOCK, (j + 1) * BLOCK)
        part = (nn(back, wb_t[:, c]) * slope[r, c].astype(F32)).astype(BF16)
        g_norm += nn(part, wh_t[c, :])
        g = nn(n_t[...], part)
        for u in range(2):
            halves[u][pl.ds(j, width, stride=BLOCKS), :] = g[0:width, u * 128 : (u + 1) * 128]
        vec_grad[9 + j : 10 + j, :] = g[width : width + 1, :]
        at = first + FF + j * BLOCK
        gff[at : at + BLOCK, :] = nn(b_t[...], act[:, c]).T.astype(BF16)
    gs = g_norm * vec[4:5, :]
    g_res = inv_one * (gs - row_mean(gs) - hat_one * row_mean(gs * hat_one))
    g_one[r, :] = g_res
    out_low = g_res.astype(BF16)
    out_all[r, :] = out_low
    acc[3] += fold_rows(out_low.astype(F32))
    acc[4] += fold_rows(g_norm * hat_one)
    acc[5] += fold_rows(g_norm)

    for u in range(2):
        gff[first : first + FF, u * 128 : (u + 1) * 128] = halves[u][...].astype(BF16)
    g = nn(attn_t[...], out_all[...]).astype(BF16)
    dwo[...] = g[0:first, :]
    gff[0:first, :] = g[first:, :]
    sums = jnp.sum(acc[...], axis=1)
    vec_grad[0:3, :] = jnp.zeros((3, width), F32)
    for row, at in ((3, 3), (4, 4), (5, 5), (6, 0), (7, 1), (8, 2)):
        vec_grad[row : row + 1, :] = sums[at : at + 1, :]
    if flat:
        res[5][...] = gff[...]
    else:
        split_cores(place, gff, res[5], res[6])


def split_cores(place, grads, keep, send):
    core = place[3]
    piece = keep.shape[1]
    for m in range(keep.shape[0]):
        keep[m] = grads[pl.ds(pl.multiple_of((2 * m + core) * piece, 16), piece), :]
        send[m] = grads[pl.ds(pl.multiple_of((2 * m + 1 - core) * piece, 16), piece), :]


def feed(flat, place, emb, attn_t, cot, vec, wa, pieces, ff_rows):
    tok, width = emb.shape
    piece = pieces[0].shape[-2]
    outs = [
        shape((tok, width), F32),
        shape((tok, width), F32),
        shape((width, width), BF16),
        shape(vec.shape, F32),
        shape((width // 2, width), BF16),
    ]
    if flat:
        outs += [shape((ff_rows, width), BF16)]
    else:
        outs += [shape((ff_rows // piece // 2, piece, width), BF16)] * 2
    return call(
        functools.partial(feed_kernel, flat, piece),
        outs,
        [place, emb, attn_t, cot, vec, wa, *pieces],
        [
            VMEM((ff_rows, width), BF16),
            VMEM((width, FF), BF16),
            VMEM((FF, width), BF16),
            VMEM((width, FF), BF16),
            VMEM((FF, 128), F32),
            VMEM((FF, 128), F32),
            VMEM((tok, FF), BF16),
            VMEM((tok, FF), BF16),
            VMEM((width + 8, tok), BF16),
            VMEM((width, tok), BF16),
            VMEM((tok, width), BF16),
            VMEM((6, 8, width), F32),
            VMEM((ff_rows, width), BF16),
        ],
        "feed_forward_both",
        14_000_000_000,
        [pltpu.SMEM] + [VMEM] * (5 + len(pieces)),
        vmem=34,
    )


def attention_back(g_one, q, k, v, p, scale_inv, attn_t, w_out, ql, kl, vl, *scratch):
    ag, k_t, ds_all, a_t, scaled, qm, am, dk, dv = scratch
    tok, width = g_one.shape
    size = width // HEADS
    scale = size ** (-0.5)
    for i in range(tok // ROWS):
        r = pl.ds(i * ROWS, ROWS)
        ag[r, :] = nt(g_one[r, :].astype(BF16), w_out[...]).astype(BF16)
    k_t[...] = k[...].T
    dk[...] = jnp.zeros_like(dk)
    dv[...] = jnp.zeros_like(dv)
    a_t[...] = jnp.zeros_like(a_t)

    def tile(i, carry):
        rows = pl.ds(pl.multiple_of(i * TILE, TILE), TILE)
        win = pl.ds(pl.multiple_of(window_start(i, tok), TILE), WINDOW)
        own_q = q[rows, :]
        own_t = ag[rows, :].T
        vals = v[win, :]
        keys_t = k_t[:, win]
        inner = []
        for h in range(HEADS):
            d = slice(h * size, (h + 1) * size)
            grad = own_t[d, :].astype(F32) * scale_inv[i, h : h + 1, :]
            inner.append(jnp.sum(grad * attn_t[d, rows].astype(F32), axis=0, keepdims=True))
            a_t[d, h * TILE : (h + 1) * TILE] = grad.astype(BF16)
            scaled[d, :] = grad.astype(BF16)
        own_a = scaled[...].T
        for h in range(HEADS):
            lanes = head_lanes(h, TILE, width)
            c = slice(h * TILE, (h + 1) * TILE)
            qm[c, :] = jnp.where(lanes, own_q, jnp.zeros_like(own_q))
            am[c, :] = jnp.where(lanes, own_a, jnp.zeros_like(own_a))
        parts = []
        for g in range(HEADS // 8):
            both = nn(vals, a_t[:, 8 * g * TILE : (8 * g + 8) * TILE])
            for u in range(8):
                h = 8 * g + u
                c = slice(h * TILE, (h + 1) * TILE)
                dp = both[:, u * TILE : (u + 1) * TILE]
                ds = (p[i, :, c].astype(F32) * (dp - inner[h])).astype(BF16)
                ds_all[:, c] = ds
        for g in range(HEADS // 2):
            o = nn(
                keys_t[2 * g * size : (2 * g + 2) * size, :],
                ds_all[:, 2 * g * TILE : (2 * g + 2) * TILE],
            )
            parts += [o[0:size, 0:TILE], o[size : 2 * size, TILE : 2 * TILE]]
        ql[rows, :] = (jnp.concatenate(parts, axis=0).T * scale).astype(BF16)
        dk[win, :] += nn(ds_all[...], qm[...])
        dv[win, :] += nn(p[i], am[...])
        return carry

    lax.fori_loop(0, tok // TILE, tile, 0, unroll=8)
    kl[...] = (dk[...] * scale).astype(BF16)
    vl[...] = dv[...].astype(BF16)


def backward_kernel(flat, piece, place, g_one, q, k, v, p, scale_inv, attn_t, w_out, *rest):
    count = 9 if flat else 10
    feat, emb, src, dwo, vg, wa, low_out, *outs = rest[:count]
    grads, ql, kl, vl, *scratch = rest[count:]
    attention_back(g_one, q, k, v, p, scale_inv, attn_t, w_out, ql, kl, vl, *scratch)
    tok, width = g_one.shape
    at = feat.shape[1]
    total = jnp.zeros((1, width), F32)
    for i in range(tok // ROWS):
        r = pl.ds(i * ROWS, ROWS)
        e = (
            g_one[r, :]
            + nt(ql[r, :], wa[at : at + width, :])
            + nt(kl[r, :], wa[at + width : at + 2 * width, :])
            + nt(vl[r, :], wa[at + 2 * width : at + 3 * width, :])
        )
        low = e.astype(BF16)
        low_out[r, :] = low
        total += column_sum(low)
    src_t = src[...].T
    grads[at : at + width, :] = nn(src_t, ql[...]).astype(BF16)
    grads[at + width : at + 2 * width, :] = nn(src_t, kl[...]).astype(BF16)
    grads[at + 2 * width : at + 3 * width, :] = nn(emb[...].astype(BF16).T, vl[...]).astype(BF16)
    grads[0:at, :] = nn(feat[...].T, low_out[...]).astype(BF16)
    grads[at + 3 * width :, :] = dwo[...]
    front = jnp.concatenate([total, column_sum(ql[...]), column_sum(vl[...])], axis=0)
    if flat:
        outs[0][...] = grads[...]
        outs[1][...] = vg[...]
        outs[1][0:3, :] = front
        return
    keep, send_one, send_two = outs
    core = place[3]
    for m in range(4):
        send = (send_one, send_two)[m // 2]
        to = pl.ds((m % 2) * piece, piece)
        keep[pl.ds(m * piece, piece), :] = grads[
            pl.ds(pl.multiple_of((2 * m + core) * piece, 16), piece), :
        ]
        send[to, :] = grads[pl.ds(pl.multiple_of((2 * m + 1 - core) * piece, 16), piece), :]
    rows = vg.shape[0]
    pad = jnp.zeros((VEC_PAD - rows, width), F32)
    tail = jnp.concatenate([front, vg[3:rows, :], pad], axis=0).astype(BF16)
    keep[4 * piece :, :] = tail
    send_two[2 * piece :, :] = tail


def backward(flat, place, g_one, q, k, v, p, scale_inv, attn_t, w_out, feat, emb, src, *rest):
    dwo, vg, wa, piece = rest
    tok, width = g_one.shape
    outs = [shape((tok, width), BF16)]
    if flat:
        outs += [shape(wa.shape, BF16), shape(vg.shape, F32)]
    else:
        outs += [shape((4 * piece + VEC_PAD, width), BF16)]
        outs += [shape((2 * piece, width), BF16), shape((2 * piece + VEC_PAD, width), BF16)]
    ins = [place, g_one, q, k, v, p, scale_inv, attn_t, w_out, feat, emb, src, dwo, vg, wa]
    low = VMEM((tok, width), BF16)
    return call(
        functools.partial(backward_kernel, flat, piece),
        outs,
        ins,
        [
            VMEM(wa.shape, BF16),
            low,
            low,
            low,
            low,
            VMEM((width, tok), BF16),
            VMEM((WINDOW, HEADS * TILE), BF16),
            VMEM((width, HEADS * TILE), BF16),
            VMEM((width, TILE), BF16),
            VMEM((HEADS * TILE, width), BF16),
            VMEM((HEADS * TILE, width), BF16),
            VMEM((tok, width), F32),
            VMEM((tok, width), F32),
        ],
        "attention_backward",
        16_000_000_000,
        [pltpu.SMEM] + [VMEM] * (len(ins) - 1),
        vmem=24,
    )


def feature_kernel(low, wa, out):
    for i in range(low.shape[0] // ROWS):
        r = pl.ds(i * ROWS, ROWS)
        out[r, :] = nt(low[r, :], wa[0 : out.shape[1], :])


def feature_back(low, wa, feat_dim):
    return call(
        feature_kernel,
        [shape((low.shape[0], feat_dim), F32)],
        [low, wa],
        [],
        "feature_gradient",
        300_000_000,
    )[0]


def plane_kernel(place, own, one, two, three, attn, rest):
    got = (own, one, two, three)
    z = place[0]
    for slot in range(4):

        @pl.when(z == slot)
        def _(slot=slot):
            attn[...] = got[slot][...]
            for plane in range(1, 4):
                rest[plane - 1] = got[slot ^ plane][...]


def pick_planes(place, own, one, two, three):
    return call(
        plane_kernel,
        [shape(own.shape, BF16), shape((3, *own.shape), BF16)],
        [place, own, one, two, three],
        [],
        "pick_planes",
        1_000_000,
        [pltpu.SMEM] + [VMEM] * 4,
    )


def ff_sum_kernel(place, keep, recv, *outs):
    yx = place[1]
    for slot in range(4):
        for plane in range(3):
            at = 4 * plane + (yx ^ slot)
            outs[slot][plane] = (keep[at].astype(F32) + recv[at].astype(F32)).astype(BF16)


def ff_sum(place, keep, recv):
    one = shape((3, *keep.shape[1:]), BF16)
    return call(
        ff_sum_kernel,
        [one] * 4,
        [place, keep, recv],
        [],
        "sum_cores_ff",
        1_000_000,
        [pltpu.SMEM] + [VMEM] * 2,
    )


def four_kernel(a, b, c, d, out):
    out[...] = (
        (a[...].astype(F32) + b[...].astype(F32)) + (c[...].astype(F32) + d[...].astype(F32))
    ).astype(BF16)


def four_sum(a, b, c, d):
    return call(four_kernel, [shape(a.shape, BF16)], [a, b, c, d], [], "sum_plane_ff", 1_000_000)[0]


def tail_sum_kernel(piece, place, keep, one, two, *outs):
    vec = keep[4 * piece :, :].astype(F32) + two[2 * piece :, :].astype(F32)
    for slot in range(4):
        m = place[1] ^ slot
        own = keep[pl.ds(pl.multiple_of(m * piece, 16), piece), :].astype(F32)
        at = pl.ds(pl.multiple_of((m & 1) * piece, 16), piece)
        outs[slot][piece:, :] = vec.astype(BF16)
        for half, recv in enumerate((one, two)):

            @pl.when((m >> 1) == half)
            def _(slot=slot, own=own, at=at, recv=recv):
                outs[slot][0:piece, :] = (own + recv[at, :].astype(F32)).astype(BF16)


def tail_sum(place, keep, one, two, piece):
    return call(
        functools.partial(tail_sum_kernel, piece),
        [shape((piece + VEC_PAD, keep.shape[1]), BF16)] * 4,
        [place, keep, one, two],
        [],
        "sum_cores_tail",
        1_000_000,
        [pltpu.SMEM] + [VMEM] * 3,
    )


def plane_sum_kernel(place, a, b, c, d, ff, *outs):
    z = place[0]
    total = (
        (a[...].astype(F32) + b[...].astype(F32)) + (c[...].astype(F32) + d[...].astype(F32))
    ).astype(BF16)
    piece = ff.shape[1]
    for slot in range(4):
        goal = z ^ slot
        outs[slot][piece:, :] = total[piece:, :]

        @pl.when(goal == 0)
        def _(slot=slot):
            outs[slot][0:piece, :] = total[0:piece, :]

        @pl.when(goal != 0)
        def _(slot=slot, goal=goal):
            outs[slot][0:piece, :] = ff[jnp.maximum(goal - 1, 0)]


def plane_sum(place, a, b, c, d, ff):
    return call(
        plane_sum_kernel,
        [shape(a.shape, BF16)] * 4,
        [place, a, b, c, d, ff],
        [],
        "sum_plane_tail",
        1_000_000,
        [pltpu.SMEM] + [VMEM] * 5,
    )


def adam_step(weight, moment_one, moment_two, gradient, step_rate, decay_rate):
    moment_one = BETA_ONE * moment_one + (1.0 - BETA_ONE) * gradient
    moment_two = BETA_TWO * moment_two + (1.0 - BETA_TWO) * gradient * gradient
    mean_hat = moment_one / (1.0 - BETA_ONE**STEP)
    square_hat = moment_two / (1.0 - BETA_TWO**STEP)
    weight = weight - step_rate * (
        mean_hat / (jnp.sqrt(square_hat) + ADAM_EPS) + decay_rate * weight
    )
    return (weight, moment_one, moment_two)


def adam_kernel(feat_dim, place, a, b, c, d, w, m, v, vw, vm, vv, *outs):
    total = (a[...].astype(F32) + b[...].astype(F32)) + (c[...].astype(F32) + d[...].astype(F32))
    piece = w.shape[0]
    rows = place[2] * piece + lax.broadcasted_iota(jnp.int32, w.shape, 0)
    rate = jnp.where(rows < feat_dim, 0.1 * RATE, RATE)
    new = adam_step(w[...], m[...], v[...], total[0:piece, :], rate, DECAY)
    for ref, value in zip(outs[:3], new):
        ref[...] = value
    outs[3][...] = new[0].astype(BF16)
    new = adam_step(vw[...], vm[...], vv[...], total[piece : piece + vw.shape[0], :], RATE, 0.0)
    for ref, value in zip(outs[4:], new):
        ref[...] = value


def adam(place, parts, mats, mats_m, mats_v, vecs, vecs_m, vecs_v, feat_dim):
    mat, vec = shape(mats.shape, F32), shape(vecs.shape, F32)
    return call(
        functools.partial(adam_kernel, feat_dim),
        [mat, mat, mat, shape(mats.shape, BF16), vec, vec, vec],
        [place, *parts, mats, mats_m, mats_v, vecs, vecs_m, vecs_v],
        [],
        "adam",
        10_000_000,
        [pltpu.SMEM] + [VMEM] * 10,
    )


def grid_swap(dz, dyx):
    return [(4 * z + yx, 4 * (z ^ dz) + (yx ^ dyx)) for z in range(4) for yx in range(4)]


PAIR_SWAP = [(0, 1), (1, 0)]


def per_device(
    flat,
    features,
    cotangent,
    canvas_lengths,
    crop_ids,
    mats,
    mats_m,
    mats_v,
    vecs,
    vecs_m,
    vecs_v,
):
    tok = features.shape[0]
    feat_dim = features.shape[1]
    width = vecs.shape[1]
    attn_rows = feat_dim + 3 * width + width // 2
    ff_rows = width // 2 + 2 * FF
    piece = mats.shape[0]
    dp, core = lax.axis_index("dp"), lax.axis_index("pair")
    device = lax.axis_index(("dp", "pair"))
    place = jnp.stack([dp // 4, dp % 4, device, core]).astype(jnp.int32)

    near = prepare(canvas_lengths, crop_ids, features, vecs)
    mats_low = mats.astype(BF16)
    if flat:
        gathered = lax.all_gather(mats_low, ("dp", "pair"), axis=0, tiled=True)
        attn_pieces = [gathered[:attn_rows]]
        ff_pieces = [gathered[attn_rows:]]
    else:
        planes = [lax.ppermute(mats_low, "dp", grid_swap(dz, 0)) for dz in (1, 2, 3)]
        near, planes = lax.optimization_barrier((near, planes))
        one, three = pick_planes(place, mats_low, *planes)
        attn_pieces = [one] + [lax.ppermute(one, "dp", grid_swap(0, s)) for s in (1, 2, 3)]
        attn_pieces += [lax.ppermute(a, "pair", PAIR_SWAP) for a in attn_pieces]
        ff_pieces = [three] + [lax.ppermute(three, "dp", grid_swap(0, s)) for s in (1, 2, 3)]

    pos_table, seg_col, seg_row, features, vec = near
    wa, emb, src, q, k, v, attn_t, probs, scale_inv = attention(
        flat, place, features, pos_table, (seg_col, seg_row), vec, attn_pieces, attn_rows
    )
    if not flat:
        own_swap = lax.ppermute(ff_pieces[0], "pair", PAIR_SWAP)
        attn_t, *moved = lax.optimization_barrier((attn_t, *ff_pieces[1:]))
        moved_swap = [lax.ppermute(a, "pair", PAIR_SWAP) for a in moved]
        ff_pieces = [ff_pieces[0], *moved, own_swap, *moved_swap]
    output, g_one, w_out, vg, dwo, *ff_grads = feed(
        flat, place, emb, attn_t, cotangent, vec, wa, ff_pieces, ff_rows
    )
    if not flat:
        keep, send = ff_grads
        sums = ff_sum(place, keep, lax.ppermute(send, "pair", PAIR_SWAP))
        g_one, *sums = lax.optimization_barrier((g_one, *sums))
        ff_parts = [sums[0]] + [lax.ppermute(sums[s], "dp", grid_swap(0, s)) for s in (1, 2, 3)]
    low, *tail = backward(
        flat,
        place,
        g_one,
        q,
        k,
        v,
        probs,
        scale_inv,
        attn_t,
        w_out,
        features,
        emb,
        src,
        dwo,
        vg,
        wa,
        piece,
    )
    feature_grad = feature_back(low, wa, feat_dim)
    if flat:
        grads = jnp.concatenate([tail[0], ff_grads[0]], axis=0).astype(F32)
        total = lax.psum_scatter(grads, ("dp", "pair"), scatter_dimension=0, tiled=True)
        vec_total = lax.psum(tail[1], ("dp", "pair"))
        row_ids = device * piece + jnp.arange(piece, dtype=jnp.int32)
        rate = jnp.where(row_ids < feat_dim, 0.1 * RATE, RATE)[:, None]
        new = adam_step(mats, mats_m, mats_v, total, rate, DECAY)
        new_vec = adam_step(vecs, vecs_m, vecs_v, vec_total, RATE, 0.0)
        return (output, feature_grad, *new, new[0].astype(BF16), *new_vec)
    keep, *send = tail
    recv = [lax.ppermute(a, "pair", PAIR_SWAP) for a in send]
    sums = tail_sum(place, keep, *recv, piece)
    sums, ff_parts = lax.optimization_barrier((sums, ff_parts))
    ff = four_sum(*ff_parts)
    parts = [sums[0]] + [lax.ppermute(sums[s], "dp", grid_swap(0, s)) for s in (1, 2, 3)]
    sums = plane_sum(place, *parts, ff)
    parts = [sums[0]] + [lax.ppermute(sums[s], "dp", grid_swap(s, 0)) for s in (1, 2, 3)]
    new = adam(place, parts, mats, mats_m, mats_v, vecs, vecs_m, vecs_v, feat_dim)
    return (output, feature_grad, *new)


def solution(mesh):
    rows = P(("dp", "pair"), None)
    in_specs = (rows, rows, rows, P(("dp", "pair")), rows, rows, rows, P(), P(), P())
    out_specs = (rows, rows, rows, rows, rows, rows, P(), P(), P())
    flat = mesh.shape["dp"] != 16 or mesh.shape["pair"] != 2
    return jax.shard_map(
        functools.partial(per_device, flat),
        mesh=mesh,
        in_specs=in_specs,
        out_specs=out_specs,
        check_vma=False,
    )
```

```python
import functools
import math

import jax
import jax.numpy as jnp
from jax import lax
from jax.experimental import pallas as pl
from jax.experimental.pallas import tpu as pltpu
from jax.sharding import PartitionSpec as P

HEADS = 8
FF = 2048
STEP = 10

EPS_NORM = 1e-05
RATE = 0.2
BETA_ONE = 0.9
BETA_TWO = 0.999
ADAM_EPS = 1e-08
DECAY = 0.0001
MASKED = -1000000000.0

TILE = 128
WINDOW = 384
ROWS = 512
FEED_ROWS = 1024
BLOCK = 256
BLOCKS = FF // BLOCK
GELU_A = 0.7978845608028654
GELU_B = 0.044715
LOG2_E = 1.4426950408889634
VEC_PAD = 24

F32 = jnp.float32
BF16 = jnp.bfloat16
VMEM = pltpu.VMEM


def nn(a, b):
    return lax.dot_general(a, b, (((1,), (0,)), ((), ())), preferred_element_type=F32)


def nt(a, b):
    return lax.dot_general(a, b, (((1,), (1,)), ((), ())), preferred_element_type=F32)


def tn(a, b):
    return lax.dot_general(a, b, (((0,), (0,)), ((), ())), preferred_element_type=F32)


def row_mean(x):
    return jnp.sum(x, axis=1, keepdims=True) * (1.0 / x.shape[1])


def fold_rows(x):
    return jnp.sum(x.reshape(x.shape[0] // 8, 8, x.shape[1]), axis=0)


def column_sum(x):
    return jnp.sum(x.astype(F32), axis=0, keepdims=True)


def head_lanes(h, rows, width):
    lane = lax.broadcasted_iota(jnp.int32, (rows, width), 1)
    size = width // HEADS
    return (lane >= h * size) & (lane < (h + 1) * size)


def window_start(i, tok):
    return jnp.clip((i - 1) * TILE, 0, tok - WINDOW)


def call(kernel, outs, ins, scratch, name, flops, spaces=None, vmem=12):
    spaces = spaces or [VMEM] * len(ins)
    nbytes = 0 * sum(a.size * a.dtype.itemsize for a in ins) + sum(
        a.size * a.dtype.itemsize for a in outs
    )
    return pl.pallas_call(
        kernel,
        out_shape=tuple(outs),
        in_specs=[pl.BlockSpec(memory_space=s) for s in spaces],
        out_specs=tuple(pl.BlockSpec(memory_space=VMEM) for _ in outs),
        scratch_shapes=scratch,
        compiler_params=pltpu.CompilerParams(vmem_limit_bytes=vmem << 20),
        cost_estimate=pl.CostEstimate(flops=flops, bytes_accessed=nbytes, transcendentals=0),
        name=name,
    )(*ins)


def shape(dims, kind):
    return jax.ShapeDtypeStruct(dims, kind)


def load_pieces(refs, offsets, dst):
    for ref, offs in zip(refs, offsets):
        if len(ref.shape) == 2:
            dst[pl.ds(offs[0], ref.shape[0]), :] = ref[...]
        else:
            for i, off in enumerate(offs):
                dst[pl.ds(off, ref.shape[1]), :] = ref[i]


def place_offsets(place, piece, planes):
    offsets = []
    for other in (0, 1):
        for slot in (0, 3, 2, 1):
            core = place[3] ^ other if other else place[3]
            inner = 2 * (place[1] ^ slot) + core
            offsets.append(
                [pl.multiple_of((8 * plane + inner) * piece, 16) for plane in range(planes)]
            )
    return offsets


def prepare_kernel(lens, crops, feat, vec, pos, seg_col, seg_row, feat_near, vec_near):
    feat_near[...] = feat[...]
    vec_near[...] = vec[...]
    tok, width = pos.shape
    half = width // 2
    first = lens[0, 0]
    lane = lax.broadcasted_iota(jnp.int32, (TILE, half), 1)
    frequency = jnp.exp(lane.astype(F32) * (-math.log(10000.0) / half))
    at = lax.broadcasted_iota(jnp.int32, (tok // TILE, TILE), 0) * TILE
    at = at + lax.broadcasted_iota(jnp.int32, (tok // TILE, TILE), 1)
    seg_row[...] = (2 * crops[...] + (at >= first).astype(jnp.int32)).astype(F32)
    for i in range(tok // TILE):
        r = slice(i * TILE, (i + 1) * TILE)
        row = lax.broadcasted_iota(jnp.int32, (TILE, half), 0) + i * TILE
        angle = (row - jnp.where(row >= first, first, 0)).astype(F32) * frequency
        pos[r, 0:half] = jnp.sin(angle)
        pos[r, half:width] = jnp.cos(angle)
        seg_col[r, :] = jnp.broadcast_to(seg_row[i : i + 1, :], (TILE, TILE)).T


def prepare(lens, crops, feat, vec):
    tok, width = crops.shape[0], vec.shape[1]
    crops = crops.reshape(-1, TILE)
    return call(
        prepare_kernel,
        [
            shape((tok, width), F32),
            shape((tok, TILE), F32),
            shape(crops.shape, F32),
            shape(feat.shape, BF16),
            shape(vec.shape, F32),
        ],
        [lens, crops, feat, vec],
        [],
        "positions_segments",
        1_000_000,
        [pltpu.SMEM, VMEM, VMEM, VMEM],
    )


def attention_kernel(flat, piece, place, feat, pos, seg_col, seg_row, vec, *rest):
    count = 1 if flat else 8
    pieces, rest = rest[:count], rest[count:]
    w, emb, src, q, k, v, attn_t, p, scale_inv, v_t, q_t = rest
    tok, width = emb.shape
    feat_dim = feat.shape[1]
    size = width // HEADS
    scale = size ** (-0.5)
    offsets = [[0]] if flat else place_offsets(place, piece, 1)
    load_pieces(pieces, offsets, w)
    for i in range(tok // ROWS):
        r = pl.ds(i * ROWS, ROWS)
        e = nn(feat[r, :], w[0:feat_dim, :]) + vec[0:1, :]
        emb[r, :] = e
        s = (e + pos[r, :]).astype(BF16)
        src[r, :] = s
        low = e.astype(BF16)
        at = feat_dim
        q[r, :] = (nn(s, w[at : at + width, :]) + vec[1:2, :]).astype(BF16)
        k[r, :] = nn(s, w[at + width : at + 2 * width, :]).astype(BF16)
        v[r, :] = (nn(low, w[at + 2 * width : at + 3 * width, :]) + vec[2:3, :]).astype(BF16)
    pad = v_t.shape[0] // HEADS
    vals = v[...].T
    for h in range(HEADS):
        v_t[h * pad : h * pad + size, :] = vals[h * size : (h + 1) * size, :]
        v_t[h * pad + size : (h + 1) * pad, :] = jnp.ones((pad - size, tok), BF16)
    q_t[...] = jnp.zeros_like(q_t)
    masked = MASKED / scale
    factor = scale * LOG2_E

    def tile(i, carry):
        rows = pl.ds(pl.multiple_of(i * TILE, TILE), TILE)
        win = pl.ds(pl.multiple_of(window_start(i, tok), TILE), WINDOW)
        own_t = q[rows, :].T
        keys = k[win, :]
        vals_t = v_t[:, win]
        allowed = seg_col[win, :] == seg_row[pl.ds(i, 1), :]
        for h in range(HEADS):
            d = slice(h * size, (h + 1) * size)
            q_t[d, h * TILE : (h + 1) * TILE] = own_t[d, :]
        for g in range(HEADS // 8):
            both = nn(keys, q_t[:, 8 * g * TILE : (8 * g + 8) * TILE])
            for u in range(8):
                h = 8 * g + u
                s = jnp.where(allowed, both[:, u * TILE : (u + 1) * TILE], masked)
                top = jnp.max(s, axis=0, keepdims=True)
                e = jnp.exp2((s - top) * factor).astype(BF16)
                p[i, :, h * TILE : (h + 1) * TILE] = e
        for g in range(HEADS // 2):
            o = nn(
                vals_t[2 * g * pad : (2 * g + 2) * pad, :],
                p[i, :, 2 * g * TILE : (2 * g + 2) * TILE],
            )
            for u in range(2):
                h = 2 * g + u
                own = o[u * pad : (u + 1) * pad, u * TILE : (u + 1) * TILE]
                inv = 1.0 / own[size : size + 1, :]
                scale_inv[i, h : h + 1, :] = inv
                attn_t[h * size : (h + 1) * size, rows] = (own[0:size, :] * inv).astype(BF16)
        return carry

    lax.fori_loop(0, tok // TILE, tile, 0, unroll=8)


def attention(flat, place, feat, pos, segment, vec, pieces, attn_rows):
    tok, width = feat.shape[0], vec.shape[1]
    piece = pieces[0].shape[0]
    low = shape((tok, width), BF16)
    outs = [
        shape((attn_rows, width), BF16),
        shape((tok, width), F32),
        low,
        low,
        low,
        low,
        shape((width, tok), BF16),
        shape((tok // TILE, WINDOW, HEADS * TILE), BF16),
        shape((tok // TILE, HEADS, TILE), F32),
    ]
    ins = [place, feat, pos, *segment, vec, *pieces]
    return call(
        functools.partial(attention_kernel, flat, piece),
        outs,
        ins,
        [
            VMEM((width + 16 * HEADS, tok), BF16),
            VMEM((width, HEADS * TILE), BF16),
        ],
        "attention_forward",
        1_200_000_000,
        [pltpu.SMEM] + [VMEM] * (5 + len(pieces)),
        vmem=20,
    )


def feed_kernel(flat, piece, place, emb, attn_t, cot, vec, wa, *rest):
    count = 1 if flat else 8
    pieces, rest = rest[:count], rest[count:]
    outs = 5 if flat else 6
    res, rest = rest[: outs + 1], rest[outs + 1 :]
    out, g_one, w_out, vec_grad, dwo = res[:5]
    (wf, wh, wh_t, wb_t, half_a, half_b, act, slope, n_t, b_t, out_all, acc, gff) = rest
    halves = (half_a, half_b)
    tok, width = emb.shape
    first = width // 2
    offsets = [[0]] if flat else place_offsets(place, piece, 3)
    load_pieces(pieces, offsets, wf)
    for u in range(2):
        halves[u][...] = wf[first : first + FF, u * 128 : (u + 1) * 128].astype(F32)
    w_out[0:first, :] = wa[wa.shape[0] - first :, :]
    w_out[first:, :] = wf[0:first, :]
    for j in range(BLOCKS):
        c = slice(j * BLOCK, (j + 1) * BLOCK)
        w = jnp.concatenate(
            [halves[u][pl.ds(j, width, stride=BLOCKS), :] for u in range(2)], axis=1
        ).astype(BF16)
        wh[:, c] = w
        wh_t[c, :] = w.T
        wb_t[:, c] = wf[first + FF + j * BLOCK : first + FF + (j + 1) * BLOCK, :].T
    acc[...] = jnp.zeros_like(acc)
    n_t[width : width + 8, :] = jnp.ones((8, tok), BF16)

    r = slice(0, tok)
    res_one = emb[r, :] + tn(attn_t[:, r], w_out[...]) + vec[3:4, :]
    cen = res_one - row_mean(res_one)
    inv_one = lax.rsqrt(row_mean(cen * cen) + EPS_NORM)
    hat_one = cen * inv_one
    normed = hat_one * vec[4:5, :] + vec[5:6, :]
    low = normed.astype(BF16)
    res_two = normed + vec[6:7, :]
    for j in range(BLOCKS):
        c = slice(j * BLOCK, (j + 1) * BLOCK)
        at = first + FF + j * BLOCK
        x = nn(low, wh[:, c]) + vec[9 + j : 10 + j, :]
        sq = x * x
        t = jnp.tanh((x * (GELU_A + (GELU_A * GELU_B) * sq)).astype(BF16))
        half = t * jnp.bfloat16(0.5) + jnp.bfloat16(0.5)
        act[r, c] = x.astype(BF16) * half
        bend = (x * ((2 * GELU_A) + (6 * GELU_A * GELU_B) * sq)).astype(BF16)
        slope[r, c] = half + (half - half * half) * bend
        res_two += nn(act[r, c], wf[at : at + BLOCK, :])
    cen = res_two - row_mean(res_two)
    inv_two = lax.rsqrt(row_mean(cen * cen) + EPS_NORM)
    hat_two = cen * inv_two
    out[r, :] = hat_two * vec[7:8, :] + vec[8:9, :]
    ct = cot[r, :].astype(F32)
    gs = ct * vec[7:8, :]
    g_two = inv_two * (gs - row_mean(gs) - hat_two * row_mean(gs * hat_two))
    back = g_two.astype(BF16)
    b_t[:, r] = back.T
    acc[0] += fold_rows(back.astype(F32))
    acc[1] += fold_rows(ct * hat_two)
    acc[2] += fold_rows(ct)
    n_t[0:width, r] = low.T
    g_norm = g_two
    for j in range(BLOCKS):
        c = slice(j * BLOCK, (j + 1) * BLOCK)
        part = (nn(back, wb_t[:, c]) * slope[r, c].astype(F32)).astype(BF16)
        g_norm += nn(part, wh_t[c, :])
        g = nn(n_t[...], part)
        for u in range(2):
            halves[u][pl.ds(j, width, stride=BLOCKS), :] = g[0:width, u * 128 : (u + 1) * 128]
        vec_grad[9 + j : 10 + j, :] = g[width : width + 1, :]
        at = first + FF + j * BLOCK
        gff[at : at + BLOCK, :] = nn(b_t[...], act[:, c]).T.astype(BF16)
    gs = g_norm * vec[4:5, :]
    g_res = inv_one * (gs - row_mean(gs) - hat_one * row_mean(gs * hat_one))
    g_one[r, :] = g_res
    out_low = g_res.astype(BF16)
    out_all[r, :] = out_low
    acc[3] += fold_rows(out_low.astype(F32))
    acc[4] += fold_rows(g_norm * hat_one)
    acc[5] += fold_rows(g_norm)

    for u in range(2):
        gff[first : first + FF, u * 128 : (u + 1) * 128] = halves[u][...].astype(BF16)
    g = nn(attn_t[...], out_all[...]).astype(BF16)
    dwo[...] = g[0:first, :]
    gff[0:first, :] = g[first:, :]
    sums = jnp.sum(acc[...], axis=1)
    vec_grad[0:3, :] = jnp.zeros((3, width), F32)
    for row, at in ((3, 3), (4, 4), (5, 5), (6, 0), (7, 1), (8, 2)):
        vec_grad[row : row + 1, :] = sums[at : at + 1, :]
    if flat:
        res[5][...] = gff[...]
    else:
        split_cores(place, gff, res[5], res[6])


def split_cores(place, grads, keep, send):
    core = place[3]
    piece = keep.shape[1]
    for m in range(keep.shape[0]):
        keep[m] = grads[pl.ds(pl.multiple_of((2 * m + core) * piece, 16), piece), :]
        send[m] = grads[pl.ds(pl.multiple_of((2 * m + 1 - core) * piece, 16), piece), :]


def feed(flat, place, emb, attn_t, cot, vec, wa, pieces, ff_rows):
    tok, width = emb.shape
    piece = pieces[0].shape[-2]
    outs = [
        shape((tok, width), F32),
        shape((tok, width), F32),
        shape((width, width), BF16),
        shape(vec.shape, F32),
        shape((width // 2, width), BF16),
    ]
    if flat:
        outs += [shape((ff_rows, width), BF16)]
    else:
        outs += [shape((ff_rows // piece // 2, piece, width), BF16)] * 2
    return call(
        functools.partial(feed_kernel, flat, piece),
        outs,
        [place, emb, attn_t, cot, vec, wa, *pieces],
        [
            VMEM((ff_rows, width), BF16),
            VMEM((width, FF), BF16),
            VMEM((FF, width), BF16),
            VMEM((width, FF), BF16),
            VMEM((FF, 128), F32),
            VMEM((FF, 128), F32),
            VMEM((tok, FF), BF16),
            VMEM((tok, FF), BF16),
            VMEM((width + 8, tok), BF16),
            VMEM((width, tok), BF16),
            VMEM((tok, width), BF16),
            VMEM((6, 8, width), F32),
            VMEM((ff_rows, width), BF16),
        ],
        "feed_forward_both",
        14_000_000_000,
        [pltpu.SMEM] + [VMEM] * (5 + len(pieces)),
        vmem=34,
    )


def attention_back(g_one, q, k, v, p, scale_inv, attn_t, w_out, ql, kl, vl, *scratch):
    ag, k_t, ds_all, a_t, scaled, qm, am, dk, dv = scratch
    tok, width = g_one.shape
    size = width // HEADS
    scale = size ** (-0.5)
    for i in range(tok // ROWS):
        r = pl.ds(i * ROWS, ROWS)
        ag[r, :] = nt(g_one[r, :].astype(BF16), w_out[...]).astype(BF16)
    k_t[...] = k[...].T
    dk[...] = jnp.zeros_like(dk)
    dv[...] = jnp.zeros_like(dv)
    a_t[...] = jnp.zeros_like(a_t)

    def tile(i, carry):
        rows = pl.ds(pl.multiple_of(i * TILE, TILE), TILE)
        win = pl.ds(pl.multiple_of(window_start(i, tok), TILE), WINDOW)
        own_q = q[rows, :]
        own_t = ag[rows, :].T
        vals = v[win, :]
        keys_t = k_t[:, win]
        inner = []
        for h in range(HEADS):
            d = slice(h * size, (h + 1) * size)
            grad = own_t[d, :].astype(F32) * scale_inv[i, h : h + 1, :]
            inner.append(jnp.sum(grad * attn_t[d, rows].astype(F32), axis=0, keepdims=True))
            a_t[d, h * TILE : (h + 1) * TILE] = grad.astype(BF16)
            scaled[d, :] = grad.astype(BF16)
        own_a = scaled[...].T
        for h in range(HEADS):
            lanes = head_lanes(h, TILE, width)
            c = slice(h * TILE, (h + 1) * TILE)
            qm[c, :] = jnp.where(lanes, own_q, jnp.zeros_like(own_q))
            am[c, :] = jnp.where(lanes, own_a, jnp.zeros_like(own_a))
        parts = []
        for g in range(HEADS // 8):
            both = nn(vals, a_t[:, 8 * g * TILE : (8 * g + 8) * TILE])
            for u in range(8):
                h = 8 * g + u
                c = slice(h * TILE, (h + 1) * TILE)
                dp = both[:, u * TILE : (u + 1) * TILE]
                ds = (p[i, :, c].astype(F32) * (dp - inner[h])).astype(BF16)
                ds_all[:, c] = ds
        for g in range(HEADS // 2):
            o = nn(
                keys_t[2 * g * size : (2 * g + 2) * size, :],
                ds_all[:, 2 * g * TILE : (2 * g + 2) * TILE],
            )
            parts += [o[0:size, 0:TILE], o[size : 2 * size, TILE : 2 * TILE]]
        ql[rows, :] = (jnp.concatenate(parts, axis=0).T * scale).astype(BF16)
        dk[win, :] += nn(ds_all[...], qm[...])
        dv[win, :] += nn(p[i], am[...])
        return carry

    lax.fori_loop(0, tok // TILE, tile, 0, unroll=8)
    kl[...] = (dk[...] * scale).astype(BF16)
    vl[...] = dv[...].astype(BF16)


def backward_kernel(flat, piece, place, g_one, q, k, v, p, scale_inv, attn_t, w_out, *rest):
    count = 9 if flat else 10
    feat, emb, src, dwo, vg, wa, low_out, *outs = rest[:count]
    grads, ql, kl, vl, *scratch = rest[count:]
    attention_back(g_one, q, k, v, p, scale_inv, attn_t, w_out, ql, kl, vl, *scratch)
    tok, width = g_one.shape
    at = feat.shape[1]
    total = jnp.zeros((1, width), F32)
    for i in range(tok // ROWS):
        r = pl.ds(i * ROWS, ROWS)
        e = (
            g_one[r, :]
            + nt(ql[r, :], wa[at : at + width, :])
            + nt(kl[r, :], wa[at + width : at + 2 * width, :])
            + nt(vl[r, :], wa[at + 2 * width : at + 3 * width, :])
        )
        low = e.astype(BF16)
        low_out[r, :] = low
        total += column_sum(low)
    src_t = src[...].T
    grads[at : at + width, :] = nn(src_t, ql[...]).astype(BF16)
    grads[at + width : at + 2 * width, :] = nn(src_t, kl[...]).astype(BF16)
    grads[at + 2 * width : at + 3 * width, :] = nn(emb[...].astype(BF16).T, vl[...]).astype(BF16)
    grads[0:at, :] = nn(feat[...].T, low_out[...]).astype(BF16)
    grads[at + 3 * width :, :] = dwo[...]
    front = jnp.concatenate([total, column_sum(ql[...]), column_sum(vl[...])], axis=0)
    if flat:
        outs[0][...] = grads[...]
        outs[1][...] = vg[...]
        outs[1][0:3, :] = front
        return
    keep, send_one, send_two = outs
    core = place[3]
    for m in range(4):
        send = (send_one, send_two)[m // 2]
        to = pl.ds((m % 2) * piece, piece)
        keep[pl.ds(m * piece, piece), :] = grads[
            pl.ds(pl.multiple_of((2 * m + core) * piece, 16), piece), :
        ]
        send[to, :] = grads[pl.ds(pl.multiple_of((2 * m + 1 - core) * piece, 16), piece), :]
    rows = vg.shape[0]
    pad = jnp.zeros((VEC_PAD - rows, width), F32)
    tail = jnp.concatenate([front, vg[3:rows, :], pad], axis=0).astype(BF16)
    keep[4 * piece :, :] = tail
    send_two[2 * piece :, :] = tail


def backward(flat, place, g_one, q, k, v, p, scale_inv, attn_t, w_out, feat, emb, src, *rest):
    dwo, vg, wa, piece = rest
    tok, width = g_one.shape
    outs = [shape((tok, width), BF16)]
    if flat:
        outs += [shape(wa.shape, BF16), shape(vg.shape, F32)]
    else:
        outs += [shape((4 * piece + VEC_PAD, width), BF16)]
        outs += [shape((2 * piece, width), BF16), shape((2 * piece + VEC_PAD, width), BF16)]
    ins = [place, g_one, q, k, v, p, scale_inv, attn_t, w_out, feat, emb, src, dwo, vg, wa]
    low = VMEM((tok, width), BF16)
    return call(
        functools.partial(backward_kernel, flat, piece),
        outs,
        ins,
        [
            VMEM(wa.shape, BF16),
            low,
            low,
            low,
            low,
            VMEM((width, tok), BF16),
            VMEM((WINDOW, HEADS * TILE), BF16),
            VMEM((width, HEADS * TILE), BF16),
            VMEM((width, TILE), BF16),
            VMEM((HEADS * TILE, width), BF16),
            VMEM((HEADS * TILE, width), BF16),
            VMEM((tok, width), F32),
            VMEM((tok, width), F32),
        ],
        "attention_backward",
        16_000_000_000,
        [pltpu.SMEM] + [VMEM] * (len(ins) - 1),
        vmem=24,
    )


def feature_kernel(low, wa, out):
    for i in range(low.shape[0] // ROWS):
        r = pl.ds(i * ROWS, ROWS)
        out[r, :] = nt(low[r, :], wa[0 : out.shape[1], :])


def feature_back(low, wa, feat_dim):
    return call(
        feature_kernel,
        [shape((low.shape[0], feat_dim), F32)],
        [low, wa],
        [],
        "feature_gradient",
        300_000_000,
    )[0]


def plane_kernel(place, own, one, two, three, attn, rest):
    got = (own, one, two, three)
    z = place[0]
    for slot in range(4):

        @pl.when(z == slot)
        def _(slot=slot):
            attn[...] = got[slot][...]
            for plane in range(1, 4):
                rest[plane - 1] = got[slot ^ plane][...]


def pick_planes(place, own, one, two, three):
    return call(
        plane_kernel,
        [shape(own.shape, BF16), shape((3, *own.shape), BF16)],
        [place, own, one, two, three],
        [],
        "pick_planes",
        1_000_000,
        [pltpu.SMEM] + [VMEM] * 4,
    )


def ff_sum_kernel(place, keep, recv, *outs):
    yx = place[1]
    for slot in range(4):
        for plane in range(3):
            at = 4 * plane + (yx ^ slot)
            outs[slot][plane] = keep[at] + recv[at]


def ff_sum(place, keep, recv):
    one = shape((3, *keep.shape[1:]), BF16)
    return call(
        ff_sum_kernel,
        [one] * 4,
        [place, keep, recv],
        [],
        "sum_cores_ff",
        1_000_000,
        [pltpu.SMEM] + [VMEM] * 2,
    )


def four_kernel(a, b, c, d, out):
    out[...] = (
        (a[...].astype(F32) + b[...].astype(F32)) + (c[...].astype(F32) + d[...].astype(F32))
    ).astype(BF16)


def four_sum(a, b, c, d):
    return call(four_kernel, [shape(a.shape, BF16)], [a, b, c, d], [], "sum_plane_ff", 1_000_000)[0]


def tail_sum_kernel(piece, place, keep, one, two, *outs):
    vec = keep[4 * piece :, :].astype(F32) + two[2 * piece :, :].astype(F32)
    for slot in range(4):
        m = place[1] ^ slot
        own = keep[pl.ds(pl.multiple_of(m * piece, 16), piece), :]
        at = pl.ds(pl.multiple_of((m & 1) * piece, 16), piece)
        outs[slot][piece:, :] = vec.astype(BF16)
        for half, recv in enumerate((one, two)):

            @pl.when((m >> 1) == half)
            def _(slot=slot, own=own, at=at, recv=recv):
                outs[slot][0:piece, :] = own + recv[at, :]


def tail_sum(place, keep, one, two, piece):
    return call(
        functools.partial(tail_sum_kernel, piece),
        [shape((piece + VEC_PAD, keep.shape[1]), BF16)] * 4,
        [place, keep, one, two],
        [],
        "sum_cores_tail",
        1_000_000,
        [pltpu.SMEM] + [VMEM] * 3,
    )


def plane_sum_kernel(place, a, b, c, d, ff, *outs):
    z = place[0]
    total = (
        (a[...].astype(F32) + b[...].astype(F32)) + (c[...].astype(F32) + d[...].astype(F32))
    ).astype(BF16)
    piece = ff.shape[1]
    for slot in range(4):
        goal = z ^ slot
        outs[slot][piece:, :] = total[piece:, :]

        @pl.when(goal == 0)
        def _(slot=slot):
            outs[slot][0:piece, :] = total[0:piece, :]

        @pl.when(goal != 0)
        def _(slot=slot, goal=goal):
            outs[slot][0:piece, :] = ff[jnp.maximum(goal - 1, 0)]


def plane_sum(place, a, b, c, d, ff):
    return call(
        plane_sum_kernel,
        [shape(a.shape, BF16)] * 4,
        [place, a, b, c, d, ff],
        [],
        "sum_plane_tail",
        1_000_000,
        [pltpu.SMEM] + [VMEM] * 5,
    )


def adam_step(weight, moment_one, moment_two, gradient, step_rate, decay_rate):
    moment_one = BETA_ONE * moment_one + (1.0 - BETA_ONE) * gradient
    moment_two = BETA_TWO * moment_two + (1.0 - BETA_TWO) * gradient * gradient
    mean_hat = moment_one / (1.0 - BETA_ONE**STEP)
    square_hat = moment_two / (1.0 - BETA_TWO**STEP)
    weight = weight - step_rate * (
        mean_hat / (jnp.sqrt(square_hat) + ADAM_EPS) + decay_rate * weight
    )
    return (weight, moment_one, moment_two)


def adam_kernel(feat_dim, place, a, b, c, d, w, m, v, vw, vm, vv, *outs):
    total = (a[...].astype(F32) + b[...].astype(F32)) + (c[...].astype(F32) + d[...].astype(F32))
    piece = w.shape[0]
    rows = place[2] * piece + lax.broadcasted_iota(jnp.int32, w.shape, 0)
    rate = jnp.where(rows < feat_dim, 0.1 * RATE, RATE)
    new = adam_step(w[...], m[...], v[...], total[0:piece, :], rate, DECAY)
    for ref, value in zip(outs[:3], new):
        ref[...] = value
    outs[3][...] = new[0].astype(BF16)
    new = adam_step(vw[...], vm[...], vv[...], total[piece : piece + vw.shape[0], :], RATE, 0.0)
    for ref, value in zip(outs[4:], new):
        ref[...] = value


def adam(place, parts, mats, mats_m, mats_v, vecs, vecs_m, vecs_v, feat_dim):
    mat, vec = shape(mats.shape, F32), shape(vecs.shape, F32)
    return call(
        functools.partial(adam_kernel, feat_dim),
        [mat, mat, mat, shape(mats.shape, BF16), vec, vec, vec],
        [place, *parts, mats, mats_m, mats_v, vecs, vecs_m, vecs_v],
        [],
        "adam",
        10_000_000,
        [pltpu.SMEM] + [VMEM] * 10,
    )


def grid_swap(dz, dyx):
    return [(4 * z + yx, 4 * (z ^ dz) + (yx ^ dyx)) for z in range(4) for yx in range(4)]


PAIR_SWAP = [(0, 1), (1, 0)]


def per_device(
    flat,
    features,
    cotangent,
    canvas_lengths,
    crop_ids,
    mats,
    mats_m,
    mats_v,
    vecs,
    vecs_m,
    vecs_v,
):
    tok = features.shape[0]
    feat_dim = features.shape[1]
    width = vecs.shape[1]
    attn_rows = feat_dim + 3 * width + width // 2
    ff_rows = width // 2 + 2 * FF
    piece = mats.shape[0]
    dp, core = lax.axis_index("dp"), lax.axis_index("pair")
    device = lax.axis_index(("dp", "pair"))
    place = jnp.stack([dp // 4, dp % 4, device, core]).astype(jnp.int32)

    near = prepare(canvas_lengths, crop_ids, features, vecs)
    mats_low = mats.astype(BF16)
    if flat:
        gathered = lax.all_gather(mats_low, ("dp", "pair"), axis=0, tiled=True)
        attn_pieces = [gathered[:attn_rows]]
        ff_pieces = [gathered[attn_rows:]]
    else:
        planes = [lax.ppermute(mats_low, "dp", grid_swap(dz, 0)) for dz in (1, 2, 3)]
        near, planes = lax.optimization_barrier((near, planes))
        one, three = pick_planes(place, mats_low, *planes)
        attn_pieces = [one] + [lax.ppermute(one, "dp", grid_swap(0, s)) for s in (3, 2, 1)]
        attn_pieces += [lax.ppermute(a, "pair", PAIR_SWAP) for a in attn_pieces]
        ff_pieces = [three] + [lax.ppermute(three, "dp", grid_swap(0, s)) for s in (3, 2, 1)]

    pos_table, seg_col, seg_row, features, vec = near
    wa, emb, src, q, k, v, attn_t, probs, scale_inv = attention(
        flat, place, features, pos_table, (seg_col, seg_row), vec, attn_pieces, attn_rows
    )
    if not flat:
        own_swap = lax.ppermute(ff_pieces[0], "pair", PAIR_SWAP)
        attn_t, *moved = lax.optimization_barrier((attn_t, *ff_pieces[1:]))
        moved_swap = [lax.ppermute(a, "pair", PAIR_SWAP) for a in moved]
        ff_pieces = [ff_pieces[0], *moved, own_swap, *moved_swap]
    output, g_one, w_out, vg, dwo, *ff_grads = feed(
        flat, place, emb, attn_t, cotangent, vec, wa, ff_pieces, ff_rows
    )
    if not flat:
        keep, send = ff_grads
        sums = ff_sum(place, keep, lax.ppermute(send, "pair", PAIR_SWAP))
        g_one, *sums = lax.optimization_barrier((g_one, *sums))
        ff_parts = [sums[0]] + [lax.ppermute(sums[s], "dp", grid_swap(0, s)) for s in (1, 2, 3)]
    low, *tail = backward(
        flat,
        place,
        g_one,
        q,
        k,
        v,
        probs,
        scale_inv,
        attn_t,
        w_out,
        features,
        emb,
        src,
        dwo,
        vg,
        wa,
        piece,
    )
    feature_grad = feature_back(low, wa, feat_dim)
    if flat:
        grads = jnp.concatenate([tail[0], ff_grads[0]], axis=0).astype(F32)
        total = lax.psum_scatter(grads, ("dp", "pair"), scatter_dimension=0, tiled=True)
        vec_total = lax.psum(tail[1], ("dp", "pair"))
        row_ids = device * piece + jnp.arange(piece, dtype=jnp.int32)
        rate = jnp.where(row_ids < feat_dim, 0.1 * RATE, RATE)[:, None]
        new = adam_step(mats, mats_m, mats_v, total, rate, DECAY)
        new_vec = adam_step(vecs, vecs_m, vecs_v, vec_total, RATE, 0.0)
        return (output, feature_grad, *new, new[0].astype(BF16), *new_vec)
    keep, *send = tail
    recv = [lax.ppermute(a, "pair", PAIR_SWAP) for a in send]
    sums = tail_sum(place, keep, *recv, piece)
    sums, ff_parts = lax.optimization_barrier((sums, ff_parts))
    ff = four_sum(*ff_parts)
    parts = [sums[0]] + [lax.ppermute(sums[s], "dp", grid_swap(0, s)) for s in (1, 2, 3)]
    sums = plane_sum(place, *parts, ff)
    parts = [sums[0]] + [lax.ppermute(sums[s], "dp", grid_swap(s, 0)) for s in (1, 2, 3)]
    new = adam(place, parts, mats, mats_m, mats_v, vecs, vecs_m, vecs_v, feat_dim)
    return (output, feature_grad, *new)


def solution(mesh):
    rows = P(("dp", "pair"), None)
    in_specs = (rows, rows, rows, P(("dp", "pair")), rows, rows, rows, P(), P(), P())
    out_specs = (rows, rows, rows, rows, rows, rows, P(), P(), P())
    flat = mesh.shape["dp"] != 16 or mesh.shape["pair"] != 2
    return jax.shard_map(
        functools.partial(per_device, flat),
        mesh=mesh,
        in_specs=in_specs,
        out_specs=out_specs,
        check_vma=False,
    )
```

```python
import functools
import math

import jax
import jax.numpy as jnp
from jax import lax
from jax.experimental import pallas as pl
from jax.experimental.pallas import tpu as pltpu
from jax.sharding import PartitionSpec as P

HEADS = 8
FF = 2048
STEP = 10

EPS_NORM = 1e-05
RATE = 0.2
BETA_ONE = 0.9
BETA_TWO = 0.999
ADAM_EPS = 1e-08
DECAY = 0.0001
MASKED = -1000000000.0

TILE = 128
WINDOW = 384
ROWS = 512
FEED_ROWS = 1024
BLOCK = 256
BLOCKS = FF // BLOCK
GELU_A = 0.7978845608028654
GELU_B = 0.044715
LOG2_E = 1.4426950408889634
VEC_PAD = 24

F32 = jnp.float32
BF16 = jnp.bfloat16
VMEM = pltpu.VMEM


def nn(a, b):
    return lax.dot_general(a, b, (((1,), (0,)), ((), ())), preferred_element_type=F32)


def nt(a, b):
    return lax.dot_general(a, b, (((1,), (1,)), ((), ())), preferred_element_type=F32)


def tn(a, b):
    return lax.dot_general(a, b, (((0,), (0,)), ((), ())), preferred_element_type=F32)


def row_mean(x):
    return jnp.sum(x, axis=1, keepdims=True) * (1.0 / x.shape[1])


def fold_rows(x):
    return jnp.sum(x.reshape(x.shape[0] // 8, 8, x.shape[1]), axis=0)


def column_sum(x):
    return jnp.sum(x.astype(F32), axis=0, keepdims=True)


def head_lanes(h, rows, width):
    lane = lax.broadcasted_iota(jnp.int32, (rows, width), 1)
    size = width // HEADS
    return (lane >= h * size) & (lane < (h + 1) * size)


def window_start(i, tok):
    return jnp.clip((i - 1) * TILE, 0, tok - WINDOW)


def call(kernel, outs, ins, scratch, name, flops, spaces=None, vmem=12):
    spaces = spaces or [VMEM] * len(ins)
    nbytes = 0 * sum(a.size * a.dtype.itemsize for a in ins) + sum(
        a.size * a.dtype.itemsize for a in outs
    )
    return pl.pallas_call(
        kernel,
        out_shape=tuple(outs),
        in_specs=[pl.BlockSpec(memory_space=s) for s in spaces],
        out_specs=tuple(pl.BlockSpec(memory_space=VMEM) for _ in outs),
        scratch_shapes=scratch,
        compiler_params=pltpu.CompilerParams(vmem_limit_bytes=vmem << 20),
        cost_estimate=pl.CostEstimate(flops=flops, bytes_accessed=nbytes, transcendentals=0),
        name=name,
    )(*ins)


def shape(dims, kind):
    return jax.ShapeDtypeStruct(dims, kind)


def load_pieces(refs, offsets, dst):
    for ref, offs in zip(refs, offsets):
        if len(ref.shape) == 2:
            dst[pl.ds(offs[0], ref.shape[0]), :] = ref[...]
        else:
            for i, off in enumerate(offs):
                dst[pl.ds(off, ref.shape[1]), :] = ref[i]


def place_offsets(place, piece, planes):
    offsets = []
    for other in (0, 1):
        for slot in (0, 3, 1, 2):
            core = place[3] ^ other if other else place[3]
            inner = 2 * (place[1] ^ slot) + core
            offsets.append(
                [pl.multiple_of((8 * plane + inner) * piece, 16) for plane in range(planes)]
            )
    return offsets


def prepare_kernel(lens, crops, feat, vec, pos, seg_col, seg_row, feat_near, vec_near):
    feat_near[...] = feat[...]
    vec_near[...] = vec[...]
    tok, width = pos.shape
    half = width // 2
    first = lens[0, 0]
    lane = lax.broadcasted_iota(jnp.int32, (TILE, half), 1)
    frequency = jnp.exp(lane.astype(F32) * (-math.log(10000.0) / half))
    at = lax.broadcasted_iota(jnp.int32, (tok // TILE, TILE), 0) * TILE
    at = at + lax.broadcasted_iota(jnp.int32, (tok // TILE, TILE), 1)
    seg_row[...] = (2 * crops[...] + (at >= first).astype(jnp.int32)).astype(F32)
    for i in range(tok // TILE):
        r = slice(i * TILE, (i + 1) * TILE)
        row = lax.broadcasted_iota(jnp.int32, (TILE, half), 0) + i * TILE
        angle = (row - jnp.where(row >= first, first, 0)).astype(F32) * frequency
        pos[r, 0:half] = jnp.sin(angle)
        pos[r, half:width] = jnp.cos(angle)
        seg_col[r, :] = jnp.broadcast_to(seg_row[i : i + 1, :], (TILE, TILE)).T


def prepare(lens, crops, feat, vec):
    tok, width = crops.shape[0], vec.shape[1]
    crops = crops.reshape(-1, TILE)
    return call(
        prepare_kernel,
        [
            shape((tok, width), F32),
            shape((tok, TILE), F32),
            shape(crops.shape, F32),
            shape(feat.shape, BF16),
            shape(vec.shape, F32),
        ],
        [lens, crops, feat, vec],
        [],
        "positions_segments",
        1_000_000,
        [pltpu.SMEM, VMEM, VMEM, VMEM],
    )


def attention_kernel(flat, piece, place, feat, pos, seg_col, seg_row, vec, *rest):
    count = 1 if flat else 8
    pieces, rest = rest[:count], rest[count:]
    w, emb, src, q, k, v, attn_t, p, scale_inv, v_t, q_t = rest
    tok, width = emb.shape
    feat_dim = feat.shape[1]
    size = width // HEADS
    scale = size ** (-0.5)
    offsets = [[0]] if flat else place_offsets(place, piece, 1)
    load_pieces(pieces, offsets, w)
    for i in range(tok // ROWS):
        r = pl.ds(i * ROWS, ROWS)
        e = nn(feat[r, :], w[0:feat_dim, :]) + vec[0:1, :]
        emb[r, :] = e
        s = (e + pos[r, :]).astype(BF16)
        src[r, :] = s
        low = e.astype(BF16)
        at = feat_dim
        q[r, :] = (nn(s, w[at : at + width, :]) + vec[1:2, :]).astype(BF16)
        k[r, :] = nn(s, w[at + width : at + 2 * width, :]).astype(BF16)
        v[r, :] = (nn(low, w[at + 2 * width : at + 3 * width, :]) + vec[2:3, :]).astype(BF16)
    pad = v_t.shape[0] // HEADS
    vals = v[...].T
    for h in range(HEADS):
        v_t[h * pad : h * pad + size, :] = vals[h * size : (h + 1) * size, :]
        v_t[h * pad + size : (h + 1) * pad, :] = jnp.ones((pad - size, tok), BF16)
    q_t[...] = jnp.zeros_like(q_t)
    masked = MASKED / scale
    factor = scale * LOG2_E

    def tile(i, carry):
        rows = pl.ds(pl.multiple_of(i * TILE, TILE), TILE)
        win = pl.ds(pl.multiple_of(window_start(i, tok), TILE), WINDOW)
        own_t = q[rows, :].T
        keys = k[win, :]
        vals_t = v_t[:, win]
        allowed = seg_col[win, :] == seg_row[pl.ds(i, 1), :]
        for h in range(HEADS):
            d = slice(h * size, (h + 1) * size)
            q_t[d, h * TILE : (h + 1) * TILE] = own_t[d, :]
        for g in range(HEADS // 8):
            both = nn(keys, q_t[:, 8 * g * TILE : (8 * g + 8) * TILE])
            for u in range(8):
                h = 8 * g + u
                s = jnp.where(allowed, both[:, u * TILE : (u + 1) * TILE], masked)
                top = jnp.max(s, axis=0, keepdims=True)
                e = jnp.exp2((s - top) * factor).astype(BF16)
                p[i, :, h * TILE : (h + 1) * TILE] = e
        for g in range(HEADS // 2):
            o = nn(
                vals_t[2 * g * pad : (2 * g + 2) * pad, :],
                p[i, :, 2 * g * TILE : (2 * g + 2) * TILE],
            )
            for u in range(2):
                h = 2 * g + u
                own = o[u * pad : (u + 1) * pad, u * TILE : (u + 1) * TILE]
                inv = 1.0 / own[size : size + 1, :]
                scale_inv[i, h : h + 1, :] = inv
                attn_t[h * size : (h + 1) * size, rows] = (own[0:size, :] * inv).astype(BF16)
        return carry

    lax.fori_loop(0, tok // TILE, tile, 0, unroll=8)


def attention(flat, place, feat, pos, segment, vec, pieces, attn_rows):
    tok, width = feat.shape[0], vec.shape[1]
    piece = pieces[0].shape[0]
    low = shape((tok, width), BF16)
    outs = [
        shape((attn_rows, width), BF16),
        shape((tok, width), F32),
        low,
        low,
        low,
        low,
        shape((width, tok), BF16),
        shape((tok // TILE, WINDOW, HEADS * TILE), BF16),
        shape((tok // TILE, HEADS, TILE), F32),
    ]
    ins = [place, feat, pos, *segment, vec, *pieces]
    return call(
        functools.partial(attention_kernel, flat, piece),
        outs,
        ins,
        [
            VMEM((width + 16 * HEADS, tok), BF16),
            VMEM((width, HEADS * TILE), BF16),
        ],
        "attention_forward",
        1_200_000_000,
        [pltpu.SMEM] + [VMEM] * (5 + len(pieces)),
        vmem=20,
    )


def feed_kernel(flat, piece, place, emb, attn_t, cot, vec, wa, *rest):
    count = 1 if flat else 8
    pieces, rest = rest[:count], rest[count:]
    outs = 5 if flat else 6
    res, rest = rest[: outs + 1], rest[outs + 1 :]
    out, g_one, w_out, vec_grad, dwo = res[:5]
    (wf, wh, wh_t, wb_t, half_a, half_b, act, slope, n_t, b_t, out_all, acc, gff) = rest
    halves = (half_a, half_b)
    tok, width = emb.shape
    first = width // 2
    offsets = [[0]] if flat else place_offsets(place, piece, 3)
    load_pieces(pieces, offsets, wf)
    for u in range(2):
        halves[u][...] = wf[first : first + FF, u * 128 : (u + 1) * 128].astype(F32)
    w_out[0:first, :] = wa[wa.shape[0] - first :, :]
    w_out[first:, :] = wf[0:first, :]
    for j in range(BLOCKS):
        c = slice(j * BLOCK, (j + 1) * BLOCK)
        w = jnp.concatenate(
            [halves[u][pl.ds(j, width, stride=BLOCKS), :] for u in range(2)], axis=1
        ).astype(BF16)
        wh[:, c] = w
        wh_t[c, :] = w.T
        wb_t[:, c] = wf[first + FF + j * BLOCK : first + FF + (j + 1) * BLOCK, :].T
    acc[...] = jnp.zeros_like(acc)
    n_t[width : width + 8, :] = jnp.ones((8, tok), BF16)

    r = slice(0, tok)
    res_one = emb[r, :] + tn(attn_t[:, r], w_out[...]) + vec[3:4, :]
    cen = res_one - row_mean(res_one)
    inv_one = lax.rsqrt(row_mean(cen * cen) + EPS_NORM)
    hat_one = cen * inv_one
    normed = hat_one * vec[4:5, :] + vec[5:6, :]
    low = normed.astype(BF16)
    res_two = normed + vec[6:7, :]
    for j in range(BLOCKS):
        c = slice(j * BLOCK, (j + 1) * BLOCK)
        at = first + FF + j * BLOCK
        x = nn(low, wh[:, c]) + vec[9 + j : 10 + j, :]
        sq = x * x
        t = jnp.tanh((x * (GELU_A + (GELU_A * GELU_B) * sq)).astype(BF16))
        half = t * jnp.bfloat16(0.5) + jnp.bfloat16(0.5)
        act[r, c] = x.astype(BF16) * half
        bend = (x * ((2 * GELU_A) + (6 * GELU_A * GELU_B) * sq)).astype(BF16)
        slope[r, c] = half + (half - half * half) * bend
        res_two += nn(act[r, c], wf[at : at + BLOCK, :])
    cen = res_two - row_mean(res_two)
    inv_two = lax.rsqrt(row_mean(cen * cen) + EPS_NORM)
    hat_two = cen * inv_two
    out[r, :] = hat_two * vec[7:8, :] + vec[8:9, :]
    ct = cot[r, :].astype(F32)
    gs = ct * vec[7:8, :]
    g_two = inv_two * (gs - row_mean(gs) - hat_two * row_mean(gs * hat_two))
    back = g_two.astype(BF16)
    b_t[:, r] = back.T
    acc[0] += fold_rows(back.astype(F32))
    acc[1] += fold_rows(ct * hat_two)
    acc[2] += fold_rows(ct)
    n_t[0:width, r] = low.T
    g_norm = g_two
    for j in range(BLOCKS):
        c = slice(j * BLOCK, (j + 1) * BLOCK)
        part = (nn(back, wb_t[:, c]) * slope[r, c].astype(F32)).astype(BF16)
        g_norm += nn(part, wh_t[c, :])
        g = nn(n_t[...], part)
        for u in range(2):
            halves[u][pl.ds(j, width, stride=BLOCKS), :] = g[0:width, u * 128 : (u + 1) * 128]
        vec_grad[9 + j : 10 + j, :] = g[width : width + 1, :]
        at = first + FF + j * BLOCK
        gff[at : at + BLOCK, :] = nn(b_t[...], act[:, c]).T.astype(BF16)
    gs = g_norm * vec[4:5, :]
    g_res = inv_one * (gs - row_mean(gs) - hat_one * row_mean(gs * hat_one))
    g_one[r, :] = g_res
    out_low = g_res.astype(BF16)
    out_all[r, :] = out_low
    acc[3] += fold_rows(out_low.astype(F32))
    acc[4] += fold_rows(g_norm * hat_one)
    acc[5] += fold_rows(g_norm)

    for u in range(2):
        gff[first : first + FF, u * 128 : (u + 1) * 128] = halves[u][...].astype(BF16)
    g = nn(attn_t[...], out_all[...]).astype(BF16)
    dwo[...] = g[0:first, :]
    gff[0:first, :] = g[first:, :]
    sums = jnp.sum(acc[...], axis=1)
    vec_grad[0:3, :] = jnp.zeros((3, width), F32)
    for row, at in ((3, 3), (4, 4), (5, 5), (6, 0), (7, 1), (8, 2)):
        vec_grad[row : row + 1, :] = sums[at : at + 1, :]
    if flat:
        res[5][...] = gff[...]
    else:
        split_cores(place, gff, res[5], res[6])


def split_cores(place, grads, keep, send):
    core = place[3]
    piece = keep.shape[1]
    for m in range(keep.shape[0]):
        keep[m] = grads[pl.ds(pl.multiple_of((2 * m + core) * piece, 16), piece), :]
        send[m] = grads[pl.ds(pl.multiple_of((2 * m + 1 - core) * piece, 16), piece), :]


def feed(flat, place, emb, attn_t, cot, vec, wa, pieces, ff_rows):
    tok, width = emb.shape
    piece = pieces[0].shape[-2]
    outs = [
        shape((tok, width), F32),
        shape((tok, width), F32),
        shape((width, width), BF16),
        shape(vec.shape, F32),
        shape((width // 2, width), BF16),
    ]
    if flat:
        outs += [shape((ff_rows, width), BF16)]
    else:
        outs += [shape((ff_rows // piece // 2, piece, width), BF16)] * 2
    return call(
        functools.partial(feed_kernel, flat, piece),
        outs,
        [place, emb, attn_t, cot, vec, wa, *pieces],
        [
            VMEM((ff_rows, width), BF16),
            VMEM((width, FF), BF16),
            VMEM((FF, width), BF16),
            VMEM((width, FF), BF16),
            VMEM((FF, 128), F32),
            VMEM((FF, 128), F32),
            VMEM((tok, FF), BF16),
            VMEM((tok, FF), BF16),
            VMEM((width + 8, tok), BF16),
            VMEM((width, tok), BF16),
            VMEM((tok, width), BF16),
            VMEM((6, 8, width), F32),
            VMEM((ff_rows, width), BF16),
        ],
        "feed_forward_both",
        14_000_000_000,
        [pltpu.SMEM] + [VMEM] * (5 + len(pieces)),
        vmem=34,
    )


def attention_back(g_one, q, k, v, p, scale_inv, attn_t, w_out, ql, kl, vl, *scratch):
    ag, k_t, ds_all, a_t, scaled, qm, am, dk, dv = scratch
    tok, width = g_one.shape
    size = width // HEADS
    scale = size ** (-0.5)
    for i in range(tok // ROWS):
        r = pl.ds(i * ROWS, ROWS)
        ag[r, :] = nt(g_one[r, :].astype(BF16), w_out[...]).astype(BF16)
    k_t[...] = k[...].T
    dk[...] = jnp.zeros_like(dk)
    dv[...] = jnp.zeros_like(dv)
    a_t[...] = jnp.zeros_like(a_t)

    def tile(i, carry):
        rows = pl.ds(pl.multiple_of(i * TILE, TILE), TILE)
        win = pl.ds(pl.multiple_of(window_start(i, tok), TILE), WINDOW)
        own_q = q[rows, :]
        own_t = ag[rows, :].T
        vals = v[win, :]
        keys_t = k_t[:, win]
        inner = []
        for h in range(HEADS):
            d = slice(h * size, (h + 1) * size)
            grad = own_t[d, :].astype(F32) * scale_inv[i, h : h + 1, :]
            inner.append(jnp.sum(grad * attn_t[d, rows].astype(F32), axis=0, keepdims=True))
            a_t[d, h * TILE : (h + 1) * TILE] = grad.astype(BF16)
            scaled[d, :] = grad.astype(BF16)
        own_a = scaled[...].T
        for h in range(HEADS):
            lanes = head_lanes(h, TILE, width)
            c = slice(h * TILE, (h + 1) * TILE)
            qm[c, :] = jnp.where(lanes, own_q, jnp.zeros_like(own_q))
            am[c, :] = jnp.where(lanes, own_a, jnp.zeros_like(own_a))
        parts = []
        for g in range(HEADS // 8):
            both = nn(vals, a_t[:, 8 * g * TILE : (8 * g + 8) * TILE])
            for u in range(8):
                h = 8 * g + u
                c = slice(h * TILE, (h + 1) * TILE)
                dp = both[:, u * TILE : (u + 1) * TILE]
                ds = (p[i, :, c].astype(F32) * (dp - inner[h])).astype(BF16)
                ds_all[:, c] = ds
        for g in range(HEADS // 2):
            o = nn(
                keys_t[2 * g * size : (2 * g + 2) * size, :],
                ds_all[:, 2 * g * TILE : (2 * g + 2) * TILE],
            )
            parts += [o[0:size, 0:TILE], o[size : 2 * size, TILE : 2 * TILE]]
        ql[rows, :] = (jnp.concatenate(parts, axis=0).T * scale).astype(BF16)
        dk[win, :] += nn(ds_all[...], qm[...])
        dv[win, :] += nn(p[i], am[...])
        return carry

    lax.fori_loop(0, tok // TILE, tile, 0, unroll=8)
    kl[...] = (dk[...] * scale).astype(BF16)
    vl[...] = dv[...].astype(BF16)


def backward_kernel(flat, piece, place, g_one, q, k, v, p, scale_inv, attn_t, w_out, *rest):
    count = 9 if flat else 10
    feat, emb, src, dwo, vg, wa, low_out, *outs = rest[:count]
    grads, ql, kl, vl, *scratch = rest[count:]
    attention_back(g_one, q, k, v, p, scale_inv, attn_t, w_out, ql, kl, vl, *scratch)
    tok, width = g_one.shape
    at = feat.shape[1]
    total = jnp.zeros((1, width), F32)
    for i in range(tok // ROWS):
        r = pl.ds(i * ROWS, ROWS)
        e = (
            g_one[r, :]
            + nt(ql[r, :], wa[at : at + width, :])
            + nt(kl[r, :], wa[at + width : at + 2 * width, :])
            + nt(vl[r, :], wa[at + 2 * width : at + 3 * width, :])
        )
        low = e.astype(BF16)
        low_out[r, :] = low
        total += column_sum(low)
    src_t = src[...].T
    grads[at : at + width, :] = nn(src_t, ql[...]).astype(BF16)
    grads[at + width : at + 2 * width, :] = nn(src_t, kl[...]).astype(BF16)
    grads[at + 2 * width : at + 3 * width, :] = nn(emb[...].astype(BF16).T, vl[...]).astype(BF16)
    grads[0:at, :] = nn(feat[...].T, low_out[...]).astype(BF16)
    grads[at + 3 * width :, :] = dwo[...]
    front = jnp.concatenate([total, column_sum(ql[...]), column_sum(vl[...])], axis=0)
    if flat:
        outs[0][...] = grads[...]
        outs[1][...] = vg[...]
        outs[1][0:3, :] = front
        return
    keep, send_one, send_two = outs
    core = place[3]
    for m in range(4):
        send = (send_one, send_two)[m // 2]
        to = pl.ds((m % 2) * piece, piece)
        keep[pl.ds(m * piece, piece), :] = grads[
            pl.ds(pl.multiple_of((2 * m + core) * piece, 16), piece), :
        ]
        send[to, :] = grads[pl.ds(pl.multiple_of((2 * m + 1 - core) * piece, 16), piece), :]
    rows = vg.shape[0]
    pad = jnp.zeros((VEC_PAD - rows, width), F32)
    tail = jnp.concatenate([front, vg[3:rows, :], pad], axis=0).astype(BF16)
    keep[4 * piece :, :] = tail
    send_two[2 * piece :, :] = tail


def backward(flat, place, g_one, q, k, v, p, scale_inv, attn_t, w_out, feat, emb, src, *rest):
    dwo, vg, wa, piece = rest
    tok, width = g_one.shape
    outs = [shape((tok, width), BF16)]
    if flat:
        outs += [shape(wa.shape, BF16), shape(vg.shape, F32)]
    else:
        outs += [shape((4 * piece + VEC_PAD, width), BF16)]
        outs += [shape((2 * piece, width), BF16), shape((2 * piece + VEC_PAD, width), BF16)]
    ins = [place, g_one, q, k, v, p, scale_inv, attn_t, w_out, feat, emb, src, dwo, vg, wa]
    low = VMEM((tok, width), BF16)
    return call(
        functools.partial(backward_kernel, flat, piece),
        outs,
        ins,
        [
            VMEM(wa.shape, BF16),
            low,
            low,
            low,
            low,
            VMEM((width, tok), BF16),
            VMEM((WINDOW, HEADS * TILE), BF16),
            VMEM((width, HEADS * TILE), BF16),
            VMEM((width, TILE), BF16),
            VMEM((HEADS * TILE, width), BF16),
            VMEM((HEADS * TILE, width), BF16),
            VMEM((tok, width), F32),
            VMEM((tok, width), F32),
        ],
        "attention_backward",
        16_000_000_000,
        [pltpu.SMEM] + [VMEM] * (len(ins) - 1),
        vmem=24,
    )


def feature_kernel(low, wa, out):
    for i in range(low.shape[0] // ROWS):
        r = pl.ds(i * ROWS, ROWS)
        out[r, :] = nt(low[r, :], wa[0 : out.shape[1], :])


def feature_back(low, wa, feat_dim):
    return call(
        feature_kernel,
        [shape((low.shape[0], feat_dim), F32)],
        [low, wa],
        [],
        "feature_gradient",
        300_000_000,
    )[0]


def plane_kernel(place, own, one, two, three, attn, rest):
    got = (own, one, two, three)
    z = place[0]
    for slot in range(4):

        @pl.when(z == slot)
        def _(slot=slot):
            attn[...] = got[slot][...]
            for plane in range(1, 4):
                rest[plane - 1] = got[slot ^ plane][...]


def pick_planes(place, own, one, two, three):
    return call(
        plane_kernel,
        [shape(own.shape, BF16), shape((3, *own.shape), BF16)],
        [place, own, one, two, three],
        [],
        "pick_planes",
        1_000_000,
        [pltpu.SMEM] + [VMEM] * 4,
    )


def ff_sum_kernel(place, keep, recv, *outs):
    yx = place[1]
    for slot in range(4):
        for plane in range(3):
            at = 4 * plane + (yx ^ slot)
            outs[slot][plane] = keep[at] + recv[at]


def ff_sum(place, keep, recv):
    one = shape((3, *keep.shape[1:]), BF16)
    return call(
        ff_sum_kernel,
        [one] * 4,
        [place, keep, recv],
        [],
        "sum_cores_ff",
        1_000_000,
        [pltpu.SMEM] + [VMEM] * 2,
    )


def four_kernel(a, b, c, d, out):
    out[...] = (
        (a[...].astype(F32) + b[...].astype(F32)) + (c[...].astype(F32) + d[...].astype(F32))
    ).astype(BF16)


def four_sum(a, b, c, d):
    return call(four_kernel, [shape(a.shape, BF16)], [a, b, c, d], [], "sum_plane_ff", 1_000_000)[0]


def tail_sum_kernel(piece, place, keep, one, two, *outs):
    vec = keep[4 * piece :, :].astype(F32) + two[2 * piece :, :].astype(F32)
    for slot in range(4):
        m = place[1] ^ slot
        own = keep[pl.ds(pl.multiple_of(m * piece, 16), piece), :]
        at = pl.ds(pl.multiple_of((m & 1) * piece, 16), piece)
        outs[slot][piece:, :] = vec.astype(BF16)
        for half, recv in enumerate((one, two)):

            @pl.when((m >> 1) == half)
            def _(slot=slot, own=own, at=at, recv=recv):
                outs[slot][0:piece, :] = own + recv[at, :]


def tail_sum(place, keep, one, two, piece):
    return call(
        functools.partial(tail_sum_kernel, piece),
        [shape((piece + VEC_PAD, keep.shape[1]), BF16)] * 4,
        [place, keep, one, two],
        [],
        "sum_cores_tail",
        1_000_000,
        [pltpu.SMEM] + [VMEM] * 3,
    )


def plane_sum_kernel(place, a, b, c, d, ff, *outs):
    z = place[0]
    total = (
        (a[...].astype(F32) + b[...].astype(F32)) + (c[...].astype(F32) + d[...].astype(F32))
    ).astype(BF16)
    piece = ff.shape[1]
    for slot in range(4):
        goal = z ^ slot
        outs[slot][piece:, :] = total[piece:, :]

        @pl.when(goal == 0)
        def _(slot=slot):
            outs[slot][0:piece, :] = total[0:piece, :]

        @pl.when(goal != 0)
        def _(slot=slot, goal=goal):
            outs[slot][0:piece, :] = ff[jnp.maximum(goal - 1, 0)]


def plane_sum(place, a, b, c, d, ff):
    return call(
        plane_sum_kernel,
        [shape(a.shape, BF16)] * 4,
        [place, a, b, c, d, ff],
        [],
        "sum_plane_tail",
        1_000_000,
        [pltpu.SMEM] + [VMEM] * 5,
    )


def adam_step(weight, moment_one, moment_two, gradient, step_rate, decay_rate):
    moment_one = BETA_ONE * moment_one + (1.0 - BETA_ONE) * gradient
    moment_two = BETA_TWO * moment_two + (1.0 - BETA_TWO) * gradient * gradient
    mean_hat = moment_one / (1.0 - BETA_ONE**STEP)
    square_hat = moment_two / (1.0 - BETA_TWO**STEP)
    weight = weight - step_rate * (
        mean_hat / (jnp.sqrt(square_hat) + ADAM_EPS) + decay_rate * weight
    )
    return (weight, moment_one, moment_two)


def adam_kernel(feat_dim, place, a, b, c, d, w, m, v, vw, vm, vv, *outs):
    total = (a[...].astype(F32) + b[...].astype(F32)) + (c[...].astype(F32) + d[...].astype(F32))
    piece = w.shape[0]
    rows = place[2] * piece + lax.broadcasted_iota(jnp.int32, w.shape, 0)
    rate = jnp.where(rows < feat_dim, 0.1 * RATE, RATE)
    new = adam_step(w[...], m[...], v[...], total[0:piece, :], rate, DECAY)
    for ref, value in zip(outs[:3], new):
        ref[...] = value
    outs[3][...] = new[0].astype(BF16)
    new = adam_step(vw[...], vm[...], vv[...], total[piece : piece + vw.shape[0], :], RATE, 0.0)
    for ref, value in zip(outs[4:], new):
        ref[...] = value


def adam(place, parts, mats, mats_m, mats_v, vecs, vecs_m, vecs_v, feat_dim):
    mat, vec = shape(mats.shape, F32), shape(vecs.shape, F32)
    return call(
        functools.partial(adam_kernel, feat_dim),
        [mat, mat, mat, shape(mats.shape, BF16), vec, vec, vec],
        [place, *parts, mats, mats_m, mats_v, vecs, vecs_m, vecs_v],
        [],
        "adam",
        10_000_000,
        [pltpu.SMEM] + [VMEM] * 10,
    )


def grid_swap(dz, dyx):
    return [(4 * z + yx, 4 * (z ^ dz) + (yx ^ dyx)) for z in range(4) for yx in range(4)]


PAIR_SWAP = [(0, 1), (1, 0)]


def per_device(
    flat,
    features,
    cotangent,
    canvas_lengths,
    crop_ids,
    mats,
    mats_m,
    mats_v,
    vecs,
    vecs_m,
    vecs_v,
):
    tok = features.shape[0]
    feat_dim = features.shape[1]
    width = vecs.shape[1]
    attn_rows = feat_dim + 3 * width + width // 2
    ff_rows = width // 2 + 2 * FF
    piece = mats.shape[0]
    dp, core = lax.axis_index("dp"), lax.axis_index("pair")
    device = lax.axis_index(("dp", "pair"))
    place = jnp.stack([dp // 4, dp % 4, device, core]).astype(jnp.int32)

    near = prepare(canvas_lengths, crop_ids, features, vecs)
    mats_low = mats.astype(BF16)
    if flat:
        gathered = lax.all_gather(mats_low, ("dp", "pair"), axis=0, tiled=True)
        attn_pieces = [gathered[:attn_rows]]
        ff_pieces = [gathered[attn_rows:]]
    else:
        planes = [lax.ppermute(mats_low, "dp", grid_swap(dz, 0)) for dz in (1, 2, 3)]
        near, planes = lax.optimization_barrier((near, planes))
        one, three = pick_planes(place, mats_low, *planes)
        attn_pieces = [one] + [lax.ppermute(one, "dp", grid_swap(0, s)) for s in (3, 1, 2)]
        attn_pieces += [lax.ppermute(a, "pair", PAIR_SWAP) for a in attn_pieces]
        ff_pieces = [three] + [lax.ppermute(three, "dp", grid_swap(0, s)) for s in (3, 1, 2)]

    pos_table, seg_col, seg_row, features, vec = near
    wa, emb, src, q, k, v, attn_t, probs, scale_inv = attention(
        flat, place, features, pos_table, (seg_col, seg_row), vec, attn_pieces, attn_rows
    )
    if not flat:
        own_swap = lax.ppermute(ff_pieces[0], "pair", PAIR_SWAP)
        attn_t, *moved = lax.optimization_barrier((attn_t, *ff_pieces[1:]))
        moved_swap = [lax.ppermute(a, "pair", PAIR_SWAP) for a in moved]
        ff_pieces = [ff_pieces[0], *moved, own_swap, *moved_swap]
    output, g_one, w_out, vg, dwo, *ff_grads = feed(
        flat, place, emb, attn_t, cotangent, vec, wa, ff_pieces, ff_rows
    )
    if not flat:
        keep, send = ff_grads
        sums = ff_sum(place, keep, lax.ppermute(send, "pair", PAIR_SWAP))
        g_one, *sums = lax.optimization_barrier((g_one, *sums))
        ff_parts = [sums[0]] + [lax.ppermute(sums[s], "dp", grid_swap(0, s)) for s in (2, 1, 3)]
    low, *tail = backward(
        flat,
        place,
        g_one,
        q,
        k,
        v,
        probs,
        scale_inv,
        attn_t,
        w_out,
        features,
        emb,
        src,
        dwo,
        vg,
        wa,
        piece,
    )
    feature_grad = feature_back(low, wa, feat_dim)
    if flat:
        grads = jnp.concatenate([tail[0], ff_grads[0]], axis=0).astype(F32)
        total = lax.psum_scatter(grads, ("dp", "pair"), scatter_dimension=0, tiled=True)
        vec_total = lax.psum(tail[1], ("dp", "pair"))
        row_ids = device * piece + jnp.arange(piece, dtype=jnp.int32)
        rate = jnp.where(row_ids < feat_dim, 0.1 * RATE, RATE)[:, None]
        new = adam_step(mats, mats_m, mats_v, total, rate, DECAY)
        new_vec = adam_step(vecs, vecs_m, vecs_v, vec_total, RATE, 0.0)
        return (output, feature_grad, *new, new[0].astype(BF16), *new_vec)
    keep, *send = tail
    recv = [lax.ppermute(a, "pair", PAIR_SWAP) for a in send]
    sums = tail_sum(place, keep, *recv, piece)
    sums, ff_parts = lax.optimization_barrier((sums, ff_parts))
    ff = four_sum(*ff_parts)
    parts = [sums[0]] + [lax.ppermute(sums[s], "dp", grid_swap(0, s)) for s in (2, 1, 3)]
    sums = plane_sum(place, *parts, ff)
    parts = [sums[0]] + [lax.ppermute(sums[s], "dp", grid_swap(s, 0)) for s in (2, 1, 3)]
    new = adam(place, parts, mats, mats_m, mats_v, vecs, vecs_m, vecs_v, feat_dim)
    return (output, feature_grad, *new)


def solution(mesh):
    rows = P(("dp", "pair"), None)
    in_specs = (rows, rows, rows, P(("dp", "pair")), rows, rows, rows, P(), P(), P())
    out_specs = (rows, rows, rows, rows, rows, rows, P(), P(), P())
    flat = mesh.shape["dp"] != 16 or mesh.shape["pair"] != 2
    return jax.shard_map(
        functools.partial(per_device, flat),
        mesh=mesh,
        in_specs=in_specs,
        out_specs=out_specs,
        check_vma=False,
    )
```

```python
import functools
import math

import jax
import jax.numpy as jnp
from jax import lax
from jax.experimental import pallas as pl
from jax.experimental.pallas import tpu as pltpu
from jax.sharding import PartitionSpec as P

HEADS = 8
FF = 2048
STEP = 10

EPS_NORM = 1e-05
RATE = 0.2
BETA_ONE = 0.9
BETA_TWO = 0.999
ADAM_EPS = 1e-08
DECAY = 0.0001
MASKED = -1000000000.0

TILE = 128
WINDOW = 384
ROWS = 512
FEED_ROWS = 1024
BLOCK = 256
BLOCKS = FF // BLOCK
GELU_A = 0.7978845608028654
GELU_B = 0.044715
LOG2_E = 1.4426950408889634
VEC_PAD = 24

F32 = jnp.float32
BF16 = jnp.bfloat16
VMEM = pltpu.VMEM


def nn(a, b):
    return lax.dot_general(a, b, (((1,), (0,)), ((), ())), preferred_element_type=F32)


def nt(a, b):
    return lax.dot_general(a, b, (((1,), (1,)), ((), ())), preferred_element_type=F32)


def tn(a, b):
    return lax.dot_general(a, b, (((0,), (0,)), ((), ())), preferred_element_type=F32)


def row_mean(x):
    return jnp.sum(x, axis=1, keepdims=True) * (1.0 / x.shape[1])


def fold_rows(x):
    return jnp.sum(x.reshape(x.shape[0] // 8, 8, x.shape[1]), axis=0)


def column_sum(x):
    return jnp.sum(x.astype(F32), axis=0, keepdims=True)


def head_lanes(h, rows, width):
    lane = lax.broadcasted_iota(jnp.int32, (rows, width), 1)
    size = width // HEADS
    return (lane >= h * size) & (lane < (h + 1) * size)


def window_start(i, tok):
    return jnp.clip((i - 1) * TILE, 0, tok - WINDOW)


def call(kernel, outs, ins, scratch, name, flops, spaces=None, vmem=12):
    spaces = spaces or [VMEM] * len(ins)
    nbytes = 0 * sum(a.size * a.dtype.itemsize for a in ins) + sum(
        a.size * a.dtype.itemsize for a in outs
    )
    return pl.pallas_call(
        kernel,
        out_shape=tuple(outs),
        in_specs=[pl.BlockSpec(memory_space=s) for s in spaces],
        out_specs=tuple(pl.BlockSpec(memory_space=VMEM) for _ in outs),
        scratch_shapes=scratch,
        compiler_params=pltpu.CompilerParams(vmem_limit_bytes=vmem << 20),
        cost_estimate=pl.CostEstimate(flops=flops, bytes_accessed=nbytes, transcendentals=0),
        name=name,
    )(*ins)


def shape(dims, kind):
    return jax.ShapeDtypeStruct(dims, kind)


def load_pieces(refs, offsets, dst):
    for ref, offs in zip(refs, offsets):
        if len(ref.shape) == 2:
            dst[pl.ds(offs[0], ref.shape[0]), :] = ref[...]
        else:
            for i, off in enumerate(offs):
                dst[pl.ds(off, ref.shape[1]), :] = ref[i]


def place_offsets(place, piece, planes):
    offsets = []
    for other in (0, 1):
        for slot in (0, 3, 1, 2):
            core = place[3] ^ other if other else place[3]
            inner = 2 * (place[1] ^ slot) + core
            offsets.append(
                [pl.multiple_of((8 * plane + inner) * piece, 16) for plane in range(planes)]
            )
    return offsets


def prepare_kernel(lens, crops, feat, vec, pos, seg_col, seg_row, feat_near, vec_near):
    feat_near[...] = feat[...]
    vec_near[...] = vec[...]
    tok, width = pos.shape
    half = width // 2
    first = lens[0, 0]
    lane = lax.broadcasted_iota(jnp.int32, (TILE, half), 1)
    frequency = jnp.exp(lane.astype(F32) * (-math.log(10000.0) / half))
    at = lax.broadcasted_iota(jnp.int32, (tok // TILE, TILE), 0) * TILE
    at = at + lax.broadcasted_iota(jnp.int32, (tok // TILE, TILE), 1)
    seg_row[...] = (2 * crops[...] + (at >= first).astype(jnp.int32)).astype(F32)
    for i in range(tok // TILE):
        r = slice(i * TILE, (i + 1) * TILE)
        row = lax.broadcasted_iota(jnp.int32, (TILE, half), 0) + i * TILE
        angle = (row - jnp.where(row >= first, first, 0)).astype(F32) * frequency
        pos[r, 0:half] = jnp.sin(angle)
        pos[r, half:width] = jnp.cos(angle)
        seg_col[r, :] = jnp.broadcast_to(seg_row[i : i + 1, :], (TILE, TILE)).T


def prepare(lens, crops, feat, vec):
    tok, width = crops.shape[0], vec.shape[1]
    crops = crops.reshape(-1, TILE)
    return call(
        prepare_kernel,
        [
            shape((tok, width), F32),
            shape((tok, TILE), F32),
            shape(crops.shape, F32),
            shape(feat.shape, BF16),
            shape(vec.shape, F32),
        ],
        [lens, crops, feat, vec],
        [],
        "positions_segments",
        1_000_000,
        [pltpu.SMEM, VMEM, VMEM, VMEM],
    )


def attention_kernel(flat, piece, place, feat, pos, seg_col, seg_row, vec, *rest):
    count = 1 if flat else 8
    pieces, rest = rest[:count], rest[count:]
    w, emb, src, q, k, v, attn_t, p, scale_inv, v_t, q_t = rest
    tok, width = emb.shape
    feat_dim = feat.shape[1]
    size = width // HEADS
    scale = size ** (-0.5)
    offsets = [[0]] if flat else place_offsets(place, piece, 1)
    load_pieces(pieces, offsets, w)
    for i in range(tok // ROWS):
        r = pl.ds(i * ROWS, ROWS)
        e = nn(feat[r, :], w[0:feat_dim, :]) + vec[0:1, :]
        emb[r, :] = e
        s = (e + pos[r, :]).astype(BF16)
        src[r, :] = s
        low = e.astype(BF16)
        at = feat_dim
        q[r, :] = (nn(s, w[at : at + width, :]) + vec[1:2, :]).astype(BF16)
        k[r, :] = nn(s, w[at + width : at + 2 * width, :]).astype(BF16)
        v[r, :] = (nn(low, w[at + 2 * width : at + 3 * width, :]) + vec[2:3, :]).astype(BF16)
    pad = v_t.shape[0] // HEADS
    vals = v[...].T
    for h in range(HEADS):
        v_t[h * pad : h * pad + size, :] = vals[h * size : (h + 1) * size, :]
        v_t[h * pad + size : (h + 1) * pad, :] = jnp.ones((pad - size, tok), BF16)
    q_t[...] = jnp.zeros_like(q_t)
    masked = MASKED / scale
    factor = scale * LOG2_E

    def tile(i, carry):
        rows = pl.ds(pl.multiple_of(i * TILE, TILE), TILE)
        win = pl.ds(pl.multiple_of(window_start(i, tok), TILE), WINDOW)
        own_t = q[rows, :].T
        keys = k[win, :]
        vals_t = v_t[:, win]
        allowed = seg_col[win, :] == seg_row[pl.ds(i, 1), :]
        for h in range(HEADS):
            d = slice(h * size, (h + 1) * size)
            q_t[d, h * TILE : (h + 1) * TILE] = own_t[d, :]
        for g in range(HEADS // 8):
            both = nn(keys, q_t[:, 8 * g * TILE : (8 * g + 8) * TILE])
            for u in range(8):
                h = 8 * g + u
                s = jnp.where(allowed, both[:, u * TILE : (u + 1) * TILE], masked)
                top = jnp.max(s, axis=0, keepdims=True)
                e = jnp.exp2((s - top) * factor).astype(BF16)
                p[i, :, h * TILE : (h + 1) * TILE] = e
        for g in range(HEADS // 2):
            o = nn(
                vals_t[2 * g * pad : (2 * g + 2) * pad, :],
                p[i, :, 2 * g * TILE : (2 * g + 2) * TILE],
            )
            for u in range(2):
                h = 2 * g + u
                own = o[u * pad : (u + 1) * pad, u * TILE : (u + 1) * TILE]
                inv = 1.0 / own[size : size + 1, :]
                scale_inv[i, h : h + 1, :] = inv
                attn_t[h * size : (h + 1) * size, rows] = (own[0:size, :] * inv).astype(BF16)
        return carry

    lax.fori_loop(0, tok // TILE, tile, 0, unroll=8)


def attention(flat, place, feat, pos, segment, vec, pieces, attn_rows):
    tok, width = feat.shape[0], vec.shape[1]
    piece = pieces[0].shape[0]
    low = shape((tok, width), BF16)
    outs = [
        shape((attn_rows, width), BF16),
        shape((tok, width), F32),
        low,
        low,
        low,
        low,
        shape((width, tok), BF16),
        shape((tok // TILE, WINDOW, HEADS * TILE), BF16),
        shape((tok // TILE, HEADS, TILE), F32),
    ]
    ins = [place, feat, pos, *segment, vec, *pieces]
    return call(
        functools.partial(attention_kernel, flat, piece),
        outs,
        ins,
        [
            VMEM((width + 16 * HEADS, tok), BF16),
            VMEM((width, HEADS * TILE), BF16),
        ],
        "attention_forward",
        1_200_000_000,
        [pltpu.SMEM] + [VMEM] * (5 + len(pieces)),
        vmem=20,
    )


def feed_kernel(flat, piece, place, emb, attn_t, cot, vec, wa, *rest):
    count = 1 if flat else 8
    pieces, rest = rest[:count], rest[count:]
    outs = 5 if flat else 6
    res, rest = rest[: outs + 1], rest[outs + 1 :]
    out, g_one, w_out, vec_grad, dwo = res[:5]
    (wf, wh, wh_t, wb_t, half_a, half_b, act, slope, n_t, b_t, out_all, acc, gff) = rest
    halves = (half_a, half_b)
    tok, width = emb.shape
    first = width // 2
    offsets = [[0]] if flat else place_offsets(place, piece, 3)
    load_pieces(pieces, offsets, wf)
    for u in range(2):
        halves[u][...] = wf[first : first + FF, u * 128 : (u + 1) * 128].astype(F32)
    w_out[0:first, :] = wa[wa.shape[0] - first :, :]
    w_out[first:, :] = wf[0:first, :]
    for j in range(BLOCKS):
        c = slice(j * BLOCK, (j + 1) * BLOCK)
        w = jnp.concatenate(
            [halves[u][pl.ds(j, width, stride=BLOCKS), :] for u in range(2)], axis=1
        ).astype(BF16)
        wh[:, c] = w
        wh_t[c, :] = w.T
        wb_t[:, c] = wf[first + FF + j * BLOCK : first + FF + (j + 1) * BLOCK, :].T
    acc[...] = jnp.zeros_like(acc)
    n_t[width : width + 8, :] = jnp.ones((8, tok), BF16)

    r = slice(0, tok)
    res_one = emb[r, :] + tn(attn_t[:, r], w_out[...]) + vec[3:4, :]
    cen = res_one - row_mean(res_one)
    inv_one = lax.rsqrt(row_mean(cen * cen) + EPS_NORM)
    hat_one = cen * inv_one
    normed = hat_one * vec[4:5, :] + vec[5:6, :]
    low = normed.astype(BF16)
    res_two = normed + vec[6:7, :]
    for j in range(BLOCKS):
        c = slice(j * BLOCK, (j + 1) * BLOCK)
        at = first + FF + j * BLOCK
        x = nn(low, wh[:, c]) + vec[9 + j : 10 + j, :]
        sq = x * x
        t = jnp.tanh((x * (GELU_A + (GELU_A * GELU_B) * sq)).astype(BF16))
        half = t * jnp.bfloat16(0.5) + jnp.bfloat16(0.5)
        act[r, c] = x.astype(BF16) * half
        bend = (x * ((2 * GELU_A) + (6 * GELU_A * GELU_B) * sq)).astype(BF16)
        slope[r, c] = half + (half - half * half) * bend
        res_two += nn(act[r, c], wf[at : at + BLOCK, :])
    cen = res_two - row_mean(res_two)
    inv_two = lax.rsqrt(row_mean(cen * cen) + EPS_NORM)
    hat_two = cen * inv_two
    out[r, :] = hat_two * vec[7:8, :] + vec[8:9, :]
    ct = cot[r, :].astype(F32)
    gs = ct * vec[7:8, :]
    g_two = inv_two * (gs - row_mean(gs) - hat_two * row_mean(gs * hat_two))
    back = g_two.astype(BF16)
    b_t[:, r] = back.T
    acc[0] += fold_rows(back.astype(F32))
    acc[1] += fold_rows(ct * hat_two)
    acc[2] += fold_rows(ct)
    n_t[0:width, r] = low.T
    g_norm = g_two
    for j in range(BLOCKS):
        c = slice(j * BLOCK, (j + 1) * BLOCK)
        part = (nn(back, wb_t[:, c]) * slope[r, c].astype(F32)).astype(BF16)
        g_norm += nn(part, wh_t[c, :])
        g = nn(n_t[...], part)
        for u in range(2):
            halves[u][pl.ds(j, width, stride=BLOCKS), :] = g[0:width, u * 128 : (u + 1) * 128]
        vec_grad[9 + j : 10 + j, :] = g[width : width + 1, :]
        at = first + FF + j * BLOCK
        gff[at : at + BLOCK, :] = nn(b_t[...], act[:, c]).T.astype(BF16)
    gs = g_norm * vec[4:5, :]
    g_res = inv_one * (gs - row_mean(gs) - hat_one * row_mean(gs * hat_one))
    g_one[r, :] = g_res
    out_low = g_res.astype(BF16)
    out_all[r, :] = out_low
    acc[3] += fold_rows(out_low.astype(F32))
    acc[4] += fold_rows(g_norm * hat_one)
    acc[5] += fold_rows(g_norm)

    for u in range(2):
        gff[first : first + FF, u * 128 : (u + 1) * 128] = halves[u][...].astype(BF16)
    g = nn(attn_t[...], out_all[...]).astype(BF16)
    dwo[...] = g[0:first, :]
    gff[0:first, :] = g[first:, :]
    sums = jnp.sum(acc[...], axis=1)
    vec_grad[0:3, :] = jnp.zeros((3, width), F32)
    for row, at in ((3, 3), (4, 4), (5, 5), (6, 0), (7, 1), (8, 2)):
        vec_grad[row : row + 1, :] = sums[at : at + 1, :]
    if flat:
        res[5][...] = gff[...]
    else:
        split_cores(place, gff, res[5], res[6])


def split_cores(place, grads, keep, send):
    core = place[3]
    piece = keep.shape[1]
    for m in range(keep.shape[0]):
        keep[m] = grads[pl.ds(pl.multiple_of((2 * m + core) * piece, 16), piece), :]
        send[m] = grads[pl.ds(pl.multiple_of((2 * m + 1 - core) * piece, 16), piece), :]


def feed(flat, place, emb, attn_t, cot, vec, wa, pieces, ff_rows):
    tok, width = emb.shape
    piece = pieces[0].shape[-2]
    outs = [
        shape((tok, width), F32),
        shape((tok, width), F32),
        shape((width, width), BF16),
        shape(vec.shape, F32),
        shape((width // 2, width), BF16),
    ]
    if flat:
        outs += [shape((ff_rows, width), BF16)]
    else:
        outs += [shape((ff_rows // piece // 2, piece, width), BF16)] * 2
    return call(
        functools.partial(feed_kernel, flat, piece),
        outs,
        [place, emb, attn_t, cot, vec, wa, *pieces],
        [
            VMEM((ff_rows, width), BF16),
            VMEM((width, FF), BF16),
            VMEM((FF, width), BF16),
            VMEM((width, FF), BF16),
            VMEM((FF, 128), F32),
            VMEM((FF, 128), F32),
            VMEM((tok, FF), BF16),
            VMEM((tok, FF), BF16),
            VMEM((width + 8, tok), BF16),
            VMEM((width, tok), BF16),
            VMEM((tok, width), BF16),
            VMEM((6, 8, width), F32),
            VMEM((ff_rows, width), BF16),
        ],
        "feed_forward_both",
        14_000_000_000,
        [pltpu.SMEM] + [VMEM] * (5 + len(pieces)),
        vmem=34,
    )


def attention_back(g_one, q, k, v, p, scale_inv, attn_t, w_out, ql, kl, vl, *scratch):
    ag, k_t, ds_all, a_t, scaled, qm, am, dk, dv = scratch
    tok, width = g_one.shape
    size = width // HEADS
    scale = size ** (-0.5)
    for i in range(tok // ROWS):
        r = pl.ds(i * ROWS, ROWS)
        ag[r, :] = nt(g_one[r, :].astype(BF16), w_out[...]).astype(BF16)
    k_t[...] = k[...].T
    dk[...] = jnp.zeros_like(dk)
    dv[...] = jnp.zeros_like(dv)
    a_t[...] = jnp.zeros_like(a_t)

    def tile(i, carry):
        rows = pl.ds(pl.multiple_of(i * TILE, TILE), TILE)
        win = pl.ds(pl.multiple_of(window_start(i, tok), TILE), WINDOW)
        own_q = q[rows, :]
        own_t = ag[rows, :].T
        vals = v[win, :]
        keys_t = k_t[:, win]
        inner = []
        for h in range(HEADS):
            d = slice(h * size, (h + 1) * size)
            grad = own_t[d, :].astype(F32) * scale_inv[i, h : h + 1, :]
            inner.append(jnp.sum(grad * attn_t[d, rows].astype(F32), axis=0, keepdims=True))
            a_t[d, h * TILE : (h + 1) * TILE] = grad.astype(BF16)
            scaled[d, :] = grad.astype(BF16)
        own_a = scaled[...].T
        for h in range(HEADS):
            lanes = head_lanes(h, TILE, width)
            c = slice(h * TILE, (h + 1) * TILE)
            qm[c, :] = jnp.where(lanes, own_q, jnp.zeros_like(own_q))
            am[c, :] = jnp.where(lanes, own_a, jnp.zeros_like(own_a))
        parts = []
        for g in range(HEADS // 8):
            both = nn(vals, a_t[:, 8 * g * TILE : (8 * g + 8) * TILE])
            for u in range(8):
                h = 8 * g + u
                c = slice(h * TILE, (h + 1) * TILE)
                dp = both[:, u * TILE : (u + 1) * TILE]
                ds = (p[i, :, c].astype(F32) * (dp - inner[h])).astype(BF16)
                ds_all[:, c] = ds
        for g in range(HEADS // 2):
            o = nn(
                keys_t[2 * g * size : (2 * g + 2) * size, :],
                ds_all[:, 2 * g * TILE : (2 * g + 2) * TILE],
            )
            parts += [o[0:size, 0:TILE], o[size : 2 * size, TILE : 2 * TILE]]
        ql[rows, :] = (jnp.concatenate(parts, axis=0).T * scale).astype(BF16)
        dk[win, :] += nn(ds_all[...], qm[...])
        dv[win, :] += nn(p[i], am[...])
        return carry

    lax.fori_loop(0, tok // TILE, tile, 0, unroll=8)
    kl[...] = (dk[...] * scale).astype(BF16)
    vl[...] = dv[...].astype(BF16)


def backward_kernel(flat, piece, place, g_one, q, k, v, p, scale_inv, attn_t, w_out, *rest):
    count = 9 if flat else 10
    feat, emb, src, dwo, vg, wa, low_out, *outs = rest[:count]
    grads, ql, kl, vl, *scratch = rest[count:]
    attention_back(g_one, q, k, v, p, scale_inv, attn_t, w_out, ql, kl, vl, *scratch)
    tok, width = g_one.shape
    at = feat.shape[1]
    total = jnp.zeros((1, width), F32)
    for i in range(tok // ROWS):
        r = pl.ds(i * ROWS, ROWS)
        e = (
            g_one[r, :]
            + nt(ql[r, :], wa[at : at + width, :])
            + nt(kl[r, :], wa[at + width : at + 2 * width, :])
            + nt(vl[r, :], wa[at + 2 * width : at + 3 * width, :])
        )
        low = e.astype(BF16)
        low_out[r, :] = low
        total += column_sum(low)
    src_t = src[...].T
    grads[at : at + width, :] = nn(src_t, ql[...]).astype(BF16)
    grads[at + width : at + 2 * width, :] = nn(src_t, kl[...]).astype(BF16)
    grads[at + 2 * width : at + 3 * width, :] = nn(emb[...].astype(BF16).T, vl[...]).astype(BF16)
    grads[0:at, :] = nn(feat[...].T, low_out[...]).astype(BF16)
    grads[at + 3 * width :, :] = dwo[...]
    front = jnp.concatenate([total, column_sum(ql[...]), column_sum(vl[...])], axis=0)
    if flat:
        outs[0][...] = grads[...]
        outs[1][...] = vg[...]
        outs[1][0:3, :] = front
        return
    keep, send_one, send_two = outs
    core = place[3]
    for m in range(4):
        send = (send_one, send_two)[m // 2]
        to = pl.ds((m % 2) * piece, piece)
        keep[pl.ds(m * piece, piece), :] = grads[
            pl.ds(pl.multiple_of((2 * m + core) * piece, 16), piece), :
        ]
        send[to, :] = grads[pl.ds(pl.multiple_of((2 * m + 1 - core) * piece, 16), piece), :]
    rows = vg.shape[0]
    pad = jnp.zeros((VEC_PAD - rows, width), F32)
    tail = jnp.concatenate([front, vg[3:rows, :], pad], axis=0).astype(BF16)
    keep[4 * piece :, :] = tail
    send_two[2 * piece :, :] = tail


def backward(flat, place, g_one, q, k, v, p, scale_inv, attn_t, w_out, feat, emb, src, *rest):
    dwo, vg, wa, piece = rest
    tok, width = g_one.shape
    outs = [shape((tok, width), BF16)]
    if flat:
        outs += [shape(wa.shape, BF16), shape(vg.shape, F32)]
    else:
        outs += [shape((4 * piece + VEC_PAD, width), BF16)]
        outs += [shape((2 * piece, width), BF16), shape((2 * piece + VEC_PAD, width), BF16)]
    ins = [place, g_one, q, k, v, p, scale_inv, attn_t, w_out, feat, emb, src, dwo, vg, wa]
    low = VMEM((tok, width), BF16)
    return call(
        functools.partial(backward_kernel, flat, piece),
        outs,
        ins,
        [
            VMEM(wa.shape, BF16),
            low,
            low,
            low,
            low,
            VMEM((width, tok), BF16),
            VMEM((WINDOW, HEADS * TILE), BF16),
            VMEM((width, HEADS * TILE), BF16),
            VMEM((width, TILE), BF16),
            VMEM((HEADS * TILE, width), BF16),
            VMEM((HEADS * TILE, width), BF16),
            VMEM((tok, width), F32),
            VMEM((tok, width), F32),
        ],
        "attention_backward",
        16_000_000_000,
        [pltpu.SMEM] + [VMEM] * (len(ins) - 1),
        vmem=24,
    )


def feature_kernel(low, wa, out):
    for i in range(low.shape[0] // ROWS):
        r = pl.ds(i * ROWS, ROWS)
        out[r, :] = nt(low[r, :], wa[0 : out.shape[1], :])


def feature_back(low, wa, feat_dim):
    return call(
        feature_kernel,
        [shape((low.shape[0], feat_dim), F32)],
        [low, wa],
        [],
        "feature_gradient",
        300_000_000,
    )[0]


def plane_kernel(place, own, one, two, three, attn, rest):
    got = (own, one, two, three)
    z = place[0]
    for slot in range(4):

        @pl.when(z == slot)
        def _(slot=slot):
            attn[...] = got[slot][...]
            for plane in range(1, 4):
                rest[plane - 1] = got[slot ^ plane][...]


def pick_planes(place, own, one, two, three):
    return call(
        plane_kernel,
        [shape(own.shape, BF16), shape((3, *own.shape), BF16)],
        [place, own, one, two, three],
        [],
        "pick_planes",
        1_000_000,
        [pltpu.SMEM] + [VMEM] * 4,
    )


def ff_sum_kernel(place, keep, recv, *outs):
    yx = place[1]
    for slot in range(4):
        for plane in range(3):
            at = 4 * plane + (yx ^ slot)
            outs[slot][plane] = keep[at] + recv[at]


def ff_sum(place, keep, recv):
    one = shape((3, *keep.shape[1:]), BF16)
    return call(
        ff_sum_kernel,
        [one] * 4,
        [place, keep, recv],
        [],
        "sum_cores_ff",
        1_000_000,
        [pltpu.SMEM] + [VMEM] * 2,
    )


def four_kernel(a, b, c, d, out):
    out[...] = (
        (a[...].astype(F32) + b[...].astype(F32)) + (c[...].astype(F32) + d[...].astype(F32))
    ).astype(BF16)


def four_sum(a, b, c, d):
    return call(four_kernel, [shape(a.shape, BF16)], [a, b, c, d], [], "sum_plane_ff", 1_000_000)[0]


def tail_sum_kernel(piece, place, keep, one, two, *outs):
    vec = keep[4 * piece :, :].astype(F32) + two[2 * piece :, :].astype(F32)
    for slot in range(4):
        m = place[1] ^ slot
        own = keep[pl.ds(pl.multiple_of(m * piece, 16), piece), :]
        at = pl.ds(pl.multiple_of((m & 1) * piece, 16), piece)
        outs[slot][piece:, :] = vec.astype(BF16)
        for half, recv in enumerate((one, two)):

            @pl.when((m >> 1) == half)
            def _(slot=slot, own=own, at=at, recv=recv):
                outs[slot][0:piece, :] = own + recv[at, :]


def tail_sum(place, keep, one, two, piece):
    return call(
        functools.partial(tail_sum_kernel, piece),
        [shape((piece + VEC_PAD, keep.shape[1]), BF16)] * 4,
        [place, keep, one, two],
        [],
        "sum_cores_tail",
        1_000_000,
        [pltpu.SMEM] + [VMEM] * 3,
    )


def plane_sum_kernel(place, a, b, c, d, ff, *outs):
    z = place[0]
    total = (
        (a[...].astype(F32) + b[...].astype(F32)) + (c[...].astype(F32) + d[...].astype(F32))
    ).astype(BF16)
    piece = ff.shape[1]
    for slot in range(4):
        goal = z ^ slot
        outs[slot][piece:, :] = total[piece:, :]

        @pl.when(goal == 0)
        def _(slot=slot):
            outs[slot][0:piece, :] = total[0:piece, :]

        @pl.when(goal != 0)
        def _(slot=slot, goal=goal):
            outs[slot][0:piece, :] = ff[jnp.maximum(goal - 1, 0)]


def plane_sum(place, a, b, c, d, ff):
    return call(
        plane_sum_kernel,
        [shape(a.shape, BF16)] * 4,
        [place, a, b, c, d, ff],
        [],
        "sum_plane_tail",
        1_000_000,
        [pltpu.SMEM] + [VMEM] * 5,
    )


def adam_step(weight, moment_one, moment_two, gradient, step_rate, decay_rate):
    moment_one = BETA_ONE * moment_one + (1.0 - BETA_ONE) * gradient
    moment_two = BETA_TWO * moment_two + (1.0 - BETA_TWO) * gradient * gradient
    mean_hat = moment_one / (1.0 - BETA_ONE**STEP)
    square_hat = moment_two / (1.0 - BETA_TWO**STEP)
    weight = weight - step_rate * (
        mean_hat / (jnp.sqrt(square_hat) + ADAM_EPS) + decay_rate * weight
    )
    return (weight, moment_one, moment_two)


def adam_kernel(feat_dim, place, a, b, c, d, w, m, v, vw, vm, vv, *outs):
    total = (a[...].astype(F32) + b[...].astype(F32)) + (c[...].astype(F32) + d[...].astype(F32))
    piece = w.shape[0]
    rows = place[2] * piece + lax.broadcasted_iota(jnp.int32, w.shape, 0)
    rate = jnp.where(rows < feat_dim, 0.1 * RATE, RATE)
    new = adam_step(w[...], m[...], v[...], total[0:piece, :], rate, DECAY)
    for ref, value in zip(outs[:3], new):
        ref[...] = value
    outs[3][...] = new[0].astype(BF16)
    new = adam_step(vw[...], vm[...], vv[...], total[piece : piece + vw.shape[0], :], RATE, 0.0)
    for ref, value in zip(outs[4:], new):
        ref[...] = value


def adam(place, parts, mats, mats_m, mats_v, vecs, vecs_m, vecs_v, feat_dim):
    mat, vec = shape(mats.shape, F32), shape(vecs.shape, F32)
    return call(
        functools.partial(adam_kernel, feat_dim),
        [mat, mat, mat, shape(mats.shape, BF16), vec, vec, vec],
        [place, *parts, mats, mats_m, mats_v, vecs, vecs_m, vecs_v],
        [],
        "adam",
        10_000_000,
        [pltpu.SMEM] + [VMEM] * 10,
    )


def grid_swap(dz, dyx):
    return [(4 * z + yx, 4 * (z ^ dz) + (yx ^ dyx)) for z in range(4) for yx in range(4)]


PAIR_SWAP = [(0, 1), (1, 0)]


def per_device(
    flat,
    features,
    cotangent,
    canvas_lengths,
    crop_ids,
    mats,
    mats_m,
    mats_v,
    vecs,
    vecs_m,
    vecs_v,
):
    tok = features.shape[0]
    feat_dim = features.shape[1]
    width = vecs.shape[1]
    attn_rows = feat_dim + 3 * width + width // 2
    ff_rows = width // 2 + 2 * FF
    piece = mats.shape[0]
    dp, core = lax.axis_index("dp"), lax.axis_index("pair")
    device = lax.axis_index(("dp", "pair"))
    place = jnp.stack([dp // 4, dp % 4, device, core]).astype(jnp.int32)

    near = prepare(canvas_lengths, crop_ids, features, vecs)
    mats_low = mats.astype(BF16)
    if flat:
        gathered = lax.all_gather(mats_low, ("dp", "pair"), axis=0, tiled=True)
        attn_pieces = [gathered[:attn_rows]]
        ff_pieces = [gathered[attn_rows:]]
    else:
        planes = [lax.ppermute(mats_low, "dp", grid_swap(dz, 0)) for dz in (1, 3, 2)]
        near, planes = lax.optimization_barrier((near, planes))
        one, three = pick_planes(place, mats_low, planes[0], planes[2], planes[1])
        attn_pieces = [one] + [lax.ppermute(one, "dp", grid_swap(0, s)) for s in (3, 1, 2)]
        attn_pieces += [lax.ppermute(a, "pair", PAIR_SWAP) for a in attn_pieces]
        ff_pieces = [three] + [lax.ppermute(three, "dp", grid_swap(0, s)) for s in (3, 1, 2)]

    pos_table, seg_col, seg_row, features, vec = near
    wa, emb, src, q, k, v, attn_t, probs, scale_inv = attention(
        flat, place, features, pos_table, (seg_col, seg_row), vec, attn_pieces, attn_rows
    )
    if not flat:
        own_swap = lax.ppermute(ff_pieces[0], "pair", PAIR_SWAP)
        attn_t, *moved = lax.optimization_barrier((attn_t, *ff_pieces[1:]))
        moved_swap = [lax.ppermute(a, "pair", PAIR_SWAP) for a in moved]
        ff_pieces = [ff_pieces[0], *moved, own_swap, *moved_swap]
    output, g_one, w_out, vg, dwo, *ff_grads = feed(
        flat, place, emb, attn_t, cotangent, vec, wa, ff_pieces, ff_rows
    )
    if not flat:
        keep, send = ff_grads
        sums = ff_sum(place, keep, lax.ppermute(send, "pair", PAIR_SWAP))
        g_one, *sums = lax.optimization_barrier((g_one, *sums))
        ff_parts = [sums[0]] + [lax.ppermute(sums[s], "dp", grid_swap(0, s)) for s in (2, 1, 3)]
    low, *tail = backward(
        flat,
        place,
        g_one,
        q,
        k,
        v,
        probs,
        scale_inv,
        attn_t,
        w_out,
        features,
        emb,
        src,
        dwo,
        vg,
        wa,
        piece,
    )
    feature_grad = feature_back(low, wa, feat_dim)
    if flat:
        grads = jnp.concatenate([tail[0], ff_grads[0]], axis=0).astype(F32)
        total = lax.psum_scatter(grads, ("dp", "pair"), scatter_dimension=0, tiled=True)
        vec_total = lax.psum(tail[1], ("dp", "pair"))
        row_ids = device * piece + jnp.arange(piece, dtype=jnp.int32)
        rate = jnp.where(row_ids < feat_dim, 0.1 * RATE, RATE)[:, None]
        new = adam_step(mats, mats_m, mats_v, total, rate, DECAY)
        new_vec = adam_step(vecs, vecs_m, vecs_v, vec_total, RATE, 0.0)
        return (output, feature_grad, *new, new[0].astype(BF16), *new_vec)
    keep, *send = tail
    recv = [lax.ppermute(a, "pair", PAIR_SWAP) for a in send]
    sums = tail_sum(place, keep, *recv, piece)
    sums, ff_parts = lax.optimization_barrier((sums, ff_parts))
    ff = four_sum(*ff_parts)
    parts = [sums[0]] + [lax.ppermute(sums[s], "dp", grid_swap(0, s)) for s in (2, 1, 3)]
    sums = plane_sum(place, *parts, ff)
    parts = [sums[0]] + [lax.ppermute(sums[s], "dp", grid_swap(s, 0)) for s in (2, 1, 3)]
    new = adam(place, parts, mats, mats_m, mats_v, vecs, vecs_m, vecs_v, feat_dim)
    return (output, feature_grad, *new)


def solution(mesh):
    rows = P(("dp", "pair"), None)
    in_specs = (rows, rows, rows, P(("dp", "pair")), rows, rows, rows, P(), P(), P())
    out_specs = (rows, rows, rows, rows, rows, rows, P(), P(), P())
    flat = mesh.shape["dp"] != 16 or mesh.shape["pair"] != 2
    return jax.shard_map(
        functools.partial(per_device, flat),
        mesh=mesh,
        in_specs=in_specs,
        out_specs=out_specs,
        check_vma=False,
    )
```
